32 devices in a mesh: section: 2 (over core), expert: 4 (over y, x), tensor: 4 (over z).
Axes of the slice: x: 2, y: 2, z: 4, core: 2. Of those that a mesh axis runs over, the one named last changes fastest.
Arguments:
- inputs: float32 [1, 788, 768], P(None, 'expert'), may hold values from -6 to 6
- cotangent: float32 [1, 788, 768], P(None, 'expert'), may hold values from -6 to 6
- norm_scale: float32 [2, 2, 768], P('section'), may hold values from 0.5 to 1.5
- norm_shift: float32 [2, 2, 768], P('section'), may hold values from -3 to 3
- proj_weight: bfloat16 [2, 768, 3, 768], P('section', None, None, 'tensor'), may hold values from -0.21875 to 0.21875
- proj_bias: float32 [2, 2, 768], P('section', None, 'tensor'), may hold values from -3 to 3
- attn_weight: bfloat16 [2, 768, 768], P('section', 'tensor'), may hold values from -0.75 to 0.75
- attn_bias: float32 [2, 768], P('section'), may hold values from -3 to 3
- expert_in: bfloat16 [2, 4, 768, 3072], P('section', 'expert', None, 'tensor'), may hold values from -0.21875 to 0.21875
- expert_in_bias: float32 [2, 4, 3072], P('section', 'expert', 'tensor'), may hold values from -3 to 3
- expert_out: bfloat16 [2, 4, 3072, 768], P('section', 'expert', 'tensor'), may hold values from -0.109375 to 0.109375
- expert_out_bias: float32 [2, 4, 768], P('section', 'expert'), may hold values from -3 to 3
- routes: int32 [2, 1, 788, 2], P('section', None, 'expert'), may hold values from 0 to 3, all different within a row; in each aligned block of 197 rows (0 to 196, 197 to 393, ..., all dimensions but the last counted through in order) at most 148 rows name the same one
- gate_weights: float32 [2, 1, 788, 2], P('section', None, 'expert'), may hold values from 0.1 to 1
Outputs:
- section_out: float32 [2, 1, 788, 768], P('section', None, 'expert')
- section_in_grad: float32 [2, 1, 788, 768], P('section', None, 'expert')
- grad_norm_scale: float32 [2, 2, 768], P('section')
- grad_norm_shift: float32 [2, 2, 768], P('section')
- grad_proj_weight: float32 [2, 768, 3, 768], P('section', None, None, 'tensor')
- grad_proj_bias: float32 [2, 2, 768], P('section', None, 'tensor')
- grad_attn_weight: float32 [2, 768, 768], P('section', 'tensor')
- grad_attn_bias: float32 [2, 768], P('section')
- grad_expert_in: float32 [2, 4, 768, 3072], P('section', 'expert', None, 'tensor')
- grad_expert_in_bias: float32 [2, 4, 3072], P('section', 'expert', 'tensor')
- grad_expert_out: float32 [2, 4, 3072, 768], P('section', 'expert', 'tensor')
- grad_expert_out_bias: float32 [2, 4, 768], P('section', 'expert')
The draws below stay inside these ranges and needn't reach their ends.
Inputs may be any that keep to these rules, and one draw needn't show every extreme that they name: `routes`: each row names 2 different experts. In the rows of one index of the expert axis for one section and micro-batch, no expert is named more than 148 times, and in every draw some expert is named exactly 148 times there.
All inputs are finite; a program needn't handle non-finite values.
Results may differ from the reference program's by a relative error of at most 0.015.
Values may be sent and summed in bfloat16 or wider, within the bound.
A program may use at most 128 MiB of HBM per device.

```python
import math
import jax
import jax.numpy as jnp
import numpy as np
from jax import lax

D = 768
HEADS = 12
HEAD_DIM = 64
HIDDEN_SIZE = 3072
SEQ = 197
TOPK = 2
MICRO = 1
TOK_DEV = 197
TOKENS = 788
IMAGES = 4
EXPERTS = 4
CAP = 148
N_SECTION = 2


def block_levels(own_key, shape, cuts, low, largest):
    def one(dim, parts):
        draws = jax.random.uniform(jax.random.fold_in(jax.random.fold_in(own_key, 6), dim), (parts,), jnp.float32, low / len(cuts), largest / len(cuts))
        return jnp.repeat(jnp.exp(draws), shape[dim] // parts).reshape((-1,) + (1,) * (len(shape) - dim - 1))

    factor_of = one(*cuts[0])
    for cut in cuts[1:]:
        factor_of = factor_of * one(*cut)
    return factor_of


def shared_out(rng, own, number, rows, amount, top, limit, lean):
    ranking = jax.random.permutation(rng, amount)
    packed, ordinary = portions_of(amount, rows * top, limit, lean, True), portions_of(amount, rows * top, limit, lean, False)
    places = jnp.arange(amount)

    def named(lengths, offset_by):
        used = int((lengths > 0).sum())
        fixed = max(1, used // 4)
        passed = fixed + (places - fixed + offset_by * (used - fixed)) % max(1, amount - fixed)
        return jnp.zeros((amount,), jnp.int32).at[ranking[jnp.where(places < fixed, places, passed)]].set(jnp.asarray(lengths, jnp.int32))

    lengths = jnp.where(number % 4 == 0, named(packed, number // 4), named(ordinary, number - number // 4 - 1))
    mixed = jax.random.permutation(jax.random.fold_in(own, 3), amount)
    source_of, sink = mixed[0:amount // 2 * 2:2], mixed[1:amount // 2 * 2:2]
    margin = jnp.minimum(lengths[source_of] - 1, limit - lengths[sink]) // 2
    margin = jnp.where((source_of == ranking[0]) | (sink == ranking[0]) | (lengths[sink] == 0), 0, jnp.maximum(margin, 0))
    passed = jax.random.randint(jax.random.fold_in(own, 4), (amount // 2,), 0, 1 << 20) % (margin + 1)
    lengths = lengths.at[source_of].add(-passed).at[sink].add(passed)
    members = jnp.searchsorted(jnp.cumsum(lengths), jnp.arange(rows * top), side="right").astype(jnp.int32)
    grid = members.reshape(top, rows).T
    grid = grid[jax.random.permutation(jax.random.fold_in(own, 1), rows)]
    offset_by = jax.random.randint(jax.random.fold_in(own, 2), (rows, 1), 0, top)
    return jnp.take_along_axis(grid, (jnp.arange(top)[None, :] + offset_by) % top, axis=1)


def portions_of(number_of, total, most, slope, full):
    portions = [(1 << 20) // math.isqrt(grade ** slope) + 1 for grade in range(1, number_of + 1)]
    largest = most if full else min(most, max(-(-total // number_of), total * portions[0] // sum(portions)))
    least = 1 if total - largest >= number_of - 1 else 0
    given, spare = [largest] + [least] * (number_of - 1), total - largest - least * (number_of - 1)
    while spare > 0:
        movable = [i for i in range(1, number_of) if given[i] < largest] or [i for i in range(1, number_of) if given[i] < most]
        whole, left = sum([portions[i] for i in movable]), spare
        for i in movable:
            more = min(most - given[i], max(1, left * portions[i] // whole), spare)
            given[i] = given[i] + more
            spare = spare - more
    return np.array(given)


def bell_draw(key, shape, spread, most, pieces=(), held_as=jnp.bfloat16):
    loudness = block_levels(key, shape, pieces, -0.22, 0.18) if pieces else 1.0
    entries = jax.random.normal(key, shape, jnp.float32) * spread * loudness
    return jnp.minimum(jnp.maximum(entries, -most), most).astype(held_as)


def setup_inputs(seed: int = 0) -> dict:
    streams_of = jax.random.split(jax.random.key(seed), 15)
    inputs = bell_draw(streams_of[0], (MICRO, TOKENS, D), 1.0, 6.0, ((1, 4),), jnp.float32)
    cotangent = bell_draw(streams_of[1], (MICRO, TOKENS, D), 1.0, 6.0, ((1, 4),), jnp.float32)
    norm_scale = jnp.clip(1.0 + 0.1 * jax.random.normal(streams_of[2], (N_SECTION, 2, D), jnp.float32), 0.5, 1.5)
    norm_shift = bell_draw(streams_of[3], (N_SECTION, 2, D), 0.3, 3.0, ((0, 2),), jnp.float32)
    proj_weight = bell_draw(streams_of[4], (N_SECTION, D, 3, D), D ** -0.5, 0.21875, ((0, 2), (3, 4)))
    proj_bias = bell_draw(streams_of[5], (N_SECTION, 2, D), 0.5, 3.0, ((0, 2), (2, 4)), jnp.float32)
    attn_weight = bell_draw(streams_of[6], (N_SECTION, D, D), (D // 12) ** -0.5, 0.75, ((0, 2), (1, 4)))
    attn_bias = bell_draw(streams_of[7], (N_SECTION, D), 0.5, 3.0, ((0, 2),), jnp.float32)
    expert_in = bell_draw(streams_of[8], (N_SECTION, EXPERTS, D, HIDDEN_SIZE), D ** -0.5, 0.21875, ((0, 2), (1, 4), (3, 4)))
    expert_in_bias = bell_draw(streams_of[9], (N_SECTION, EXPERTS, HIDDEN_SIZE), 0.5, 3.0, ((0, 2), (1, 4), (2, 4)), jnp.float32)
    expert_out = bell_draw(streams_of[10], (N_SECTION, EXPERTS, HIDDEN_SIZE, D), HIDDEN_SIZE ** -0.5, 0.109375, ((0, 2), (1, 4), (2, 4)))
    expert_out_bias = bell_draw(streams_of[11], (N_SECTION, EXPERTS, D), 0.5, 3.0, ((0, 2), (1, 4)), jnp.float32)
    routes_keys = jax.random.split(jax.random.fold_in(streams_of[12], 1), N_SECTION * MICRO * TOKENS // TOK_DEV)
    routes_turns = jax.random.permutation(jax.random.fold_in(streams_of[12], 3), N_SECTION * MICRO * TOKENS // TOK_DEV)
    routes = jax.vmap(lambda own, number: shared_out(jax.random.fold_in(streams_of[12], 2), own, number, TOK_DEV, EXPERTS, TOPK, CAP, 2))(routes_keys, routes_turns).reshape((N_SECTION, MICRO, TOKENS, TOPK))
    gate_weights = jnp.clip(0.1 + 0.9 * jax.random.uniform(streams_of[13], (N_SECTION, MICRO, TOKENS, TOPK), jnp.float32) ** block_levels(streams_of[13], (N_SECTION, MICRO, TOKENS, TOPK), ((0, 2), (2, 4)), -0.2, 0.2), 0.1, 1.0)
    return dict(inputs=inputs, cotangent=cotangent, norm_scale=norm_scale, norm_shift=norm_shift, proj_weight=proj_weight, proj_bias=proj_bias, attn_weight=attn_weight, attn_bias=attn_bias, expert_in=expert_in, expert_in_bias=expert_in_bias, expert_out=expert_out, expert_out_bias=expert_out_bias, routes=routes, gate_weights=gate_weights)


NORM_EPSILON = 1e-06
GELU_FACTOR = 0.7978845608028654
CUBIC_TERM = 0.044715

def gelu_value(pre_act):
    inner_arg = GELU_FACTOR * (pre_act + CUBIC_TERM * pre_act * pre_act * pre_act)
    return 0.5 * pre_act * (1.0 + jnp.tanh(inner_arg))

def gelu_slope(pre_act):
    tangent = jnp.tanh(GELU_FACTOR * (pre_act + CUBIC_TERM * pre_act * pre_act * pre_act))
    return 0.5 * (1.0 + tangent) + 0.5 * pre_act * (1.0 - tangent * tangent) * GELU_FACTOR * (1.0 + 3.0 * CUBIC_TERM * pre_act * pre_act)

def layer_norm(values, scale_row, shift_row):
    average = lax.optimization_barrier(jnp.mean(values, axis=-1, keepdims=True))
    centred = values - average
    variance = lax.optimization_barrier(jnp.mean(centred * centred, axis=-1, keepdims=True))
    inv_std = lax.rsqrt(variance + NORM_EPSILON)
    normed = centred * inv_std
    return (normed * scale_row + shift_row, normed, inv_std)

def norm_back(grad_normed, normed, inv_std, scale_row):
    scaled = grad_normed * scale_row
    return (scaled - lax.optimization_barrier(jnp.mean(scaled, axis=-1, keepdims=True)) - normed * lax.optimization_barrier(jnp.mean(scaled * normed, axis=-1, keepdims=True))) * inv_std

def slot_table(route_rows, experts, capacity):
    flat_ids = route_rows.reshape(-1).astype(jnp.int32)
    onehot = (flat_ids[:, None] == jnp.arange(experts, dtype=jnp.int32)[None, :]).astype(jnp.int32)
    before = jnp.cumsum(onehot, axis=0) - onehot
    position = lax.optimization_barrier(jnp.sum(before * onehot, axis=1)).astype(jnp.int32)
    return flat_ids * capacity + position

def to_float(values):
    return values.astype(jnp.float32)

def fill_slots(slot_ids, block_rows):

    def one_block(id_row, value_rows):
        return jnp.zeros((EXPERTS * CAP, value_rows.shape[-1]), value_rows.dtype).at[id_row].set(value_rows)
    return jax.vmap(one_block)(slot_ids, block_rows)

def to_experts(buffer):
    width_last = buffer.shape[-1]
    return buffer.reshape(EXPERTS, EXPERTS, CAP, width_last).transpose(1, 0, 2, 3).reshape(EXPERTS, EXPERTS * CAP, width_last)

def to_blocks(by_expert):
    width_last = by_expert.shape[-1]
    return by_expert.reshape(EXPERTS, EXPERTS, CAP, width_last).transpose(1, 0, 2, 3).reshape(EXPERTS, EXPERTS * CAP, width_last)

def pick_slots(table, slot_ids):
    return jax.vmap(lambda table_rows, id_row: table_rows[id_row])(table, slot_ids)

def attend(query_rows, key_rows, value_rows):
    scores = jnp.einsum('ishe,ithe->ihst', to_float(query_rows), to_float(key_rows)) * HEAD_DIM ** (-0.5)
    log_total = jnp.log(lax.optimization_barrier(jnp.sum(jnp.exp(scores), axis=-1)))
    prob_rows = jnp.exp(scores - log_total[..., None]).astype(jnp.bfloat16)
    attn_mixed = jnp.einsum('ihst,ithe->ishe', to_float(prob_rows), to_float(value_rows)).astype(jnp.bfloat16)
    return (attn_mixed, log_total)

def attend_back(query_rows, key_rows, value_rows, attn_mixed, log_total, grad_mixed):
    scale_factor = HEAD_DIM ** (-0.5)
    scores = jnp.einsum('ishe,ithe->ihst', to_float(query_rows), to_float(key_rows)) * scale_factor
    prob_f = jnp.exp(scores - log_total[..., None])
    prob_rows = prob_f.astype(jnp.bfloat16)
    grad_values = jnp.einsum('ihst,ishe->ithe', to_float(prob_rows), to_float(grad_mixed))
    grad_probs = jnp.einsum('ishe,ithe->ihst', to_float(grad_mixed), to_float(value_rows))
    row_delta = jnp.einsum('ishe,ishe->ihs', to_float(grad_mixed), to_float(attn_mixed))
    grad_scores = (prob_f * (grad_probs - row_delta[..., None]) * scale_factor).astype(jnp.bfloat16)
    grad_query = jnp.einsum('ihst,ithe->ishe', to_float(grad_scores), to_float(key_rows))
    grad_keys = jnp.einsum('ihst,ishe->ithe', to_float(grad_scores), to_float(query_rows))
    return (grad_query, grad_keys, grad_values)

def forward_block(inputs, weights, route_rows, gate_rows):
    norm_scale, norm_shift, proj_weight, proj_bias, attn_weight, attn_bias, expert_in, expert_in_bias, expert_out, expert_out_bias = weights
    head_shape = (IMAGES, SEQ, HEADS, HEAD_DIM)
    normed_out, normed_first, inv_first = layer_norm(inputs, norm_scale[0], norm_shift[0])
    normed_a = normed_out.astype(jnp.bfloat16)
    projected = jnp.einsum('rd,dkf->rkf', to_float(normed_a), to_float(proj_weight))
    query_rows = (projected[:, 0] + proj_bias[0]).astype(jnp.bfloat16).reshape(head_shape)
    key_rows = projected[:, 1].astype(jnp.bfloat16).reshape(head_shape)
    value_rows = (projected[:, 2] + proj_bias[1]).astype(jnp.bfloat16).reshape(head_shape)
    attn_mixed, log_total = attend(query_rows, key_rows, value_rows)
    mixed_flat = attn_mixed.reshape(TOKENS, D)
    hidden_res = inputs + (jnp.dot(mixed_flat, attn_weight, preferred_element_type=jnp.float32) + attn_bias)
    normed_out_b, normed_second, inv_second = layer_norm(hidden_res, norm_scale[1], norm_shift[1])
    normed_b = normed_out_b.astype(jnp.bfloat16)
    slot_ids = jax.vmap(lambda rows_here: slot_table(rows_here, EXPERTS, CAP))(route_rows.reshape(EXPERTS, TOK_DEV, TOPK))
    repeated = jnp.repeat(normed_b.reshape(EXPERTS, TOK_DEV, D), TOPK, axis=1)
    by_expert = to_experts(fill_slots(slot_ids, repeated))

    def one_expert(operands):
        rows_here, weight_in, bias_in, weight_out, bias_out = operands
        pre_act = jnp.dot(rows_here, weight_in, preferred_element_type=jnp.float32) + bias_in
        activated = gelu_value(pre_act).astype(jnp.bfloat16)
        result_rows = (jnp.dot(activated, weight_out, preferred_element_type=jnp.float32) + bias_out).astype(jnp.bfloat16)
        return (result_rows, pre_act)
    expert_result, pre_act = lax.map(one_expert, (by_expert, expert_in, expert_in_bias, expert_out, expert_out_bias))
    picked = pick_slots(to_blocks(expert_result), slot_ids)
    branch = lax.optimization_barrier(jnp.sum(gate_rows.reshape(TOKENS, TOPK, 1) * to_float(picked).reshape(TOKENS, TOPK, D), axis=1))
    block_out = hidden_res + branch
    kept_state = (normed_first, inv_first, query_rows, key_rows, value_rows, attn_mixed, log_total, normed_second, inv_second, slot_ids, gate_rows, by_expert, pre_act)
    return (block_out, kept_state)

def backward_block(cotangent, weights, kept_state):
    norm_scale, norm_shift, proj_weight, proj_bias, attn_weight, attn_bias, expert_in, expert_in_bias, expert_out, expert_out_bias = weights
    normed_first, inv_first, query_rows, key_rows, value_rows, attn_mixed, log_total, normed_second, inv_second, slot_ids, gate_rows, by_expert, pre_act = kept_state
    head_shape = (IMAGES, SEQ, HEADS, HEAD_DIM)
    grad_rows = (gate_rows.reshape(TOKENS, TOPK, 1) * cotangent[:, None, :]).astype(jnp.bfloat16).reshape(EXPERTS, TOPK * TOK_DEV, D)
    grad_by_expert = to_experts(fill_slots(slot_ids, grad_rows))

    def one_expert_back(operands):
        rows_here, pre_here, grad_here, weight_in, weight_out = operands
        activated = gelu_value(pre_here).astype(jnp.bfloat16)
        grad_weight_out = jnp.dot(activated.T, grad_here, preferred_element_type=jnp.float32)
        grad_bias_out = lax.optimization_barrier(jnp.sum(to_float(grad_here), axis=0))
        grad_pre = jnp.dot(grad_here, weight_out.T, preferred_element_type=jnp.float32) * gelu_slope(pre_here)
        grad_bias_in = lax.optimization_barrier(jnp.sum(grad_pre, axis=0))
        grad_pre_b = grad_pre.astype(jnp.bfloat16)
        grad_weight_in = jnp.dot(rows_here.T, grad_pre_b, preferred_element_type=jnp.float32)
        grad_buffer = jnp.dot(grad_pre_b, weight_in.T, preferred_element_type=jnp.float32).astype(jnp.bfloat16)
        return (grad_weight_in, grad_bias_in, grad_weight_out, grad_bias_out, grad_buffer)
    grad_expert_in, grad_expert_in_bias, grad_expert_out, grad_expert_out_bias, grad_buffer = lax.map(one_expert_back, (by_expert, pre_act, grad_by_expert, expert_in, expert_out))
    picked = pick_slots(to_blocks(grad_buffer), slot_ids)
    grad_normed_b = lax.optimization_barrier(jnp.sum(to_float(picked).reshape(TOKENS, TOPK, D), axis=1))
    grad_hidden = cotangent + norm_back(grad_normed_b, normed_second, inv_second, norm_scale[1])
    grad_hidden_b = grad_hidden.astype(jnp.bfloat16)
    grad_attn_bias = lax.optimization_barrier(jnp.sum(grad_hidden, axis=0))
    mixed_flat = attn_mixed.reshape(TOKENS, D)
    grad_attn_weight = jnp.dot(mixed_flat.T, grad_hidden_b, preferred_element_type=jnp.float32)
    grad_mixed = jnp.dot(grad_hidden_b, attn_weight.T, preferred_element_type=jnp.float32).astype(jnp.bfloat16).reshape(head_shape)
    grad_query, grad_keys, grad_values = attend_back(query_rows, key_rows, value_rows, attn_mixed, log_total, grad_mixed)
    query_flat = grad_query.reshape(TOKENS, D)
    key_flat = grad_keys.reshape(TOKENS, D)
    value_flat = grad_values.reshape(TOKENS, D)
    grad_proj_bias = jnp.stack([lax.optimization_barrier(jnp.sum(query_flat, axis=0)), lax.optimization_barrier(jnp.sum(value_flat, axis=0))])
    grad_proj = jnp.stack([query_flat, key_flat, value_flat], axis=1).astype(jnp.bfloat16)
    normed_a = (normed_first * norm_scale[0] + norm_shift[0]).astype(jnp.bfloat16)
    grad_proj_weight = jnp.einsum('rd,rkf->dkf', to_float(normed_a), to_float(grad_proj))
    grad_normed_a = jnp.einsum('rkf,dkf->rd', to_float(grad_proj), to_float(proj_weight))
    grad_input = grad_hidden + norm_back(grad_normed_a, normed_first, inv_first, norm_scale[0])
    grad_norm_scale = jnp.stack([lax.optimization_barrier(jnp.sum(grad_normed_a * normed_first, axis=0)), lax.optimization_barrier(jnp.sum(grad_normed_b * normed_second, axis=0))])
    grad_norm_shift = jnp.stack([lax.optimization_barrier(jnp.sum(grad_normed_a, axis=0)), lax.optimization_barrier(jnp.sum(grad_normed_b, axis=0))])
    grad_parts = (grad_norm_scale, grad_norm_shift, grad_proj_weight, grad_proj_bias, grad_attn_weight, grad_attn_bias, grad_expert_in, grad_expert_in_bias, grad_expert_out, grad_expert_out_bias)
    return (grad_input, grad_parts)

def reference(inputs, cotangent, norm_scale, norm_shift, proj_weight, proj_bias, attn_weight, attn_bias, expert_in, expert_in_bias, expert_out, expert_out_bias, routes, gate_weights):
    params = (norm_scale, norm_shift, proj_weight, proj_bias, attn_weight, attn_bias, expert_in, expert_in_bias, expert_out, expert_out_bias)
    section_outputs = []
    section_kept = []
    current = [inputs[micro_index] for micro_index in range(MICRO)]
    for section_index in range(N_SECTION):
        weights = tuple((member[section_index] for member in params))
        outputs_here = []
        kept_here = []
        for micro_index in range(MICRO):
            block_out, kept_state = forward_block(current[micro_index], weights, routes[section_index, micro_index], gate_weights[section_index, micro_index])
            outputs_here.append(block_out)
            kept_here.append(kept_state)
        section_outputs.append(jnp.stack(outputs_here))
        section_kept.append(kept_here)
        current = outputs_here
    section_grads = [None] * N_SECTION
    input_grads = [None] * N_SECTION
    flowing = [cotangent[micro_index] for micro_index in range(MICRO)]
    for section_index in reversed(range(N_SECTION)):
        weights = tuple((member[section_index] for member in params))
        running = None
        grads_here = []
        for micro_index in range(MICRO):
            grad_input, grad_parts = backward_block(flowing[micro_index], weights, section_kept[section_index][micro_index])
            running = grad_parts if running is None else jax.tree.map(jnp.add, running, grad_parts)
            grads_here.append(grad_input)
        section_grads[section_index] = running
        input_grads[section_index] = jnp.stack(grads_here)
        flowing = grads_here
    stacked = [jnp.stack([section_grads[section_index][member] for section_index in range(N_SECTION)]) for member in range(10)]
    return (jnp.stack(section_outputs), jnp.stack(input_grads), stacked[0], stacked[1], stacked[2], stacked[3], stacked[4], stacked[5], stacked[6], stacked[7], stacked[8], stacked[9])
```

```python
import functools
import types

import jax
import jax.numpy as jnp
from jax import lax
from jax.experimental import pallas as pl
from jax.experimental.pallas import tpu as pltpu
from jax.sharding import PartitionSpec as P

HEAD_DIM = 64
TOPK = 2

NORM_EPSILON = 1e-06
GELU_FACTOR = 0.7978845608028654
CUBIC_TERM = 0.044715

MESH = pl.DeviceIdType.MESH
ROW_TILE = 16
BF16 = jnp.bfloat16
F32 = jnp.float32

(
    RS_ATTN,
    AG_ATTN,
    DISPATCH,
    PARTS,
    RS_MOE,
    AG_MOE,
    CROSS,
    RESID,
    GRADS,
    GRAD_PARTS,
    RS_GRAD,
    AG_GRAD,
    RS_PROJ,
    AG_PROJ,
    ALL_NORMED,
    ALL_MIXED,
    ALL_HIDDEN,
    ALL_PROJ,
    SMALL_E,
    SMALL_T,
    PHASES,
) = range(21)


def nn(left, right):
    return jnp.dot(left, right, preferred_element_type=F32)


def nt(left, right):
    return lax.dot_general(left, right, (((1,), (1,)), ((), ())), preferred_element_type=F32)


def tn(left, right):
    return lax.dot_general(left, right, (((0,), (0,)), ((), ())), preferred_element_type=F32)


def standardize(values):
    average = jnp.mean(values, axis=-1, keepdims=True)
    centred = values - average
    variance = jnp.mean(centred * centred, axis=-1, keepdims=True)
    inv_std = lax.rsqrt(variance + NORM_EPSILON)
    return centred * inv_std, inv_std


def norm_back(grad_normed, normed, inv_std, scale_row):
    scaled = grad_normed * scale_row
    return (
        scaled
        - jnp.mean(scaled, axis=-1, keepdims=True)
        - normed * jnp.mean(scaled * normed, axis=-1, keepdims=True)
    ) * inv_std


def iota(shape, axis):
    return lax.broadcasted_iota(jnp.int32, shape, axis)


class Swap:
    def __init__(self, r, phase, axis, source, landing):
        self.r, self.phase, self.axis = r, phase, axis
        self.size = lax.axis_size(axis)
        self.me = lax.axis_index(axis)
        self.source, self.landing = source, landing

    def ahead(self, k):
        return lax.rem(self.me + k, self.size)

    def behind(self, k):
        return lax.rem(self.me + self.size - k, self.size)

    def copy(self, k):
        there = self.ahead(k)
        return pltpu.make_async_remote_copy(
            src_ref=self.source(there),
            dst_ref=self.landing(k),
            send_sem=self.r.send_sem.at[self.phase, k],
            recv_sem=self.r.recv_sem.at[self.phase, k],
            device_id={self.axis: there},
            device_id_type=MESH,
        )

    def start(self, k):
        self.copy(k).start()

    def start_all(self):
        for k in range(1, self.size):
            self.start(k)

    def wait(self, k):
        self.copy(k).wait_recv()

    def wait_all(self):
        for k in range(1, self.size):
            self.wait(k)

    def drain(self):
        for k in range(1, self.size):
            self.copy(k).wait_send()


def relay_kernel(names, d, *refs):
    r = types.SimpleNamespace(**dict(zip(names, refs)))
    E, T, R, RG, RP, CH = d.E, d.T, d.R, d.RG, d.RP, d.CH
    CAP, D, W, HW = d.CAP, d.D, d.W, d.HW
    heads = W // HEAD_DIM
    scale_factor = HEAD_DIM ** (-0.5)
    s, e, t = [lax.axis_index(name) for name in ("section", "expert", "tensor")]
    other = 1 - s
    at_first, at_second = s == 0, s == 1

    def swap(phase, axis, source, landing):
        return Swap(r, phase, axis, source, landing)

    def gather(phase, axis, ref, me):
        return swap(phase, axis, lambda there: ref.at[me], lambda k: ref.at[me])

    def scatter(phase, axis, source, landing):
        return swap(phase, axis, lambda there: source.at[there], lambda k: landing.at[k - 1])

    rs_attn = scatter(RS_ATTN, "tensor", r.p1, r.l1)
    ag_attn = gather(AG_ATTN, "tensor", r.t1, t)
    rs_moe = scatter(RS_MOE, "tensor", r.p2, r.l2)
    ag_moe = gather(AG_MOE, "tensor", r.t2, t)
    rs_grad = scatter(RS_GRAD, "tensor", r.p3, r.l3)
    ag_grad = gather(AG_GRAD, "tensor", r.t3, t)
    rs_proj = scatter(RS_PROJ, "tensor", r.p4, r.l4)
    ag_proj = gather(AG_PROJ, "tensor", r.t4, t)

    def routed(phase, source, landing):
        return swap(phase, "expert", lambda there: source.at[there], lambda k: landing.at[e])

    dispatch = routed(DISPATCH, r.o1, r.b1)
    parts = routed(PARTS, r.o2, r.b2)
    grads = routed(GRADS, r.o3, r.b3)
    grad_parts = routed(GRAD_PARTS, r.o4, r.b4)
    all_normed = gather(ALL_NORMED, "expert", r.na, e)
    all_mixed = gather(ALL_MIXED, "expert", r.am, e)
    all_hidden = gather(ALL_HIDDEN, "expert", r.gh_all, e)
    all_proj = gather(ALL_PROJ, "expert", r.gp, e)
    small_e = swap(SMALL_E, "expert", lambda there: r.small, lambda k: r.small_e.at[k - 1])
    small_t = swap(SMALL_T, "tensor", lambda there: r.small2, lambda k: r.small_t.at[k - 1])

    def cross_copy(source, k):
        there = lax.rem(t + k, T)
        return pltpu.make_async_remote_copy(
            src_ref=source,
            dst_ref=r.delta_in.at[t],
            send_sem=r.send_sem.at[CROSS, k],
            recv_sem=r.recv_sem.at[CROSS, k],
            device_id={"section": other, "tensor": there},
            device_id_type=MESH,
        )

    def resid_copy(source):
        return pltpu.make_async_remote_copy(
            src_ref=source,
            dst_ref=r.resid_in,
            send_sem=r.send_sem.at[RESID, 0],
            recv_sem=r.recv_sem.at[RESID, 0],
            device_id={"section": other},
            device_id_type=MESH,
        )

    def from_other_section():
        resid_copy(r.resid_in).wait_recv()
        for k in range(T):
            cross_copy(r.delta_in.at[t], k).wait_recv()
        return r.resid_in[...] + r.delta_in[...].reshape(RP, D).astype(F32)

    barrier = pltpu.get_barrier_semaphore()
    friends = [{"tensor": lax.rem(t + k, T)} for k in range(1, T)]
    friends += [{"expert": lax.rem(e + k, E)} for k in range(1, E)]
    friends += [{"section": other, "tensor": lax.rem(t + k, T)} for k in range(T)]
    for device in friends:
        pl.semaphore_signal(barrier, inc=1, device_id=device, device_id_type=MESH)
    pl.semaphore_wait(barrier, len(friends))

    def rows_of(chunk):
        return pl.ds(pl.multiple_of(chunk * CH, CH), CH)

    def route_cols(rows=slice(None)):
        ids, gates = r.rt[rows, :], r.gt[rows, :]
        return ids[:, 0:1], ids[:, 1:2], gates[:, 0:1], gates[:, 1:2]

    def gate_of(expert, rows=slice(None)):
        id0, id1, gate0, gate1 = route_cols(rows)
        return jnp.where(id0 == expert, gate0, 0.0) + jnp.where(id1 == expert, gate1, 0.0)

    def routing():
        r.rt[...] = jnp.full((RP, TOPK), -1, jnp.int32)
        r.gt[...] = jnp.zeros((RP, TOPK), F32)
        r.rt[0:R, :] = r.routes[...]
        r.gt[0:R, :] = r.gate_weights[...]
        id0, id1, _, _ = route_cols()
        lane = iota((RP, 128), 1)
        named = jnp.where((id0 == lane) | (id1 == lane), 1.0, 0.0)
        named_b = named.astype(BF16)
        down, across = iota((RP, RP), 0), iota((RP, RP), 1)
        earlier = jnp.where(across < down, 1.0, 0.0).astype(BF16)
        later = jnp.where(down < across, 1.0, 0.0).astype(BF16)
        same = jnp.where(down == across, 1.0, 0.0).astype(BF16)
        slot = jnp.where(named > 0.5, nn(earlier, named_b), -1.0)
        slot_t = jnp.where(tn(named_b, same) > 0.5, tn(named_b, later), -1.0)
        wide = iota((RP, CAP), 1).astype(F32)
        tall = iota((CAP, RP), 0).astype(F32)
        for k in range(E):
            r.pick[k] = jnp.where(slot[:, k : k + 1] == wide, 1.0, 0.0).astype(BF16)
            r.place[k] = jnp.where(slot_t[k : k + 1, :] == tall, 1.0, 0.0).astype(BF16)

    def dispatch_grads():
        def outgoing(expert):
            weighted = (gate_of(expert) * r.g[...]).astype(BF16)
            return nn(r.place[expert], weighted).astype(BF16)

        def one(k, carry):
            there = grads.ahead(k)
            r.o3[there] = outgoing(there)
            grads.start(k)
            return carry

        lax.fori_loop(1, E, one, 0)
        r.b3[e] = outgoing(e)

    def each_block(swapped, body):
        body(e, 0)

        def one(k, carry):
            swapped.wait(k)
            body(swapped.behind(k), k)
            return carry

        lax.fori_loop(1, E, one, 0)

    def send_part(swapped, outgoing, landing, image, k, value):
        if isinstance(k, int):
            landing[image] = value
        else:
            outgoing[image] = value
            swapped.start(E - k)

    def raw_block(image):
        r.raw[image] = nt(r.b3[image], r.expert_out[...])

    def backward_part(image, k):
        grad_pre = r.raw[image] * r.slope[image]
        r.in_bias[...] = r.in_bias[...] + jnp.sum(grad_pre, axis=0, keepdims=True)
        grad_pre_b = grad_pre.astype(BF16)
        r.gpb[image] = grad_pre_b
        value = nt(grad_pre_b, r.expert_in[...]).astype(BF16)
        send_part(grad_parts, r.o4, r.b4, image, k, value)

    def forward_part(image, k):
        bias = jnp.where(t == 0, r.expert_out_bias[...], 0.0)
        value = (nn(r.act[image], r.expert_out[...]) + bias).astype(BF16)
        send_part(parts, r.o2, r.b2, image, k, value)

    def expert_block(image):
        pre = nn(r.b1[image], r.expert_in[...]) + r.expert_in_bias[...]
        square = pre * pre
        tangent = jnp.tanh(GELU_FACTOR * (pre + CUBIC_TERM * square * pre))
        half = 0.5 * (1.0 + tangent)
        r.act[image] = (pre * half).astype(BF16)
        r.slope[image] = half + 0.5 * pre * (1.0 - tangent * tangent) * GELU_FACTOR * (
            1.0 + 3.0 * CUBIC_TERM * square
        )

    def scatter_chunks(swapped, part, chunk_of):
        for k in range(1, T):
            there = swapped.ahead(k)
            part[there] = chunk_of(there).astype(BF16)
            swapped.start(k)
        return chunk_of(t)

    def collect(swapped, landing, own):
        for k in range(1, T):
            swapped.wait(k)
            own = own + landing[k - 1].astype(F32)
        return own

    def combined(landed, gated, chunk):
        rows = rows_of(chunk)
        total = None
        for k in range(E):
            term = nn(r.pick[k, rows, :], landed[k])
            if gated:
                term = gate_of(k, rows) * term
            total = term if total is None else total + term
        return total

    def finish_forward():
        parts.wait_all()
        own = scatter_chunks(rs_moe, r.p2, lambda chunk: combined(r.b2, True, chunk))
        own = collect(rs_moe, r.l2, own)
        r.t2[t] = own.astype(BF16)

    def write_forward():
        ag_moe.wait_all()
        out = r.hidden[...] + r.t2[...].reshape(RP, D).astype(F32)
        r.section_out[...] = out[0:R]

    r.in_bias[...] = jnp.zeros((1, HW), F32)
    r.small[...] = jnp.zeros((8, D), F32)

    @pl.when(at_first)
    def _():
        r.x[...] = jnp.zeros((RP, D), F32)
        r.x[0:R, :] = r.inputs[...]

    @pl.when(at_second)
    def _():
        routing()
        r.g[...] = jnp.zeros((RP, D), F32)
        r.g[0:R, :] = r.cotangent[...]
        dispatch_grads()
        each_block(grads, lambda image, k: raw_block(image))
        r.x[...] = from_other_section()

    inside = iota((RP, 1), 0) < R
    scale0, scale1 = r.norm_scale[0:1, :], r.norm_scale[1:2, :]
    shift0, shift1 = r.norm_shift[0:1, :], r.norm_shift[1:2, :]
    normed_first, _ = standardize(r.x[...])
    normed_a = jnp.where(inside, normed_first * scale0 + shift0, 0.0).astype(BF16)
    r.na[e] = normed_a[0:RG]
    query = nt(normed_a, r.proj_weight[0]) + r.proj_bias[0:1, :]
    r.qkv[0] = jnp.where(inside, query, 0.0).astype(BF16)
    r.qkv[1] = nt(normed_a, r.proj_weight[1]).astype(BF16)
    value = nt(normed_a, r.proj_weight[2]) + r.proj_bias[1:2, :]
    r.qkv[2] = jnp.where(inside, value, 0.0).astype(BF16)
    real_key = iota((RP, RP), 1) < R
    mixed = []
    for h in range(heads):
        cols = slice(h * HEAD_DIM, (h + 1) * HEAD_DIM)
        scores = nt(r.qkv[0][:, cols], r.qkv[1][:, cols]) * scale_factor
        powers = jnp.where(real_key, jnp.exp(scores), 0.0)
        probs = powers / jnp.sum(powers, axis=-1, keepdims=True)
        r.probs[h] = probs
        mixed.append(nn(probs.astype(BF16), r.qkv[2][:, cols]))
    r.mixed[...] = jnp.concatenate(mixed, axis=1).astype(BF16)
    r.am[e] = r.mixed[0:RG, :]
    own = scatter_chunks(
        rs_attn, r.p1, lambda chunk: nn(r.mixed[rows_of(chunk), :], r.attn_weight[...])
    )
    all_normed.start_all()
    all_mixed.start_all()

    @pl.when(at_first)
    def _():
        routing()

    r.t1[t] = collect(rs_attn, r.l1, own).astype(BF16)
    ag_attn.start_all()
    ag_attn.wait_all()
    hidden = r.x[...] + (r.t1[...].reshape(RP, D).astype(F32) + r.attn_bias[...])
    r.hidden[...] = hidden

    @pl.when(at_first)
    def _():
        resid_copy(r.hidden).start()

    normed_second, inv_second = standardize(hidden)
    r.h2[...] = normed_second
    r.r2[...] = inv_second
    r.nb[...] = (normed_second * scale1 + shift1).astype(BF16)

    def dispatch_one(k, carry):
        there = dispatch.ahead(k)
        r.o1[there] = nn(r.place[there], r.nb[...]).astype(BF16)
        dispatch.start(k)
        return carry

    lax.fori_loop(1, E, dispatch_one, 0)
    r.b1[e] = nn(r.place[e], r.nb[...]).astype(BF16)

    @pl.when(at_first)
    def _():
        def both(image, k):
            expert_block(image)
            forward_part(image, k)

        each_block(dispatch, both)
        finish_forward()
        for k in range(T):
            cross_copy(r.t2.at[t], k).start()
        ag_moe.start_all()
        write_forward()
        r.g[...] = from_other_section()
        dispatch_grads()

        def back(image, k):
            raw_block(image)
            backward_part(image, k)

        each_block(grads, back)

    @pl.when(at_second)
    def _():
        def both(image, k):
            expert_block(image)
            backward_part(image, k)

        each_block(dispatch, both)

    slots = E * CAP
    r.grad_expert_out[...] = tn(
        r.act[...].reshape(slots, HW), r.b3[...].reshape(slots, D)
    )
    r.grad_expert_out_bias[...] = jnp.sum(
        r.b3[...].reshape(slots, D).astype(F32), axis=0, keepdims=True
    )
    grad_parts.wait_all()
    own = scatter_chunks(rs_grad, r.p3, lambda chunk: combined(r.b4, False, chunk))
    r.grad_expert_in[...] = tn(
        r.b1[...].reshape(slots, D), r.gpb[...].reshape(slots, HW)
    )
    r.grad_expert_in_bias[...] = r.in_bias[...]
    grad_normed_b = collect(rs_grad, r.l3, own)
    mine = rows_of(t)
    normed_mine = r.h2[mine, :]
    delta = norm_back(grad_normed_b, normed_mine, r.r2[mine, :], scale1)
    r.t3[t] = delta.astype(BF16)
    ag_grad.start_all()
    r.small[1:2, :] = jnp.sum(grad_normed_b * normed_mine, axis=0, keepdims=True)
    r.small[3:4, :] = jnp.sum(grad_normed_b, axis=0, keepdims=True)
    ag_grad.wait_all()
    grad_hidden = r.g[...] + r.t3[...].reshape(RP, D).astype(F32)
    r.g[...] = grad_hidden

    @pl.when(at_second)
    def _():
        resid_copy(r.g).start()

    r.small[4:5, :] = jnp.sum(r.g[mine, :], axis=0, keepdims=True)
    grad_hidden_b = grad_hidden.astype(BF16)
    r.gh_all[e] = grad_hidden_b[0:RG]
    all_hidden.start_all()
    grad_mixed = nt(grad_hidden_b, r.attn_weight[...]).astype(BF16)
    found = [[], [], []]
    for h in range(heads):
        cols = slice(h * HEAD_DIM, (h + 1) * HEAD_DIM)
        query, key, value = r.qkv[0][:, cols], r.qkv[1][:, cols], r.qkv[2][:, cols]
        grad_mixed_h = grad_mixed[:, cols]
        probs = r.probs[h]
        grad_values = tn(probs.astype(BF16), grad_mixed_h)
        grad_probs = nt(grad_mixed_h, value)
        row_delta = jnp.sum(
            grad_mixed_h.astype(F32) * r.mixed[...][:, cols].astype(F32), axis=-1, keepdims=True
        )
        grad_scores = (probs * (grad_probs - row_delta) * scale_factor).astype(BF16)
        found[0].append(nn(grad_scores, key))
        found[1].append(tn(grad_scores, query))
        found[2].append(grad_values)
    for j in range(3):
        flat = jnp.concatenate(found[j], axis=1)
        if j != 1:
            row = 5 + j // 2
            r.small[row : row + 1, 0:W] = jnp.sum(flat, axis=0, keepdims=True)
        r.grad_flat[j] = flat.astype(BF16)
        r.gp[e, j] = r.grad_flat[j, 0:RG, :]

    def proj_chunk(chunk):
        rows = rows_of(chunk)
        total = nn(r.grad_flat[0, rows, :], r.proj_weight[0])
        for j in (1, 2):
            total = total + nn(r.grad_flat[j, rows, :], r.proj_weight[j])
        return total

    own = scatter_chunks(rs_proj, r.p4, proj_chunk)
    all_proj.start_all()
    normed_mine, inv_mine = standardize(r.x[mine, :])
    grad_normed_a = collect(rs_proj, r.l4, own)
    r.t4[t] = norm_back(grad_normed_a, normed_mine, inv_mine, scale0).astype(BF16)

    @pl.when(at_second)
    def _():
        for k in range(T):
            cross_copy(r.t4.at[t], k).start()

    ag_proj.start_all()
    r.small[0:1, :] = jnp.sum(grad_normed_a * normed_mine, axis=0, keepdims=True)
    r.small[2:3, :] = jnp.sum(grad_normed_a, axis=0, keepdims=True)
    small_e.start_all()

    @pl.when(at_second)
    def _():
        forward_part(e, 0)

        def one(k, carry):
            forward_part(parts.behind(k), k)
            return carry

        lax.fori_loop(1, E, one, 0)
        finish_forward()
        ag_moe.start_all()
        write_forward()

    all_mixed.wait_all()
    all_hidden.wait_all()
    all_normed.wait_all()
    tokens = E * RG
    r.grad_attn_weight[...] = tn(
        r.am[...].reshape(tokens, W), r.gh_all[...].reshape(tokens, D)
    )
    small_e.wait_all()
    total = r.small[...]
    for k in range(1, E):
        total = total + r.small_e[k - 1]
    r.small2[...] = total
    small_t.start_all()
    all_proj.wait_all()
    for j in range(3):
        r.grad_proj[j] = tn(
            r.gp[:, j].reshape(tokens, W), r.na[...].reshape(tokens, D)
        )
    small_t.wait_all()
    total = r.small2[...]
    r.small_out[5:8, :] = total[5:8]
    for k in range(1, T):
        total = total + r.small_t[k - 1]
    r.small_out[0:5, :] = total[0:5]
    ag_proj.wait_all()
    grad_in = r.g[...] + r.t4[...].reshape(RP, D).astype(F32)
    r.section_in_grad[...] = grad_in[0:R]

    for swapped in (
        rs_attn, ag_attn, rs_moe, ag_moe, rs_grad, ag_grad, rs_proj, ag_proj,
        dispatch, parts, grads, grad_parts,
        all_normed, all_mixed, all_hidden, all_proj, small_e, small_t,
    ):
        swapped.drain()
    resid_copy(r.resid_in).wait_send()
    for k in range(T):
        cross_copy(r.t4.at[t], k).wait_send()


def slot_count(row_count, experts):
    return max(2, (3 * TOPK * row_count + 2 * experts - 1) // (2 * experts))


def round_up(value, unit):
    return -(-value // unit) * unit


def on_device(
    inputs,
    cotangent,
    norm_scale,
    norm_shift,
    proj_weight,
    proj_bias,
    attn_weight,
    attn_bias,
    expert_in,
    expert_in_bias,
    expert_out,
    expert_out_bias,
    routes,
    gate_weights,
):
    E, T = lax.axis_size("expert"), lax.axis_size("tensor")
    R, D = inputs.shape[1:]
    W, HW = proj_weight.shape[3], expert_in.shape[3]
    CH = round_up(-(-R // T), ROW_TILE)
    RP = T * CH
    CAP = round_up(slot_count(R, E), ROW_TILE)
    RG = round_up(R, ROW_TILE)
    d = types.SimpleNamespace(E=E, T=T, R=R, RG=RG, RP=RP, CH=CH, CAP=CAP, D=D, W=W, HW=HW)
    heads = W // HEAD_DIM

    operands = dict(
        inputs=inputs[0],
        cotangent=cotangent[0],
        norm_scale=norm_scale[0],
        norm_shift=norm_shift[0],
        proj_weight=jnp.transpose(proj_weight[0], (1, 2, 0)),
        proj_bias=proj_bias[0],
        attn_weight=attn_weight[0],
        attn_bias=attn_bias,
        expert_in=expert_in[0, 0],
        expert_in_bias=expert_in_bias[0],
        expert_out=expert_out[0, 0],
        expert_out_bias=expert_out_bias[0],
        routes=routes[0, 0],
        gate_weights=gate_weights[0, 0],
    )
    results = dict(
        section_out=(R, D),
        section_in_grad=(R, D),
        small_out=(8, D),
        grad_proj=(3, W, D),
        grad_attn_weight=(W, D),
        grad_expert_in=(D, HW),
        grad_expert_in_bias=(1, HW),
        grad_expert_out=(HW, D),
        grad_expert_out_bias=(1, D),
    )
    scratch = dict(
        x=((RP, D), F32),
        g=((RP, D), F32),
        hidden=((RP, D), F32),
        h2=((RP, D), F32),
        r2=((RP, 1), F32),
        nb=((RP, D), BF16),
        resid_in=((RP, D), F32),
        delta_in=((T, CH, D), BF16),
        qkv=((3, RP, W), BF16),
        probs=((heads, RP, RP), F32),
        na=((E, RG, D), BF16),
        am=((E, RG, W), BF16),
        mixed=((RP, W), BF16),
        gh_all=((E, RG, D), BF16),
        gp=((E, 3, RG, W), BF16),
        grad_flat=((3, RP, W), BF16),
        rt=((RP, TOPK), jnp.int32),
        gt=((RP, TOPK), F32),
        pick=((E, RP, CAP), BF16),
        place=((E, CAP, RP), BF16),
        act=((E, CAP, HW), BF16),
        gpb=((E, CAP, HW), BF16),
        slope=((E, CAP, HW), F32),
        raw=((E, CAP, HW), F32),
        in_bias=((1, HW), F32),
        small=((8, D), F32),
        small2=((8, D), F32),
        small_e=((E - 1, 8, D), F32),
        small_t=((T - 1, 8, D), F32),
    )
    for k in range(1, 5):
        scratch[f"p{k}"] = ((T, CH, D), BF16)
        scratch[f"l{k}"] = ((T - 1, CH, D), BF16)
        scratch[f"t{k}"] = ((T, CH, D), BF16)
        scratch[f"o{k}"] = ((E, CAP, D), BF16)
        scratch[f"b{k}"] = ((E, CAP, D), BF16)
    sems = pltpu.SemaphoreType.DMA((PHASES, max(E, T)))
    names = list(operands) + list(results) + list(scratch) + ["send_sem", "recv_sem"]
    in_vmem = pl.BlockSpec(memory_space=pltpu.VMEM)
    found = pl.pallas_call(
        functools.partial(relay_kernel, names, d),
        out_shape=[jax.ShapeDtypeStruct(shape, F32) for shape in results.values()],
        in_specs=[in_vmem] * len(operands),
        out_specs=[in_vmem] * len(results),
        scratch_shapes=[pltpu.VMEM(shape, dtype) for shape, dtype in scratch.values()]
        + [sems, sems],
        compiler_params=pltpu.CompilerParams(
            collective_id=0, has_side_effects=True, vmem_limit_bytes=60 * 2**20
        ),
        name="relay",
    )(*operands.values())
    found = types.SimpleNamespace(**dict(zip(results, found)))
    small = found.small_out
    return (
        found.section_out[None, None],
        found.section_in_grad[None, None],
        small[None, 0:2],
        small[None, 2:4],
        jnp.transpose(found.grad_proj, (2, 0, 1))[None],
        small[None, 5:7, 0:W],
        found.grad_attn_weight[None],
        small[4:5],
        found.grad_expert_in[None, None],
        found.grad_expert_in_bias[None],
        found.grad_expert_out[None, None],
        found.grad_expert_out_bias[None],
    )


def solution(mesh):
    in_specs = (
        P(None, "expert", None),
        P(None, "expert", None),
        P("section", None, None),
        P("section", None, None),
        P("section", None, None, "tensor"),
        P("section", None, "tensor"),
        P("section", "tensor", None),
        P("section", None),
        P("section", "expert", None, "tensor"),
        P("section", "expert", "tensor"),
        P("section", "expert", "tensor", None),
        P("section", "expert", None),
        P("section", None, "expert", None),
        P("section", None, "expert", None),
    )
    out_specs = (
        P("section", None, "expert", None),
        P("section", None, "expert", None),
        P("section", None, None),
        P("section", None, None),
        P("section", None, None, "tensor"),
        P("section", None, "tensor"),
        P("section", "tensor", None),
        P("section", None),
        P("section", "expert", None, "tensor"),
        P("section", "expert", "tensor"),
        P("section", "expert", "tensor", None),
        P("section", "expert", None),
    )
    return jax.shard_map(
        on_device, mesh=mesh, in_specs=in_specs, out_specs=out_specs, check_vma=False
    )
```

```python
import functools
import math
import types

import jax
import jax.numpy as jnp
from jax import lax
from jax.experimental import pallas as pl
from jax.experimental.pallas import tpu as pltpu
from jax.sharding import PartitionSpec as P

HEAD_DIM = 64
TOPK = 2

NORM_EPSILON = 1e-06
GELU_FACTOR = 0.7978845608028654
CUBIC_TERM = 0.044715

MESH = pl.DeviceIdType.MESH
ROW_TILE = 16
BF16 = jnp.bfloat16
F32 = jnp.float32

(
    RS_ATTN,
    AG_ATTN,
    DISPATCH,
    PARTS,
    RS_MOE,
    AG_MOE,
    CROSS,
    RESID,
    GRADS,
    GRAD_PARTS,
    RS_GRAD,
    AG_GRAD,
    RS_PROJ,
    AG_PROJ,
    ALL_NORMED,
    ALL_MIXED,
    ALL_HIDDEN,
    ALL_PROJ,
    SMALL_E,
    SMALL_T,
    PHASES,
) = range(21)


def nn(left, right):
    return jnp.dot(left, right, preferred_element_type=F32)


def nt(left, right):
    return lax.dot_general(left, right, (((1,), (1,)), ((), ())), preferred_element_type=F32)


def tn(left, right):
    return lax.dot_general(left, right, (((0,), (0,)), ((), ())), preferred_element_type=F32)


def standardize(values):
    average = jnp.mean(values, axis=-1, keepdims=True)
    centred = values - average
    variance = jnp.mean(centred * centred, axis=-1, keepdims=True)
    inv_std = lax.rsqrt(variance + NORM_EPSILON)
    return centred * inv_std, inv_std


def norm_back(grad_normed, normed, inv_std, scale_row):
    scaled = grad_normed * scale_row
    return (
        scaled
        - jnp.mean(scaled, axis=-1, keepdims=True)
        - normed * jnp.mean(scaled * normed, axis=-1, keepdims=True)
    ) * inv_std


def iota(shape, axis):
    return lax.broadcasted_iota(jnp.int32, shape, axis)


class Swap:
    def __init__(self, r, phase, axis, pieces, source, landing):
        self.r, self.phase, self.axis, self.pieces = r, phase, axis, pieces
        self.size = lax.axis_size(axis)
        self.me = lax.axis_index(axis)
        side = math.isqrt(self.size)
        self.q = side if axis == "expert" and side * side == self.size else 1
        self.source, self.landing = source, landing

    def walk(self, high, low):
        return lax.rem(high, self.size // self.q) * self.q + lax.rem(low, self.q)

    def ahead(self, k):
        q = self.q
        return self.walk(self.me // q + k // q, self.me % q + k % q)

    def behind(self, k):
        q = self.q
        return self.walk(self.me // q + self.size // q - k // q, self.me % q + q - k % q)

    def back(self, k):
        q = self.q
        return self.walk(self.size // q - k // q, q - k % q)

    def copy(self, k, h):
        there = self.ahead(k)
        return pltpu.make_async_remote_copy(
            src_ref=self.source(there, h),
            dst_ref=self.landing(k, h),
            send_sem=self.r.send_sem.at[self.phase, k, h],
            recv_sem=self.r.recv_sem.at[self.phase, k, h],
            device_id={self.axis: there},
            device_id_type=MESH,
        )

    def start(self, k, h=0):
        self.copy(k, h).start()

    def start_all(self, h=0):
        for k in range(1, self.size):
            self.start(k, h)

    def wait(self, k, h=0):
        self.copy(k, h).wait_recv()

    def wait_all(self):
        for h in range(self.pieces):
            for k in range(1, self.size):
                self.wait(k, h)

    def drain(self):
        for h in range(self.pieces):
            for k in range(1, self.size):
                self.copy(k, h).wait_send()


def relay_kernel(names, d, *refs):
    r = types.SimpleNamespace(**dict(zip(names, refs)))
    E, T, R, RG, RP, CH, H, EP = d.E, d.T, d.R, d.RG, d.RP, d.CH, d.H, d.EP
    HH = CH // H
    CAP, D, W, HW = d.CAP, d.D, d.W, d.HW
    heads = W // HEAD_DIM
    scale_factor = HEAD_DIM ** (-0.5)
    s, e, t = [lax.axis_index(name) for name in ("section", "expert", "tensor")]
    other = 1 - s
    at_first, at_second = s == 0, s == 1

    def piece(h):
        return pl.ds(h * HH, HH)

    def gather(phase, ref):
        return Swap(r, phase, "expert", 1, lambda there, h: ref.at[e], lambda k, h: ref.at[e])

    def gather_rows(phase, ref):
        return Swap(
            r, phase, "tensor", H,
            lambda there, h: ref.at[t, piece(h)],
            lambda k, h: ref.at[t, piece(h)],
        )

    def scatter_rows(phase, source, landing):
        return Swap(
            r, phase, "tensor", H,
            lambda there, h: source.at[there, piece(h)],
            lambda k, h: landing.at[k - 1, piece(h)],
        )

    rs_attn = scatter_rows(RS_ATTN, r.p1, r.l1)
    ag_attn = gather_rows(AG_ATTN, r.t1)
    rs_moe = scatter_rows(RS_MOE, r.p2, r.l2)
    ag_moe = gather_rows(AG_MOE, r.t2)
    rs_grad = scatter_rows(RS_GRAD, r.p3, r.l3)
    ag_grad = gather_rows(AG_GRAD, r.t3)
    rs_proj = scatter_rows(RS_PROJ, r.p4, r.l4)
    ag_proj = gather_rows(AG_PROJ, r.t4)

    def routed(phase, source, landing):
        return Swap(
            r, phase, "expert", 1, lambda there, h: source.at[there], lambda k, h: landing.at[e]
        )

    dispatch = routed(DISPATCH, r.o1, r.b1)
    parts = routed(PARTS, r.o2, r.b2)
    grads = routed(GRADS, r.o3, r.b3)
    grad_parts = routed(GRAD_PARTS, r.o4, r.b4)
    all_normed = gather(ALL_NORMED, r.na)
    all_mixed = gather(ALL_MIXED, r.am)
    all_hidden = gather(ALL_HIDDEN, r.gh_all)
    all_proj = gather(ALL_PROJ, r.gp)
    small_e = Swap(
        r, SMALL_E, "expert", 1, lambda there, h: r.small, lambda k, h: r.small_e.at[k - 1]
    )
    small_t = Swap(
        r, SMALL_T, "tensor", 1, lambda there, h: r.small2, lambda k, h: r.small_t.at[k - 1]
    )

    def cross_copy(source, k, h):
        return pltpu.make_async_remote_copy(
            src_ref=source.at[t, piece(h)],
            dst_ref=r.delta_in.at[t, piece(h)],
            send_sem=r.send_sem.at[CROSS, k, h],
            recv_sem=r.recv_sem.at[CROSS, k, h],
            device_id={"section": other, "tensor": lax.rem(t + k, T)},
            device_id_type=MESH,
        )

    def resid_copy(source):
        return pltpu.make_async_remote_copy(
            src_ref=source,
            dst_ref=r.resid_in,
            send_sem=r.send_sem.at[RESID, 0, 0],
            recv_sem=r.recv_sem.at[RESID, 0, 0],
            device_id={"section": other},
            device_id_type=MESH,
        )

    def load(k):
        source, target = (
            (r.expert_in, r.w_in), (r.expert_out, r.w_out),
            (r.inputs.at[:, 0, :], r.rows_in), (r.cotangent.at[:, 0, :], r.rows_in),
        )[k]
        return pltpu.make_async_copy(source, target, r.load_sem.at[k])

    def from_other_section():
        resid_copy(r.resid_in).wait_recv()
        for h in range(H):
            for k in range(T):
                cross_copy(r.delta_in, k, h).wait_recv()
        return r.resid_in[...] + r.delta_in[...].reshape(RP, D).astype(F32)

    r.x[...] = jnp.zeros((RP, D), F32)
    r.g[...] = jnp.zeros((RP, D), F32)

    @pl.when(at_first)
    def _():
        load(2).start()

    @pl.when(at_second)
    def _():
        load(3).start()

    load(1).start()
    load(0).start()

    barrier = pltpu.get_barrier_semaphore()
    friends = [{"tensor": lax.rem(t + k, T)} for k in range(1, T)]
    friends += [{"expert": lax.rem(e + k, E)} for k in range(1, E)]
    friends += [{"section": other, "tensor": lax.rem(t + k, T)} for k in range(T)]
    for device in friends:
        pl.semaphore_signal(barrier, inc=1, device_id=device, device_id_type=MESH)
    pl.semaphore_wait(barrier, len(friends))

    def rows_of(chunk, h):
        return pl.ds(pl.multiple_of(chunk * CH + h * HH, HH), HH)

    def gate_of(expert, rows=slice(None)):
        ids, gates = r.rt[rows, :], r.gt[rows, :]
        named = lax.convert_element_type(expert, F32)
        return jnp.sum(jnp.where(ids == named, gates, 0.0), axis=-1, keepdims=True)

    def routing():
        r.rt_t[...] = jnp.full((8, RP), -1.0, F32)
        r.gt_t[...] = jnp.zeros((8, RP), F32)
        r.rt_t[0:TOPK, 0:R] = r.routes[...].astype(F32)
        r.gt_t[0:TOPK, 0:R] = r.gate_weights[...]
        ids = r.rt_t[...]
        r.rt[...] = jnp.transpose(ids)
        r.gt[...] = jnp.transpose(r.gt_t[...])
        expert = iota((EP, RP), 0).astype(F32)
        named = jnp.where((ids[0:1] == expert) | (ids[1:2] == expert), 1.0, 0.0)
        later = jnp.where(iota((RP, RP), 0) < iota((RP, RP), 1), 1.0, 0.0)
        slot_t = jnp.where(named > 0.5, nn(named.astype(BF16), later.astype(BF16)), -1.0)
        slot = jnp.transpose(slot_t)
        wide = iota((RP, CAP), 1).astype(F32)
        tall = iota((CAP, RP), 0).astype(F32)
        for k in range(E):
            r.pick[k] = jnp.where(slot[:, k : k + 1] == wide, 1.0, 0.0).astype(BF16)
            r.place[k] = jnp.where(slot_t[k : k + 1, :] == tall, 1.0, 0.0).astype(BF16)

    def dispatch_grads():
        def outgoing(expert):
            weighted = (gate_of(expert) * r.g[...]).astype(BF16)
            return nn(r.place[expert], weighted).astype(BF16)

        def one(k, carry):
            there = grads.ahead(k)
            r.o3[there] = outgoing(there)
            grads.start(k)
            return carry

        lax.fori_loop(1, E, one, 0)
        r.b3[e] = outgoing(e)

    def each_block(swapped, body):
        body(e, 0)

        def one(k, carry):
            swapped.wait(k)
            body(swapped.behind(k), k)
            return carry

        lax.fori_loop(1, E, one, 0)

    def send_part(swapped, outgoing, landing, image, k, value):
        if isinstance(k, int):
            landing[image] = value
        else:
            outgoing[image] = value
            swapped.start(swapped.back(k))

    def raw_block(image):
        r.raw[image] = nt(r.b3[image], r.w_out[...])

    def backward_part(image, k):
        grad_pre = r.raw[image] * r.slope[image]
        r.in_bias[...] = r.in_bias[...] + jnp.sum(grad_pre, axis=0, keepdims=True)
        grad_pre_b = grad_pre.astype(BF16)
        r.gpb[image] = grad_pre_b
        value = nt(grad_pre_b, r.w_in[...]).astype(BF16)
        send_part(grad_parts, r.o4, r.b4, image, k, value)

    def forward_part(image, k):
        bias = jnp.where(t == 0, r.expert_out_bias[...], 0.0)
        value = (nn(r.act[image], r.w_out[...]) + bias).astype(BF16)
        send_part(parts, r.o2, r.b2, image, k, value)

    def expert_block(image):
        pre = nn(r.b1[image], r.w_in[...]) + r.expert_in_bias[...]
        square = pre * pre
        tangent = jnp.tanh(GELU_FACTOR * (pre + CUBIC_TERM * square * pre))
        half = 0.5 * (1.0 + tangent)
        r.act[image] = (pre * half).astype(BF16)
        r.slope[image] = half + 0.5 * pre * (1.0 - tangent * tangent) * GELU_FACTOR * (
            1.0 + 3.0 * CUBIC_TERM * square
        )

    def scatter_chunks(swapped, part, chunk_of):
        for h in range(H):
            for k in range(1, T):
                there = swapped.ahead(k)
                part[there, piece(h)] = chunk_of(rows_of(there, h)).astype(BF16)
                swapped.start(k, h)
        return [chunk_of(rows_of(t, h)) for h in range(H)]

    def collect(swapped, landing, own, h):
        total = own[h]
        for k in range(1, T):
            swapped.wait(k, h)
            total = total + landing[k - 1, piece(h)].astype(F32)
        return total

    def hand_on(ref, gathered, crossing, h):
        if crossing is not None:

            @pl.when(crossing)
            def _():
                for k in range(T):
                    cross_copy(ref, k, h).start()

        gathered.start_all(h)

    def combined(landed, gated, rows):
        total = None
        for k in range(E):
            term = nn(r.pick[k, rows, :], landed[k])
            if gated:
                term = gate_of(k, rows) * term
            total = term if total is None else total + term
        return total

    def finish_forward(crossing):
        parts.wait_all()
        own = scatter_chunks(rs_moe, r.p2, lambda rows: combined(r.b2, True, rows))
        for h in range(H):
            r.t2[t, piece(h)] = collect(rs_moe, r.l2, own, h).astype(BF16)
            hand_on(r.t2, ag_moe, crossing, h)
        ag_moe.wait_all()
        out = r.hidden[...] + r.t2[...].reshape(RP, D).astype(F32)
        r.section_out[...] = out[0:R]

    r.in_bias[...] = jnp.zeros((1, HW), F32)
    r.small[...] = jnp.zeros((8, D), F32)

    @pl.when(at_first)
    def _():
        load(2).wait()
        r.x[0:R, :] = r.rows_in[...]

    @pl.when(at_second)
    def _():
        routing()
        load(3).wait()
        r.g[0:R, :] = r.rows_in[...]
        dispatch_grads()
        load(1).wait()
        each_block(grads, lambda image, k: raw_block(image))
        r.x[...] = from_other_section()

    inside = iota((RP, 1), 0) < R
    scale0, scale1 = r.norm_scale[0:1, :], r.norm_scale[1:2, :]
    shift0, shift1 = r.norm_shift[0:1, :], r.norm_shift[1:2, :]
    normed_first, _ = standardize(r.x[...])
    normed_a = jnp.where(inside, normed_first * scale0 + shift0, 0.0).astype(BF16)
    r.na[e] = normed_a[0:RG]
    query = nt(normed_a, r.proj_weight[0]) + r.proj_bias[0:1, :]
    r.qkv[0] = jnp.where(inside, query, 0.0).astype(BF16)
    r.qkv[1] = nt(normed_a, r.proj_weight[1]).astype(BF16)
    value = nt(normed_a, r.proj_weight[2]) + r.proj_bias[1:2, :]
    r.qkv[2] = jnp.where(inside, value, 0.0).astype(BF16)
    real_key = iota((RP, RP), 1) < R
    mixed = []
    for h in range(heads):
        cols = slice(h * HEAD_DIM, (h + 1) * HEAD_DIM)
        scores = nt(r.qkv[0][:, cols], r.qkv[1][:, cols]) * scale_factor
        powers = jnp.where(real_key, jnp.exp(scores), 0.0)
        probs = powers / jnp.sum(powers, axis=-1, keepdims=True)
        r.probs[h] = probs
        mixed.append(nn(probs.astype(BF16), r.qkv[2][:, cols]))
    r.mixed[...] = jnp.concatenate(mixed, axis=1).astype(BF16)
    r.am[e] = r.mixed[0:RG, :]
    own = scatter_chunks(
        rs_attn, r.p1, lambda rows: nn(r.mixed[rows, :], r.attn_weight[...])
    )
    all_normed.start_all()
    all_mixed.start_all()

    @pl.when(at_first)
    def _():
        routing()

    for h in range(H):
        r.t1[t, piece(h)] = collect(rs_attn, r.l1, own, h).astype(BF16)
        hand_on(r.t1, ag_attn, None, h)
    ag_attn.wait_all()
    hidden = r.x[...] + (r.t1[...].reshape(RP, D).astype(F32) + r.attn_bias[...])
    r.hidden[...] = hidden

    @pl.when(at_first)
    def _():
        resid_copy(r.hidden).start()

    normed_second, inv_second = standardize(hidden)
    r.h2[...] = normed_second
    r.r2[...] = inv_second
    r.nb[...] = (normed_second * scale1 + shift1).astype(BF16)

    def dispatch_one(k, carry):
        there = dispatch.ahead(k)
        r.o1[there] = nn(r.place[there], r.nb[...]).astype(BF16)
        dispatch.start(k)
        return carry

    lax.fori_loop(1, E, dispatch_one, 0)
    r.b1[e] = nn(r.place[e], r.nb[...]).astype(BF16)

    @pl.when(at_first)
    def _():
        load(0).wait()
        load(1).wait()

        def both(image, k):
            expert_block(image)
            forward_part(image, k)

        each_block(dispatch, both)
        finish_forward(True)
        r.g[...] = from_other_section()
        dispatch_grads()

        def back(image, k):
            raw_block(image)
            backward_part(image, k)

        each_block(grads, back)

    @pl.when(at_second)
    def _():
        load(0).wait()

        def both(image, k):
            expert_block(image)
            backward_part(image, k)

        each_block(dispatch, both)

    slots = E * CAP
    r.grad_expert_out[...] = tn(
        r.act[...].reshape(slots, HW), r.b3[...].reshape(slots, D)
    )
    r.grad_expert_out_bias[...] = jnp.sum(
        r.b3[...].reshape(slots, D).astype(F32), axis=0, keepdims=True
    )
    grad_parts.wait_all()
    own = scatter_chunks(rs_grad, r.p3, lambda rows: combined(r.b4, False, rows))
    r.grad_expert_in[...] = tn(
        r.b1[...].reshape(slots, D), r.gpb[...].reshape(slots, HW)
    )
    r.grad_expert_in_bias[...] = r.in_bias[...]
    for h in range(H):
        rows = rows_of(t, h)
        own[h] = collect(rs_grad, r.l3, own, h)
        delta = norm_back(own[h], r.h2[rows, :], r.r2[rows, :], scale1)
        r.t3[t, piece(h)] = delta.astype(BF16)
        hand_on(r.t3, ag_grad, None, h)

    def add_small(row, value):
        r.small[row : row + 1, :] = r.small[row : row + 1, :] + jnp.sum(value, axis=0, keepdims=True)

    for h in range(H):
        add_small(1, own[h] * r.h2[rows_of(t, h), :])
        add_small(3, own[h])
    ag_grad.wait_all()
    grad_hidden = r.g[...] + r.t3[...].reshape(RP, D).astype(F32)
    r.g[...] = grad_hidden

    @pl.when(at_second)
    def _():
        resid_copy(r.g).start()

    for h in range(H):
        add_small(4, r.g[rows_of(t, h), :])
    grad_hidden_b = grad_hidden.astype(BF16)
    r.gh_all[e] = grad_hidden_b[0:RG]
    all_hidden.start_all()
    grad_mixed = nt(grad_hidden_b, r.attn_weight[...]).astype(BF16)
    found = [[], [], []]
    for h in range(heads):
        cols = slice(h * HEAD_DIM, (h + 1) * HEAD_DIM)
        query, key, value = r.qkv[0][:, cols], r.qkv[1][:, cols], r.qkv[2][:, cols]
        grad_mixed_h = grad_mixed[:, cols]
        probs = r.probs[h]
        grad_values = tn(probs.astype(BF16), grad_mixed_h)
        grad_probs = nt(grad_mixed_h, value)
        row_delta = jnp.sum(
            grad_mixed_h.astype(F32) * r.mixed[...][:, cols].astype(F32), axis=-1, keepdims=True
        )
        grad_scores = (probs * (grad_probs - row_delta) * scale_factor).astype(BF16)
        found[0].append(nn(grad_scores, key))
        found[1].append(tn(grad_scores, query))
        found[2].append(grad_values)
    for j in range(3):
        flat = jnp.concatenate(found[j], axis=1)
        if j != 1:
            row = 5 + j // 2
            r.small[row : row + 1, 0:W] = jnp.sum(flat, axis=0, keepdims=True)
        r.grad_flat[j] = flat.astype(BF16)
        r.gp[e, j] = r.grad_flat[j, 0:RG, :]

    def proj_chunk(rows):
        total = nn(r.grad_flat[0, rows, :], r.proj_weight[0])
        for j in (1, 2):
            total = total + nn(r.grad_flat[j, rows, :], r.proj_weight[j])
        return total

    own = scatter_chunks(rs_proj, r.p4, proj_chunk)
    all_proj.start_all()
    normed_mine = [standardize(r.x[rows_of(t, h), :]) for h in range(H)]
    for h in range(H):
        own[h] = collect(rs_proj, r.l4, own, h)
        r.t4[t, piece(h)] = norm_back(own[h], *normed_mine[h], scale0).astype(BF16)
        hand_on(r.t4, ag_proj, at_second, h)
    for h in range(H):
        add_small(0, own[h] * normed_mine[h][0])
        add_small(2, own[h])
    small_e.start_all()

    @pl.when(at_second)
    def _():
        forward_part(e, 0)

        def one(k, carry):
            forward_part(parts.behind(k), k)
            return carry

        lax.fori_loop(1, E, one, 0)
        finish_forward(None)

    all_mixed.wait_all()
    all_hidden.wait_all()
    all_normed.wait_all()
    tokens = E * RG
    r.grad_attn_weight[...] = tn(
        r.am[...].reshape(tokens, W), r.gh_all[...].reshape(tokens, D)
    )
    small_e.wait_all()
    total = r.small[...]
    for k in range(1, E):
        total = total + r.small_e[k - 1]
    r.small2[...] = total
    small_t.start_all()
    all_proj.wait_all()
    for j in range(3):
        r.grad_proj[j] = tn(
            r.gp[:, j].reshape(tokens, W), r.na[...].reshape(tokens, D)
        )
    small_t.wait_all()
    r.grad_proj_bias[...] = r.small2[5:7, 0:W]
    total = r.small2[...]
    for k in range(1, T):
        total = total + r.small_t[k - 1]
    r.grad_norm_scale[...] = total[0:2]
    r.grad_norm_shift[...] = total[2:4]
    r.grad_attn_bias[...] = total[4:5]
    ag_proj.wait_all()
    grad_in = r.g[...] + r.t4[...].reshape(RP, D).astype(F32)
    r.section_in_grad[...] = grad_in[0:R]

    for swapped in (
        rs_attn, ag_attn, rs_moe, ag_moe, rs_grad, ag_grad, rs_proj, ag_proj,
        dispatch, parts, grads, grad_parts,
        all_normed, all_mixed, all_hidden, all_proj, small_e, small_t,
    ):
        swapped.drain()
    resid_copy(r.resid_in).wait_send()
    for h in range(H):
        for k in range(T):
            cross_copy(r.t4, k, h).wait_send()


def write_kernel(count, *refs):
    sems = refs[-1]
    copies = []
    for k in range(count):
        source, target = refs[k], refs[count + k]
        if len(target.shape) > len(source.shape):
            target = target.at[:, 0, :]
        copies.append(pltpu.make_async_copy(source, target, sems.at[k]))
    for copy in copies:
        copy.start()
    for copy in copies:
        copy.wait()


def slot_count(row_count, experts):
    return max(2, (3 * TOPK * row_count + 2 * experts - 1) // (2 * experts))


def round_up(value, unit):
    return -(-value // unit) * unit


def on_device(
    inputs,
    cotangent,
    norm_scale,
    norm_shift,
    proj_weight,
    proj_bias,
    attn_weight,
    attn_bias,
    expert_in,
    expert_in_bias,
    expert_out,
    expert_out_bias,
    routes,
    gate_weights,
):
    E, T = lax.axis_size("expert"), lax.axis_size("tensor")
    R, D = inputs.shape[1:]
    W, HW = proj_weight.shape[3], expert_in.shape[3]
    CH = round_up(-(-R // T), ROW_TILE)
    RP = T * CH
    CAP = round_up(slot_count(R, E), ROW_TILE)
    RG = round_up(R, ROW_TILE)
    H = 2 if CH % (2 * ROW_TILE) == 0 else 1
    EP = round_up(E, ROW_TILE)
    d = types.SimpleNamespace(
        E=E, T=T, R=R, RG=RG, RP=RP, CH=CH, CAP=CAP, D=D, W=W, HW=HW, H=H, EP=EP
    )
    heads = W // HEAD_DIM

    operands = dict(
        inputs=jnp.transpose(inputs, (1, 0, 2)),
        cotangent=jnp.transpose(cotangent, (1, 0, 2)),
        norm_scale=norm_scale[0],
        norm_shift=norm_shift[0],
        proj_weight=jnp.transpose(proj_weight[0], (1, 2, 0)),
        proj_bias=proj_bias[0],
        attn_weight=attn_weight[0],
        attn_bias=attn_bias,
        expert_in=expert_in[0, 0],
        expert_in_bias=expert_in_bias[0],
        expert_out=expert_out[0, 0],
        expert_out_bias=expert_out_bias[0],
        routes=routes[0, 0].T,
        gate_weights=gate_weights[0, 0].T,
    )
    results = dict(
        section_out=(R, D),
        section_in_grad=(R, D),
        grad_norm_scale=(2, D),
        grad_norm_shift=(2, D),
        grad_proj_bias=(2, W),
        grad_attn_bias=(1, D),
        grad_proj=(3, W, D),
        grad_attn_weight=(W, D),
        grad_expert_in=(D, HW),
        grad_expert_in_bias=(1, HW),
        grad_expert_out=(HW, D),
        grad_expert_out_bias=(1, D),
    )
    scratch = dict(
        x=((RP, D), F32),
        rows_in=((R, D), F32),
        g=((RP, D), F32),
        hidden=((RP, D), F32),
        h2=((RP, D), F32),
        r2=((RP, 1), F32),
        nb=((RP, D), BF16),
        resid_in=((RP, D), F32),
        delta_in=((T, CH, D), BF16),
        qkv=((3, RP, W), BF16),
        probs=((heads, RP, RP), F32),
        na=((E, RG, D), BF16),
        am=((E, RG, W), BF16),
        mixed=((RP, W), BF16),
        gh_all=((E, RG, D), BF16),
        gp=((E, 3, RG, W), BF16),
        grad_flat=((3, RP, W), BF16),
        rt=((RP, 8), F32),
        gt=((RP, 8), F32),
        rt_t=((8, RP), F32),
        gt_t=((8, RP), F32),
        w_in=((D, HW), BF16),
        w_out=((HW, D), BF16),
        pick=((E, RP, CAP), BF16),
        place=((E, CAP, RP), BF16),
        act=((E, CAP, HW), BF16),
        gpb=((E, CAP, HW), BF16),
        slope=((E, CAP, HW), F32),
        raw=((E, CAP, HW), F32),
        in_bias=((1, HW), F32),
        small=((8, D), F32),
        small2=((8, D), F32),
        small_e=((E - 1, 8, D), F32),
        small_t=((T - 1, 8, D), F32),
    )
    for k in range(1, 5):
        scratch[f"p{k}"] = ((T, CH, D), BF16)
        scratch[f"l{k}"] = ((T - 1, CH, D), BF16)
        scratch[f"t{k}"] = ((T, CH, D), BF16)
        scratch[f"o{k}"] = ((E, CAP, D), BF16)
        scratch[f"b{k}"] = ((E, CAP, D), BF16)
    sems = pltpu.SemaphoreType.DMA((PHASES, max(E, T), H))
    names = list(operands) + list(results) + list(scratch) + ["load_sem", "send_sem", "recv_sem"]
    in_vmem, in_place = pl.BlockSpec(memory_space=pltpu.VMEM), pl.BlockSpec(memory_space=pl.ANY)
    loaded = ("inputs", "cotangent", "expert_in", "expert_out")
    found = pl.pallas_call(
        functools.partial(relay_kernel, names, d),
        out_shape=[pltpu.VMEM(shape, F32) for shape in results.values()],
        in_specs=[in_place if name in loaded else in_vmem for name in operands],
        out_specs=[in_vmem] * len(results),
        scratch_shapes=[pltpu.VMEM(shape, dtype) for shape, dtype in scratch.values()]
        + [pltpu.SemaphoreType.DMA((len(loaded),)), sems, sems],
        compiler_params=pltpu.CompilerParams(
            collective_id=0, has_side_effects=True, vmem_limit_bytes=52 * 2**20
        ),
        name="relay",
    )(*operands.values())
    shapes = [
        (R, 1, D) if name.startswith("section") else shape for name, shape in results.items()
    ]
    written = pl.pallas_call(
        functools.partial(write_kernel, len(results)),
        out_shape=[jax.ShapeDtypeStruct(shape, F32) for shape in shapes],
        in_specs=[in_vmem] * len(results),
        out_specs=[in_place] * len(results),
        scratch_shapes=[pltpu.SemaphoreType.DMA((len(results),))],
        compiler_params=pltpu.CompilerParams(vmem_limit_bytes=2**20),
        name="write",
    )(*[pltpu.with_memory_space_constraint(array, pltpu.VMEM) for array in found])
    found = types.SimpleNamespace(**dict(zip(results, written)))
    return (
        jnp.transpose(found.section_out, (1, 0, 2))[None],
        jnp.transpose(found.section_in_grad, (1, 0, 2))[None],
        found.grad_norm_scale[None],
        found.grad_norm_shift[None],
        jnp.transpose(found.grad_proj, (2, 0, 1))[None],
        found.grad_proj_bias[None],
        found.grad_attn_weight[None],
        found.grad_attn_bias,
        found.grad_expert_in[None, None],
        found.grad_expert_in_bias[None],
        found.grad_expert_out[None, None],
        found.grad_expert_out_bias[None],
    )


def solution(mesh):
    in_specs = (
        P(None, "expert", None),
        P(None, "expert", None),
        P("section", None, None),
        P("section", None, None),
        P("section", None, None, "tensor"),
        P("section", None, "tensor"),
        P("section", "tensor", None),
        P("section", None),
        P("section", "expert", None, "tensor"),
        P("section", "expert", "tensor"),
        P("section", "expert", "tensor", None),
        P("section", "expert", None),
        P("section", None, "expert", None),
        P("section", None, "expert", None),
    )
    out_specs = (
        P("section", None, "expert", None),
        P("section", None, "expert", None),
        P("section", None, None),
        P("section", None, None),
        P("section", None, None, "tensor"),
        P("section", None, "tensor"),
        P("section", "tensor", None),
        P("section", None),
        P("section", "expert", None, "tensor"),
        P("section", "expert", "tensor"),
        P("section", "expert", "tensor", None),
        P("section", "expert", None),
    )
    return jax.shard_map(
        on_device, mesh=mesh, in_specs=in_specs, out_specs=out_specs, check_vma=False
    )
```

```python
import functools
import math
import types

import jax
import jax.numpy as jnp
from jax import lax
from jax.experimental import pallas as pl
from jax.experimental.pallas import tpu as pltpu
from jax.sharding import PartitionSpec as P

HEAD_DIM = 64
TOPK = 2

NORM_EPSILON = 1e-06
GELU_FACTOR = 0.7978845608028654
CUBIC_TERM = 0.044715

MESH = pl.DeviceIdType.MESH
ROW_TILE = 16
BF16 = jnp.bfloat16
F32 = jnp.float32

(
    RS_ATTN,
    AG_ATTN,
    DISPATCH,
    PARTS,
    RS_MOE,
    AG_MOE,
    CROSS,
    RESID,
    GRADS,
    GRAD_PARTS,
    RS_GRAD,
    AG_GRAD,
    RS_PROJ,
    AG_PROJ,
    ALL_NORMED,
    RS_WEIGHT,
    AG_WEIGHT,
    ALL_PROJ,
    SMALL_E,
    SMALL_T,
    PHASES,
) = range(21)


def nn(left, right):
    return jnp.dot(left, right, preferred_element_type=F32)


def nt(left, right):
    return lax.dot_general(left, right, (((1,), (1,)), ((), ())), preferred_element_type=F32)


def tn(left, right):
    return lax.dot_general(left, right, (((0,), (0,)), ((), ())), preferred_element_type=F32)


def standardize(values):
    average = jnp.mean(values, axis=-1, keepdims=True)
    centred = values - average
    variance = jnp.mean(centred * centred, axis=-1, keepdims=True)
    inv_std = lax.rsqrt(variance + NORM_EPSILON)
    return centred * inv_std, inv_std


def norm_back(grad_normed, normed, inv_std, scale_row):
    scaled = grad_normed * scale_row
    return (
        scaled
        - jnp.mean(scaled, axis=-1, keepdims=True)
        - normed * jnp.mean(scaled * normed, axis=-1, keepdims=True)
    ) * inv_std


def iota(shape, axis):
    return lax.broadcasted_iota(jnp.int32, shape, axis)


class Swap:
    def __init__(self, r, phase, axis, pieces, source, landing):
        self.r, self.phase, self.axis, self.pieces = r, phase, axis, pieces
        self.size = lax.axis_size(axis)
        self.me = lax.axis_index(axis)
        side = math.isqrt(self.size)
        self.q = side if axis == "expert" and side * side == self.size else 1
        self.source, self.landing = source, landing

    def walk(self, high, low):
        return lax.rem(high, self.size // self.q) * self.q + lax.rem(low, self.q)

    def ahead(self, k):
        q = self.q
        return self.walk(self.me // q + k // q, self.me % q + k % q)

    def behind(self, k):
        q = self.q
        return self.walk(self.me // q + self.size // q - k // q, self.me % q + q - k % q)

    def back(self, k):
        q = self.q
        return self.walk(self.size // q - k // q, q - k % q)

    def copy(self, k, h):
        there = self.ahead(k)
        return pltpu.make_async_remote_copy(
            src_ref=self.source(there, h),
            dst_ref=self.landing(k, h),
            send_sem=self.r.send_sem.at[self.phase, k, h],
            recv_sem=self.r.recv_sem.at[self.phase, k, h],
            device_id={self.axis: there},
            device_id_type=MESH,
        )

    def start(self, k, h=0):
        self.copy(k, h).start()

    def start_all(self, h=0):
        for k in range(1, self.size):
            self.start(k, h)

    def wait(self, k, h=0):
        self.copy(k, h).wait_recv()

    def wait_all(self):
        for h in range(self.pieces):
            for k in range(1, self.size):
                self.wait(k, h)

    def drain(self):
        for h in range(self.pieces):
            for k in range(1, self.size):
                self.copy(k, h).wait_send()


def relay_kernel(names, d, *refs):
    r = types.SimpleNamespace(**dict(zip(names, refs)))
    E, T, R, RG, RP, CH, H, EP = d.E, d.T, d.R, d.RG, d.RP, d.CH, d.H, d.EP
    HH, WC = CH // H, d.WC
    CAP, D, W, HW = d.CAP, d.D, d.W, d.HW
    heads = W // HEAD_DIM
    scale_factor = HEAD_DIM ** (-0.5)
    s, e, t = [lax.axis_index(name) for name in ("section", "expert", "tensor")]
    other = 1 - s
    at_first, at_second = s == 0, s == 1

    def piece(h):
        return pl.ds(h * HH, HH)

    def gather(phase, ref):
        return Swap(r, phase, "expert", 1, lambda there, h: ref.at[e], lambda k, h: ref.at[e])

    def gather_rows(phase, ref):
        return Swap(
            r, phase, "tensor", H,
            lambda there, h: ref.at[t, piece(h)],
            lambda k, h: ref.at[t, piece(h)],
        )

    def scatter_rows(phase, source, landing):
        return Swap(
            r, phase, "tensor", H,
            lambda there, h: source.at[there, piece(h)],
            lambda k, h: landing.at[k - 1, piece(h)],
        )

    rs_attn = scatter_rows(RS_ATTN, r.p1, r.l1)
    ag_attn = gather_rows(AG_ATTN, r.t1)
    rs_moe = scatter_rows(RS_MOE, r.p2, r.l2)
    ag_moe = gather_rows(AG_MOE, r.t2)
    rs_grad = scatter_rows(RS_GRAD, r.p3, r.l3)
    ag_grad = gather_rows(AG_GRAD, r.t3)
    rs_proj = scatter_rows(RS_PROJ, r.p4, r.l4)
    ag_proj = gather_rows(AG_PROJ, r.t4)

    def routed(phase, source, landing):
        return Swap(
            r, phase, "expert", 1, lambda there, h: source.at[there], lambda k, h: landing.at[e]
        )

    dispatch = routed(DISPATCH, r.o1, r.b1)
    parts = routed(PARTS, r.o2, r.b2)
    grads = routed(GRADS, r.o3, r.b3)
    grad_parts = routed(GRAD_PARTS, r.o4, r.b4)
    all_normed = gather(ALL_NORMED, r.na)

    def weight_rows(owner):
        return pl.ds(pl.multiple_of(owner * WC, WC), WC)

    rs_weight = Swap(
        r, RS_WEIGHT, "expert", 1,
        lambda there, h: r.w_part.at[weight_rows(there)],
        lambda k, h: r.w_land.at[k - 1],
    )
    ag_weight = Swap(
        r, AG_WEIGHT, "expert", 1,
        lambda there, h: r.w_sum.at[weight_rows(e)],
        lambda k, h: r.w_sum.at[weight_rows(e)],
    )
    all_proj = gather(ALL_PROJ, r.gp)
    small_e = Swap(
        r, SMALL_E, "expert", 1, lambda there, h: r.small2, lambda k, h: r.small_e.at[k - 1]
    )
    small_t = Swap(
        r, SMALL_T, "tensor", 1, lambda there, h: r.small, lambda k, h: r.small_t.at[k - 1]
    )

    def cross_copy(source, k, h):
        return pltpu.make_async_remote_copy(
            src_ref=source.at[t, piece(h)],
            dst_ref=r.delta_in.at[t, piece(h)],
            send_sem=r.send_sem.at[CROSS, k, h],
            recv_sem=r.recv_sem.at[CROSS, k, h],
            device_id={"section": other, "tensor": lax.rem(t + k, T)},
            device_id_type=MESH,
        )

    def resid_copy(source):
        return pltpu.make_async_remote_copy(
            src_ref=source,
            dst_ref=r.resid_in,
            send_sem=r.send_sem.at[RESID, 0, 0],
            recv_sem=r.recv_sem.at[RESID, 0, 0],
            device_id={"section": other},
            device_id_type=MESH,
        )

    def load(k):
        source, target = (
            (r.expert_in, r.w_in), (r.expert_out, r.w_out),
            (r.inputs.at[:, 0, :], r.rows_in), (r.cotangent.at[:, 0, :], r.rows_in),
        )[k]
        return pltpu.make_async_copy(source, target, r.load_sem.at[k])

    def from_other_section():
        resid_copy(r.resid_in).wait_recv()
        for h in range(H):
            for k in range(T):
                cross_copy(r.delta_in, k, h).wait_recv()
        return r.resid_in[...] + r.delta_in[...].reshape(RP, D).astype(F32)

    r.x[...] = jnp.zeros((RP, D), F32)
    r.g[...] = jnp.zeros((RP, D), F32)

    @pl.when(at_first)
    def _():
        load(2).start()

    @pl.when(at_second)
    def _():
        load(3).start()

    load(1).start()
    load(0).start()

    barrier = pltpu.get_barrier_semaphore()
    friends = [{"tensor": lax.rem(t + k, T)} for k in range(1, T)]
    friends += [{"expert": lax.rem(e + k, E)} for k in range(1, E)]
    friends += [{"section": other, "tensor": lax.rem(t + k, T)} for k in range(T)]
    for device in friends:
        pl.semaphore_signal(barrier, inc=1, device_id=device, device_id_type=MESH)
    pl.semaphore_wait(barrier, len(friends))

    def rows_of(chunk, h):
        return pl.ds(pl.multiple_of(chunk * CH + h * HH, HH), HH)

    def gate_of(expert, rows=slice(None)):
        ids, gates = r.rt[rows, :], r.gt[rows, :]
        named = lax.convert_element_type(expert, F32)
        return jnp.sum(jnp.where(ids == named, gates, 0.0), axis=-1, keepdims=True)

    def routing():
        r.rt_t[...] = jnp.full((8, RP), -1.0, F32)
        r.gt_t[...] = jnp.zeros((8, RP), F32)
        r.rt_t[0:TOPK, 0:R] = r.routes[...].astype(F32)
        r.gt_t[0:TOPK, 0:R] = r.gate_weights[...]
        ids = r.rt_t[...]
        r.rt[...] = jnp.transpose(ids)
        r.gt[...] = jnp.transpose(r.gt_t[...])
        expert = iota((EP, RP), 0).astype(F32)
        named = jnp.where((ids[0:1] == expert) | (ids[1:2] == expert), 1.0, 0.0)
        later = jnp.where(iota((RP, RP), 0) < iota((RP, RP), 1), 1.0, 0.0)
        slot_t = jnp.where(named > 0.5, nn(named.astype(BF16), later.astype(BF16)), -1.0)
        slot = jnp.transpose(slot_t)
        wide = iota((RP, CAP), 1).astype(F32)
        tall = iota((CAP, RP), 0).astype(F32)
        for k in range(E):
            r.pick[k] = jnp.where(slot[:, k : k + 1] == wide, 1.0, 0.0).astype(BF16)
            r.place[k] = jnp.where(slot_t[k : k + 1, :] == tall, 1.0, 0.0).astype(BF16)

    def dispatch_grads():
        def outgoing(expert):
            weighted = (gate_of(expert) * r.g[...]).astype(BF16)
            return nn(r.place[expert], weighted).astype(BF16)

        def one(k, carry):
            there = grads.ahead(k)
            r.o3[there] = outgoing(there)
            grads.start(k)
            return carry

        lax.fori_loop(1, E, one, 0)
        r.b3[e] = outgoing(e)

    def each_block(swapped, body):
        body(e, 0)

        def one(k, carry):
            swapped.wait(k)
            body(swapped.behind(k), k)
            return carry

        lax.fori_loop(1, E, one, 0)

    def send_part(swapped, outgoing, landing, image, k, value):
        if isinstance(k, int):
            landing[image] = value
        else:
            outgoing[image] = value
            swapped.start(swapped.back(k))

    def raw_block(image):
        r.raw[image] = nt(r.b3[image], r.w_out[...])

    def backward_part(image, k):
        grad_pre = r.raw[image] * r.slope[image]
        r.in_bias[...] = r.in_bias[...] + jnp.sum(grad_pre, axis=0, keepdims=True)
        grad_pre_b = grad_pre.astype(BF16)
        r.gpb[image] = grad_pre_b
        value = nt(grad_pre_b, r.w_in[...]).astype(BF16)
        send_part(grad_parts, r.o4, r.b4, image, k, value)

    def forward_part(image, k):
        bias = jnp.where(t == 0, r.expert_out_bias[...], 0.0)
        value = (nn(r.act[image], r.w_out[...]) + bias).astype(BF16)
        send_part(parts, r.o2, r.b2, image, k, value)

    def expert_block(image):
        pre = nn(r.b1[image], r.w_in[...]) + r.expert_in_bias[...]
        square = pre * pre
        tangent = jnp.tanh(GELU_FACTOR * (pre + CUBIC_TERM * square * pre))
        half = 0.5 * (1.0 + tangent)
        r.act[image] = (pre * half).astype(BF16)
        r.slope[image] = half + 0.5 * pre * (1.0 - tangent * tangent) * GELU_FACTOR * (
            1.0 + 3.0 * CUBIC_TERM * square
        )

    def scatter_chunks(swapped, part, chunk_of):
        for h in range(H):
            for k in range(1, T):
                there = swapped.ahead(k)
                part[there, piece(h)] = chunk_of(rows_of(there, h)).astype(BF16)
                swapped.start(k, h)
        return [chunk_of(rows_of(t, h)) for h in range(H)]

    def collect(swapped, landing, own, h):
        total = own[h]
        for k in range(1, T):
            swapped.wait(k, h)
            total = total + landing[k - 1, piece(h)].astype(F32)
        return total

    def hand_on(ref, gathered, crossing, h):
        if crossing is not None:

            @pl.when(crossing)
            def _():
                for k in range(T):
                    cross_copy(ref, k, h).start()

        gathered.start_all(h)

    def combined(landed, gated, rows):
        total = None
        for k in range(E):
            term = nn(r.pick[k, rows, :], landed[k])
            if gated:
                term = gate_of(k, rows) * term
            total = term if total is None else total + term
        return total

    def finish_forward(crossing):
        parts.wait_all()
        own = scatter_chunks(rs_moe, r.p2, lambda rows: combined(r.b2, True, rows))
        for h in range(H):
            r.t2[t, piece(h)] = collect(rs_moe, r.l2, own, h).astype(BF16)
            hand_on(r.t2, ag_moe, crossing, h)
        ag_moe.wait_all()
        out = r.hidden[...] + r.t2[...].reshape(RP, D).astype(F32)
        r.section_out[...] = out[0:R]

    r.in_bias[...] = jnp.zeros((1, HW), F32)
    r.small[...] = jnp.zeros((8, D), F32)

    @pl.when(at_first)
    def _():
        load(2).wait()
        r.x[0:R, :] = r.rows_in[...]

    @pl.when(at_second)
    def _():
        routing()
        load(3).wait()
        r.g[0:R, :] = r.rows_in[...]
        dispatch_grads()
        load(1).wait()
        each_block(grads, lambda image, k: raw_block(image))
        r.x[...] = from_other_section()

    inside = iota((RP, 1), 0) < R
    scale0, scale1 = r.norm_scale[0:1, :], r.norm_scale[1:2, :]
    shift0, shift1 = r.norm_shift[0:1, :], r.norm_shift[1:2, :]
    normed_first, _ = standardize(r.x[...])
    normed_a = jnp.where(inside, normed_first * scale0 + shift0, 0.0).astype(BF16)
    r.na[e] = normed_a[0:RG]
    query = nt(normed_a, r.proj_weight[0]) + r.proj_bias[0:1, :]
    r.qkv[0] = jnp.where(inside, query, 0.0).astype(BF16)
    r.qkv[1] = nt(normed_a, r.proj_weight[1]).astype(BF16)
    value = nt(normed_a, r.proj_weight[2]) + r.proj_bias[1:2, :]
    r.qkv[2] = jnp.where(inside, value, 0.0).astype(BF16)
    real_key = iota((RP, RP), 1) < R
    mixed = []
    for h in range(heads):
        cols = slice(h * HEAD_DIM, (h + 1) * HEAD_DIM)
        scores = nt(r.qkv[0][:, cols], r.qkv[1][:, cols]) * scale_factor
        powers = jnp.where(real_key, jnp.exp(scores), 0.0)
        probs = powers / jnp.sum(powers, axis=-1, keepdims=True)
        r.probs[h] = probs
        mixed.append(nn(probs.astype(BF16), r.qkv[2][:, cols]))
    r.mixed[...] = jnp.concatenate(mixed, axis=1).astype(BF16)
    own = scatter_chunks(
        rs_attn, r.p1, lambda rows: nn(r.mixed[rows, :], r.attn_weight[...])
    )
    all_normed.start_all()

    @pl.when(at_first)
    def _():
        routing()

    for h in range(H):
        r.t1[t, piece(h)] = collect(rs_attn, r.l1, own, h).astype(BF16)
        hand_on(r.t1, ag_attn, None, h)
    ag_attn.wait_all()
    hidden = r.x[...] + (r.t1[...].reshape(RP, D).astype(F32) + r.attn_bias[...])
    r.hidden[...] = hidden

    @pl.when(at_first)
    def _():
        resid_copy(r.hidden).start()

    normed_second, inv_second = standardize(hidden)
    r.h2[...] = normed_second
    r.r2[...] = inv_second
    r.nb[...] = (normed_second * scale1 + shift1).astype(BF16)

    def dispatch_one(k, carry):
        there = dispatch.ahead(k)
        r.o1[there] = nn(r.place[there], r.nb[...]).astype(BF16)
        dispatch.start(k)
        return carry

    lax.fori_loop(1, E, dispatch_one, 0)
    r.b1[e] = nn(r.place[e], r.nb[...]).astype(BF16)

    @pl.when(at_first)
    def _():
        load(0).wait()
        load(1).wait()

        def both(image, k):
            expert_block(image)
            forward_part(image, k)

        each_block(dispatch, both)
        finish_forward(True)
        r.g[...] = from_other_section()
        dispatch_grads()

        def back(image, k):
            raw_block(image)
            backward_part(image, k)

        each_block(grads, back)

    @pl.when(at_second)
    def _():
        load(0).wait()

        def both(image, k):
            expert_block(image)
            backward_part(image, k)

        each_block(dispatch, both)
        forward_part(e, 0)

        def one(k, carry):
            forward_part(parts.behind(k), k)
            return carry

        lax.fori_loop(1, E, one, 0)

    slots = E * CAP
    r.grad_expert_out[...] = tn(
        r.act[...].reshape(slots, HW), r.b3[...].reshape(slots, D)
    )
    r.grad_expert_out_bias[...] = jnp.sum(
        r.b3[...].reshape(slots, D).astype(F32), axis=0, keepdims=True
    )
    grad_parts.wait_all()
    own = scatter_chunks(rs_grad, r.p3, lambda rows: combined(r.b4, False, rows))
    r.grad_expert_in[...] = tn(
        r.b1[...].reshape(slots, D), r.gpb[...].reshape(slots, HW)
    )
    r.grad_expert_in_bias[...] = r.in_bias[...]
    for h in range(H):
        rows = rows_of(t, h)
        own[h] = collect(rs_grad, r.l3, own, h)
        delta = norm_back(own[h], r.h2[rows, :], r.r2[rows, :], scale1)
        r.t3[t, piece(h)] = delta.astype(BF16)
        hand_on(r.t3, ag_grad, None, h)

    def add_small(row, value):
        r.small[row : row + 1, :] = r.small[row : row + 1, :] + jnp.sum(value, axis=0, keepdims=True)

    for h in range(H):
        add_small(1, own[h] * r.h2[rows_of(t, h), :])
        add_small(3, own[h])
    ag_grad.wait_all()
    grad_hidden = r.g[...] + r.t3[...].reshape(RP, D).astype(F32)
    r.g[...] = grad_hidden

    @pl.when(at_second)
    def _():
        resid_copy(r.g).start()

    for h in range(H):
        add_small(4, r.g[rows_of(t, h), :])
    grad_hidden_b = grad_hidden.astype(BF16)
    grad_mixed = nt(grad_hidden_b, r.attn_weight[...]).astype(BF16)
    r.w_part[...] = jnp.zeros((E * WC, D), BF16)
    r.w_part[0:W, :] = tn(r.mixed[...], grad_hidden_b).astype(BF16)
    rs_weight.start_all()
    found = [[], [], []]
    for h in range(heads):
        cols = slice(h * HEAD_DIM, (h + 1) * HEAD_DIM)
        query, key, value = r.qkv[0][:, cols], r.qkv[1][:, cols], r.qkv[2][:, cols]
        grad_mixed_h = grad_mixed[:, cols]
        probs = r.probs[h]
        grad_values = tn(probs.astype(BF16), grad_mixed_h)
        grad_probs = nt(grad_mixed_h, value)
        row_delta = jnp.sum(
            grad_mixed_h.astype(F32) * r.mixed[...][:, cols].astype(F32), axis=-1, keepdims=True
        )
        grad_scores = (probs * (grad_probs - row_delta) * scale_factor).astype(BF16)
        found[0].append(nn(grad_scores, key))
        found[1].append(tn(grad_scores, query))
        found[2].append(grad_values)
    for j in (0, 2):
        row = 5 + j // 2
        r.small[row : row + 1, 0:W] = jnp.concatenate(
            [jnp.sum(columns, axis=0, keepdims=True) for columns in found[j]], axis=1
        )
    flat = jnp.concatenate(found[0] + found[1] + found[2], axis=1).astype(BF16)
    r.grad_flat[...] = flat
    r.gp[e] = flat[0:RG]

    def proj_chunk(rows):
        return nn(r.grad_flat[rows, :], r.proj_weight[...].reshape(3 * W, D))

    own = scatter_chunks(rs_proj, r.p4, proj_chunk)
    all_proj.start_all()
    normed_first, inv_first = standardize(r.x[...])
    for h in range(H):
        r.p4[t, piece(h)] = own[h].astype(BF16)
    partial_rows = r.p4[...].reshape(RP, D).astype(F32)
    add_small(0, partial_rows * normed_first)
    add_small(2, partial_rows)
    small_t.start_all()
    r.h1[...] = normed_first
    r.r1[...] = inv_first
    for h in range(H):
        rows = rows_of(t, h)
        own[h] = collect(rs_proj, r.l4, own, h)
        r.t4[t, piece(h)] = norm_back(own[h], r.h1[rows, :], r.r1[rows, :], scale0).astype(BF16)
        hand_on(r.t4, ag_proj, at_second, h)

    small_t.wait_all()
    total = r.small[...]
    summed = total
    for k in range(1, T):
        summed = summed + r.small_t[k - 1]
    r.small2[...] = jnp.where(iota((8, D), 0) < 5, summed, total)
    small_e.start_all()
    rs_weight.wait_all()
    total = r.w_part[weight_rows(e), :].astype(F32)
    for k in range(1, E):
        total = total + r.w_land[k - 1].astype(F32)
    r.w_sum[weight_rows(e), :] = total.astype(BF16)
    ag_weight.start_all()

    @pl.when(at_second)
    def _():
        finish_forward(None)

    all_normed.wait_all()
    all_proj.wait_all()
    tokens = E * RG
    grad_proj = tn(r.gp[...].reshape(tokens, 3 * W), r.na[...].reshape(tokens, D))
    r.grad_proj[...] = grad_proj.reshape(3, W, D)
    small_e.wait_all()
    total = r.small2[...]
    for k in range(1, E):
        total = total + r.small_e[k - 1]
    r.grad_norm_scale[...] = total[0:2]
    r.grad_norm_shift[...] = total[2:4]
    r.grad_attn_bias[...] = total[4:5]
    r.grad_proj_bias[...] = total[5:7, 0:W]
    ag_weight.wait_all()
    r.grad_attn_weight[...] = r.w_sum[0:W, :].astype(F32)
    ag_proj.wait_all()
    grad_in = r.g[...] + r.t4[...].reshape(RP, D).astype(F32)
    r.section_in_grad[...] = grad_in[0:R]

    for swapped in (
        rs_attn, ag_attn, rs_moe, ag_moe, rs_grad, ag_grad, rs_proj, ag_proj,
        dispatch, parts, grads, grad_parts,
        all_normed, all_proj, rs_weight, ag_weight, small_e, small_t,
    ):
        swapped.drain()
    resid_copy(r.resid_in).wait_send()
    for h in range(H):
        for k in range(T):
            cross_copy(r.t4, k, h).wait_send()


def write_kernel(count, *refs):
    sems = refs[-1]
    copies = []
    for k in range(count):
        source, target = refs[k], refs[count + k]
        if len(target.shape) > len(source.shape):
            target = target.at[:, 0, :]
        copies.append(pltpu.make_async_copy(source, target, sems.at[k]))
    for copy in copies:
        copy.start()
    for copy in copies:
        copy.wait()


def slot_count(row_count, experts):
    return max(2, (3 * TOPK * row_count + 2 * experts - 1) // (2 * experts))


def round_up(value, unit):
    return -(-value // unit) * unit


def on_device(
    inputs,
    cotangent,
    norm_scale,
    norm_shift,
    proj_weight,
    proj_bias,
    attn_weight,
    attn_bias,
    expert_in,
    expert_in_bias,
    expert_out,
    expert_out_bias,
    routes,
    gate_weights,
):
    E, T = lax.axis_size("expert"), lax.axis_size("tensor")
    R, D = inputs.shape[1:]
    W, HW = proj_weight.shape[3], expert_in.shape[3]
    CH = round_up(-(-R // T), ROW_TILE)
    RP = T * CH
    CAP = round_up(slot_count(R, E), ROW_TILE)
    RG = round_up(R, ROW_TILE)
    H = 2 if CH % (2 * ROW_TILE) == 0 else 1
    EP = round_up(E, ROW_TILE)
    WC = round_up(-(-W // E), ROW_TILE)
    d = types.SimpleNamespace(
        E=E, T=T, R=R, RG=RG, RP=RP, CH=CH, CAP=CAP, D=D, W=W, HW=HW, H=H, EP=EP, WC=WC
    )
    heads = W // HEAD_DIM

    operands = dict(
        inputs=jnp.transpose(inputs, (1, 0, 2)),
        cotangent=jnp.transpose(cotangent, (1, 0, 2)),
        norm_scale=norm_scale[0],
        norm_shift=norm_shift[0],
        proj_weight=jnp.transpose(proj_weight[0], (1, 2, 0)),
        proj_bias=proj_bias[0],
        attn_weight=attn_weight[0],
        attn_bias=attn_bias,
        expert_in=expert_in[0, 0],
        expert_in_bias=expert_in_bias[0],
        expert_out=expert_out[0, 0],
        expert_out_bias=expert_out_bias[0],
        routes=routes[0, 0].T,
        gate_weights=gate_weights[0, 0].T,
    )
    results = dict(
        section_out=(R, D),
        section_in_grad=(R, D),
        grad_norm_scale=(2, D),
        grad_norm_shift=(2, D),
        grad_proj_bias=(2, W),
        grad_attn_bias=(1, D),
        grad_proj=(3, W, D),
        grad_attn_weight=(W, D),
        grad_expert_in=(D, HW),
        grad_expert_in_bias=(1, HW),
        grad_expert_out=(HW, D),
        grad_expert_out_bias=(1, D),
    )
    scratch = dict(
        x=((RP, D), F32),
        rows_in=((R, D), F32),
        g=((RP, D), F32),
        hidden=((RP, D), F32),
        h2=((RP, D), F32),
        r2=((RP, 1), F32),
        nb=((RP, D), BF16),
        resid_in=((RP, D), F32),
        delta_in=((T, CH, D), BF16),
        qkv=((3, RP, W), BF16),
        probs=((heads, RP, RP), F32),
        na=((E, RG, D), BF16),
        mixed=((RP, W), BF16),
        gp=((E, RG, 3 * W), BF16),
        grad_flat=((RP, 3 * W), BF16),
        h1=((RP, D), F32),
        r1=((RP, 1), F32),
        w_part=((E * WC, D), BF16),
        w_land=((E - 1, WC, D), BF16),
        w_sum=((E * WC, D), BF16),
        rt=((RP, 8), F32),
        gt=((RP, 8), F32),
        rt_t=((8, RP), F32),
        gt_t=((8, RP), F32),
        w_in=((D, HW), BF16),
        w_out=((HW, D), BF16),
        pick=((E, RP, CAP), BF16),
        place=((E, CAP, RP), BF16),
        act=((E, CAP, HW), BF16),
        gpb=((E, CAP, HW), BF16),
        slope=((E, CAP, HW), F32),
        raw=((E, CAP, HW), F32),
        in_bias=((1, HW), F32),
        small=((8, D), F32),
        small2=((8, D), F32),
        small_e=((E - 1, 8, D), F32),
        small_t=((T - 1, 8, D), F32),
    )
    for k in range(1, 5):
        scratch[f"p{k}"] = ((T, CH, D), BF16)
        scratch[f"l{k}"] = ((T - 1, CH, D), BF16)
        scratch[f"t{k}"] = ((T, CH, D), BF16)
        scratch[f"o{k}"] = ((E, CAP, D), BF16)
        scratch[f"b{k}"] = ((E, CAP, D), BF16)
    sems = pltpu.SemaphoreType.DMA((PHASES, max(E, T), H))
    names = list(operands) + list(results) + list(scratch) + ["load_sem", "send_sem", "recv_sem"]
    in_vmem, in_place = pl.BlockSpec(memory_space=pltpu.VMEM), pl.BlockSpec(memory_space=pl.ANY)
    loaded = ("inputs", "cotangent", "expert_in", "expert_out")
    found = pl.pallas_call(
        functools.partial(relay_kernel, names, d),
        out_shape=[pltpu.VMEM(shape, F32) for shape in results.values()],
        in_specs=[in_place if name in loaded else in_vmem for name in operands],
        out_specs=[in_vmem] * len(results),
        scratch_shapes=[pltpu.VMEM(shape, dtype) for shape, dtype in scratch.values()]
        + [pltpu.SemaphoreType.DMA((len(loaded),)), sems, sems],
        compiler_params=pltpu.CompilerParams(
            collective_id=0, has_side_effects=True, vmem_limit_bytes=52 * 2**20
        ),
        name="relay",
    )(*operands.values())
    shapes = [
        (R, 1, D) if name.startswith("section") else shape for name, shape in results.items()
    ]
    written = pl.pallas_call(
        functools.partial(write_kernel, len(results)),
        out_shape=[jax.ShapeDtypeStruct(shape, F32) for shape in shapes],
        in_specs=[in_vmem] * len(results),
        out_specs=[in_place] * len(results),
        scratch_shapes=[pltpu.SemaphoreType.DMA((len(results),))],
        compiler_params=pltpu.CompilerParams(vmem_limit_bytes=2**20),
        name="write",
    )(*[pltpu.with_memory_space_constraint(array, pltpu.VMEM) for array in found])
    found = types.SimpleNamespace(**dict(zip(results, written)))
    return (
        jnp.transpose(found.section_out, (1, 0, 2))[None],
        jnp.transpose(found.section_in_grad, (1, 0, 2))[None],
        found.grad_norm_scale[None],
        found.grad_norm_shift[None],
        jnp.transpose(found.grad_proj, (2, 0, 1))[None],
        found.grad_proj_bias[None],
        found.grad_attn_weight[None],
        found.grad_attn_bias,
        found.grad_expert_in[None, None],
        found.grad_expert_in_bias[None],
        found.grad_expert_out[None, None],
        found.grad_expert_out_bias[None],
    )


def solution(mesh):
    in_specs = (
        P(None, "expert", None),
        P(None, "expert", None),
        P("section", None, None),
        P("section", None, None),
        P("section", None, None, "tensor"),
        P("section", None, "tensor"),
        P("section", "tensor", None),
        P("section", None),
        P("section", "expert", None, "tensor"),
        P("section", "expert", "tensor"),
        P("section", "expert", "tensor", None),
        P("section", "expert", None),
        P("section", None, "expert", None),
        P("section", None, "expert", None),
    )
    out_specs = (
        P("section", None, "expert", None),
        P("section", None, "expert", None),
        P("section", None, None),
        P("section", None, None),
        P("section", None, None, "tensor"),
        P("section", None, "tensor"),
        P("section", "tensor", None),
        P("section", None),
        P("section", "expert", None, "tensor"),
        P("section", "expert", "tensor"),
        P("section", "expert", "tensor", None),
        P("section", "expert", None),
    )
    return jax.shard_map(
        on_device, mesh=mesh, in_specs=in_specs, out_specs=out_specs, check_vma=False
    )
```

```python
import functools
import math
import types

import jax
import jax.numpy as jnp
from jax import lax
from jax.experimental import pallas as pl
from jax.experimental.pallas import tpu as pltpu
from jax.sharding import PartitionSpec as P

HEAD_DIM = 64
TOPK = 2

NORM_EPSILON = 1e-06
GELU_FACTOR = 0.7978845608028654
CUBIC_TERM = 0.044715

MESH = pl.DeviceIdType.MESH
ROW_TILE = 16
BF16 = jnp.bfloat16
F32 = jnp.float32

(
    RS_ATTN,
    AG_ATTN,
    DISPATCH,
    PARTS,
    RS_MOE,
    AG_MOE,
    CROSS,
    RESID,
    GRADS,
    GRAD_PARTS,
    RS_GRAD,
    AG_GRAD,
    RS_PROJ,
    AG_PROJ,
    ALL_NORMED,
    RS_WEIGHT,
    AG_WEIGHT,
    ALL_PROJ,
    SMALL_E,
    SMALL_T,
    PHASES,
) = range(21)


def nn(left, right):
    return jnp.dot(left, right, preferred_element_type=F32)


def nt(left, right):
    return lax.dot_general(left, right, (((1,), (1,)), ((), ())), preferred_element_type=F32)


def tn(left, right):
    return lax.dot_general(left, right, (((0,), (0,)), ((), ())), preferred_element_type=F32)


def standardize(values):
    average = jnp.mean(values, axis=-1, keepdims=True)
    centred = values - average
    variance = jnp.mean(centred * centred, axis=-1, keepdims=True)
    inv_std = lax.rsqrt(variance + NORM_EPSILON)
    return centred * inv_std, inv_std


def norm_back(grad_normed, normed, inv_std, scale_row):
    scaled = grad_normed * scale_row
    return (
        scaled
        - jnp.mean(scaled, axis=-1, keepdims=True)
        - normed * jnp.mean(scaled * normed, axis=-1, keepdims=True)
    ) * inv_std


def iota(shape, axis):
    return lax.broadcasted_iota(jnp.int32, shape, axis)


class Swap:
    def __init__(self, r, phase, axis, pieces, source, landing):
        self.r, self.phase, self.axis, self.pieces = r, phase, axis, pieces
        self.size = lax.axis_size(axis)
        self.me = lax.axis_index(axis)
        side = math.isqrt(self.size)
        self.q = side if axis == "expert" and side * side == self.size else 1
        self.source, self.landing = source, landing

    def walk(self, high, low):
        return lax.rem(high, self.size // self.q) * self.q + lax.rem(low, self.q)

    def ahead(self, k):
        q = self.q
        return self.walk(self.me // q + k // q, self.me % q + k % q)

    def behind(self, k):
        q = self.q
        return self.walk(self.me // q + self.size // q - k // q, self.me % q + q - k % q)

    def back(self, k):
        q = self.q
        return self.walk(self.size // q - k // q, q - k % q)

    def copy(self, k, h):
        there = self.ahead(k)
        return pltpu.make_async_remote_copy(
            src_ref=self.source(there, h),
            dst_ref=self.landing(k, h),
            send_sem=self.r.send_sem.at[self.phase, k, h],
            recv_sem=self.r.recv_sem.at[self.phase, k, h],
            device_id={self.axis: there},
            device_id_type=MESH,
        )

    def start(self, k, h=0):
        self.copy(k, h).start()

    def start_all(self, h=0):
        for k in range(1, self.size):
            self.start(k, h)

    def wait(self, k, h=0):
        self.copy(k, h).wait_recv()

    def wait_all(self):
        for h in range(self.pieces):
            for k in range(1, self.size):
                self.wait(k, h)

    def drain(self):
        for h in range(self.pieces):
            for k in range(1, self.size):
                self.copy(k, h).wait_send()


def relay_kernel(names, d, *refs):
    r = types.SimpleNamespace(**dict(zip(names, refs)))
    E, T, R, RG, RP, CH, H, EP = d.E, d.T, d.R, d.RG, d.RP, d.CH, d.H, d.EP
    HH, WC = CH // H, d.WC
    CAP, D, W, HW = d.CAP, d.D, d.W, d.HW
    heads = W // HEAD_DIM
    scale_factor = HEAD_DIM ** (-0.5)
    s, e, t = [lax.axis_index(name) for name in ("section", "expert", "tensor")]
    other = 1 - s
    at_first, at_second = s == 0, s == 1

    def piece(h):
        return pl.ds(h * HH, HH)

    def gather(phase, ref):
        return Swap(r, phase, "expert", 1, lambda there, h: ref.at[e], lambda k, h: ref.at[e])

    def gather_rows(phase, ref):
        return Swap(
            r, phase, "tensor", H,
            lambda there, h: ref.at[t, piece(h)],
            lambda k, h: ref.at[t, piece(h)],
        )

    def scatter_rows(phase, source, landing):
        return Swap(
            r, phase, "tensor", H,
            lambda there, h: source.at[there, piece(h)],
            lambda k, h: landing.at[k - 1, piece(h)],
        )

    rs_attn = scatter_rows(RS_ATTN, r.p1, r.l1)
    ag_attn = gather_rows(AG_ATTN, r.t1)
    rs_moe = scatter_rows(RS_MOE, r.p2, r.l2)
    ag_moe = gather_rows(AG_MOE, r.t2)
    rs_grad = scatter_rows(RS_GRAD, r.p3, r.l3)
    ag_grad = gather_rows(AG_GRAD, r.t3)
    rs_proj = scatter_rows(RS_PROJ, r.p4, r.l4)
    ag_proj = gather_rows(AG_PROJ, r.t4)

    def routed(phase, source, landing):
        return Swap(
            r, phase, "expert", 1, lambda there, h: source.at[there], lambda k, h: landing.at[e]
        )

    dispatch = routed(DISPATCH, r.o1, r.b1)
    parts = routed(PARTS, r.o2, r.b2)
    grads = routed(GRADS, r.o3, r.b3)
    grad_parts = routed(GRAD_PARTS, r.o4, r.b4)
    all_normed = gather(ALL_NORMED, r.na)

    def weight_rows(owner):
        return pl.ds(pl.multiple_of(owner * WC, WC), WC)

    rs_weight = Swap(
        r, RS_WEIGHT, "expert", 1,
        lambda there, h: r.w_part.at[weight_rows(there)],
        lambda k, h: r.w_land.at[k - 1],
    )
    ag_weight = Swap(
        r, AG_WEIGHT, "expert", 1,
        lambda there, h: r.w_sum.at[weight_rows(e)],
        lambda k, h: r.w_sum.at[weight_rows(e)],
    )
    all_proj = gather(ALL_PROJ, r.gp)
    small_e = Swap(
        r, SMALL_E, "expert", 1, lambda there, h: r.small2, lambda k, h: r.small_e.at[k - 1]
    )
    small_t = Swap(
        r, SMALL_T, "tensor", 1, lambda there, h: r.small, lambda k, h: r.small_t.at[k - 1]
    )

    def cross_copy(source, k, h):
        return pltpu.make_async_remote_copy(
            src_ref=source.at[t, piece(h)],
            dst_ref=r.delta_in.at[t, piece(h)],
            send_sem=r.send_sem.at[CROSS, k, h],
            recv_sem=r.recv_sem.at[CROSS, k, h],
            device_id={"section": other, "tensor": lax.rem(t + k, T)},
            device_id_type=MESH,
        )

    def resid_copy(source):
        return pltpu.make_async_remote_copy(
            src_ref=source,
            dst_ref=r.resid_in,
            send_sem=r.send_sem.at[RESID, 0, 0],
            recv_sem=r.recv_sem.at[RESID, 0, 0],
            device_id={"section": other},
            device_id_type=MESH,
        )

    def load(k):
        source, target = (
            (r.expert_in, r.w_in), (r.expert_out, r.w_out),
            (r.inputs.at[:, 0, :], r.rows_in), (r.cotangent.at[:, 0, :], r.rows_in),
        )[k]
        return pltpu.make_async_copy(source, target, r.load_sem.at[k])

    def from_other_section():
        resid_copy(r.resid_in).wait_recv()
        for h in range(H):
            for k in range(T):
                cross_copy(r.delta_in, k, h).wait_recv()
        return r.resid_in[...] + r.delta_in[...].reshape(RP, D).astype(F32)

    r.x[...] = jnp.zeros((RP, D), F32)
    r.g[...] = jnp.zeros((RP, D), F32)

    @pl.when(at_first)
    def _():
        load(2).start()

    @pl.when(at_second)
    def _():
        load(3).start()

    load(1).start()
    load(0).start()

    barrier = pltpu.get_barrier_semaphore()
    friends = [{"tensor": lax.rem(t + k, T)} for k in range(1, T)]
    friends += [{"expert": lax.rem(e + k, E)} for k in range(1, E)]
    friends += [{"section": other, "tensor": lax.rem(t + k, T)} for k in range(T)]
    for device in friends:
        pl.semaphore_signal(barrier, inc=1, device_id=device, device_id_type=MESH)

    def all_are_here():
        pl.semaphore_wait(barrier, len(friends))

    def rows_of(chunk, h):
        return pl.ds(pl.multiple_of(chunk * CH + h * HH, HH), HH)

    def gate_of(expert, rows=slice(None)):
        ids, gates = r.rt[rows, :], r.gt[rows, :]
        named = lax.convert_element_type(expert, F32)
        return jnp.sum(jnp.where(ids == named, gates, 0.0), axis=-1, keepdims=True)

    def routing():
        r.rt_t[...] = jnp.full((8, RP), -1.0, F32)
        r.gt_t[...] = jnp.zeros((8, RP), F32)
        r.rt_t[0:TOPK, 0:R] = r.routes[...].astype(F32)
        r.gt_t[0:TOPK, 0:R] = r.gate_weights[...]
        ids = r.rt_t[...]
        r.rt[...] = jnp.transpose(ids)
        r.gt[...] = jnp.transpose(r.gt_t[...])
        expert = iota((EP, RP), 0).astype(F32)
        named = jnp.where((ids[0:1] == expert) | (ids[1:2] == expert), 1.0, 0.0)
        later = jnp.where(iota((RP, RP), 0) < iota((RP, RP), 1), 1.0, 0.0)
        slot_t = jnp.where(named > 0.5, nn(named.astype(BF16), later.astype(BF16)), -1.0)
        slot = jnp.transpose(slot_t)
        wide = iota((RP, CAP), 1).astype(F32)
        tall = iota((CAP, RP), 0).astype(F32)
        for k in range(E):
            r.pick[k] = jnp.where(slot[:, k : k + 1] == wide, 1.0, 0.0).astype(BF16)
            r.place[k] = jnp.where(slot_t[k : k + 1, :] == tall, 1.0, 0.0).astype(BF16)

    def dispatch_grads():
        def outgoing(expert):
            weighted = (gate_of(expert) * r.g[...]).astype(BF16)
            return nn(r.place[expert], weighted).astype(BF16)

        def one(k, carry):
            there = grads.ahead(k)
            r.o3[there] = outgoing(there)
            grads.start(k)
            return carry

        lax.fori_loop(1, E, one, 0)
        r.b3[e] = outgoing(e)

    def each_block(swapped, body):
        body(e, 0)

        def one(k, carry):
            swapped.wait(k)
            body(swapped.behind(k), k)
            return carry

        lax.fori_loop(1, E, one, 0)

    def send_part(swapped, outgoing, landing, image, k, value):
        if isinstance(k, int):
            landing[image] = value
        else:
            outgoing[image] = value
            swapped.start(swapped.back(k))

    def raw_block(image):
        r.raw[image] = nt(r.b3[image], r.w_out[...])

    def backward_part(image, k):
        grad_pre = r.raw[image] * r.slope[image]
        r.in_bias[...] = r.in_bias[...] + jnp.sum(grad_pre, axis=0, keepdims=True)
        grad_pre_b = grad_pre.astype(BF16)
        r.gpb[image] = grad_pre_b
        value = nt(grad_pre_b, r.w_in[...]).astype(BF16)
        send_part(grad_parts, r.o4, r.b4, image, k, value)

    def forward_part(image, k):
        bias = jnp.where(t == 0, r.expert_out_bias[...], 0.0)
        value = (nn(r.act[image], r.w_out[...]) + bias).astype(BF16)
        send_part(parts, r.o2, r.b2, image, k, value)

    def expert_block(image):
        pre = nn(r.b1[image], r.w_in[...]) + r.expert_in_bias[...]
        square = pre * pre
        tangent = jnp.tanh(GELU_FACTOR * (pre + CUBIC_TERM * square * pre))
        half = 0.5 * (1.0 + tangent)
        r.act[image] = (pre * half).astype(BF16)
        r.slope[image] = half + 0.5 * pre * (1.0 - tangent * tangent) * GELU_FACTOR * (
            1.0 + 3.0 * CUBIC_TERM * square
        )

    def scatter_chunks(swapped, part, chunk_of):
        for h in range(H):
            for k in range(1, T):
                there = swapped.ahead(k)
                part[there, piece(h)] = chunk_of(rows_of(there, h)).astype(BF16)
                swapped.start(k, h)
        return [chunk_of(rows_of(t, h)) for h in range(H)]

    def collect(swapped, landing, own, h):
        total = own[h]
        for k in range(1, T):
            swapped.wait(k, h)
            total = total + landing[k - 1, piece(h)].astype(F32)
        return total

    def cross(ref, h):
        for k in range(T):
            cross_copy(ref, k, h).start()

    def combined(landed, gated, rows):
        total = None
        for k in range(E):
            term = nn(r.pick[k, rows, :], landed[k])
            if gated:
                term = gate_of(k, rows) * term
            total = term if total is None else total + term
        return total

    def finish_forward(crossing):
        parts.wait_all()
        own = scatter_chunks(rs_moe, r.p2, lambda rows: combined(r.b2, True, rows))
        for h in range(H):
            r.t2[t, piece(h)] = collect(rs_moe, r.l2, own, h).astype(BF16)
            if crossing:
                cross(r.t2, h)
        for h in range(H):
            ag_moe.start_all(h)
        ag_moe.wait_all()
        out = r.hidden[...] + r.t2[...].reshape(RP, D).astype(F32)
        r.section_out[...] = out[0:R]

    r.in_bias[...] = jnp.zeros((1, HW), F32)
    r.small[...] = jnp.zeros((8, D), F32)

    @pl.when(at_first)
    def _():
        load(2).wait()
        r.x[0:R, :] = r.rows_in[...]

    @pl.when(at_second)
    def _():
        routing()
        load(3).wait()
        all_are_here()
        r.g[0:R, :] = r.rows_in[...]
        dispatch_grads()
        load(1).wait()
        each_block(grads, lambda image, k: raw_block(image))
        r.x[...] = from_other_section()

    inside = iota((RP, 1), 0) < R
    scale0, scale1 = r.norm_scale[0:1, :], r.norm_scale[1:2, :]
    shift0, shift1 = r.norm_shift[0:1, :], r.norm_shift[1:2, :]
    normed_first, _ = standardize(r.x[...])
    normed_a = jnp.where(inside, normed_first * scale0 + shift0, 0.0).astype(BF16)
    r.na[e] = normed_a[0:RG]
    query = nt(normed_a, r.proj_weight[0]) + r.proj_bias[0:1, :]
    r.qkv[0] = jnp.where(inside, query, 0.0).astype(BF16)
    r.qkv[1] = nt(normed_a, r.proj_weight[1]).astype(BF16)
    value = nt(normed_a, r.proj_weight[2]) + r.proj_bias[1:2, :]
    r.qkv[2] = jnp.where(inside, value, 0.0).astype(BF16)
    real_key = iota((RP, RP), 1) < R
    mixed = []
    for h in range(heads):
        cols = slice(h * HEAD_DIM, (h + 1) * HEAD_DIM)
        scores = nt(r.qkv[0][:, cols], r.qkv[1][:, cols]) * scale_factor
        powers = jnp.where(real_key, jnp.exp(scores), 0.0)
        probs = powers / jnp.sum(powers, axis=-1, keepdims=True)
        r.probs[h] = probs
        mixed.append(nn(probs.astype(BF16), r.qkv[2][:, cols]))
    r.mixed[...] = jnp.concatenate(mixed, axis=1).astype(BF16)

    @pl.when(at_first)
    def _():
        all_are_here()

    own = scatter_chunks(
        rs_attn, r.p1, lambda rows: nn(r.mixed[rows, :], r.attn_weight[...])
    )
    all_normed.start_all()

    @pl.when(at_first)
    def _():
        routing()

    for h in range(H):
        r.t1[t, piece(h)] = collect(rs_attn, r.l1, own, h).astype(BF16)
        ag_attn.start_all(h)
    ag_attn.wait_all()
    hidden = r.x[...] + (r.t1[...].reshape(RP, D).astype(F32) + r.attn_bias[...])
    r.hidden[...] = hidden

    @pl.when(at_first)
    def _():
        resid_copy(r.hidden).start()

    normed_second, inv_second = standardize(hidden)
    r.h2[...] = normed_second
    r.r2[...] = inv_second
    r.nb[...] = (normed_second * scale1 + shift1).astype(BF16)

    def dispatch_one(k, carry):
        there = dispatch.ahead(k)
        r.o1[there] = nn(r.place[there], r.nb[...]).astype(BF16)
        dispatch.start(k)
        return carry

    lax.fori_loop(1, E, dispatch_one, 0)
    r.b1[e] = nn(r.place[e], r.nb[...]).astype(BF16)

    @pl.when(at_first)
    def _():
        load(0).wait()
        load(1).wait()

        def both(image, k):
            expert_block(image)
            forward_part(image, k)

        each_block(dispatch, both)
        finish_forward(True)
        r.g[...] = from_other_section()
        dispatch_grads()

        def back(image, k):
            raw_block(image)
            backward_part(image, k)

        each_block(grads, back)

    @pl.when(at_second)
    def _():
        load(0).wait()

        def both(image, k):
            expert_block(image)
            backward_part(image, k)

        each_block(dispatch, both)
        forward_part(e, 0)

        def one(k, carry):
            forward_part(parts.behind(k), k)
            return carry

        lax.fori_loop(1, E, one, 0)

    slots = E * CAP
    r.grad_expert_out[...] = tn(
        r.act[...].reshape(slots, HW), r.b3[...].reshape(slots, D)
    )
    r.grad_expert_out_bias[...] = jnp.sum(
        r.b3[...].reshape(slots, D).astype(F32), axis=0, keepdims=True
    )
    grad_parts.wait_all()
    own = scatter_chunks(rs_grad, r.p3, lambda rows: combined(r.b4, False, rows))
    r.grad_expert_in[...] = tn(
        r.b1[...].reshape(slots, D), r.gpb[...].reshape(slots, HW)
    )
    r.grad_expert_in_bias[...] = r.in_bias[...]
    for h in range(H):
        rows = rows_of(t, h)
        own[h] = collect(rs_grad, r.l3, own, h)
        delta = norm_back(own[h], r.h2[rows, :], r.r2[rows, :], scale1)
        r.t3[t, piece(h)] = delta.astype(BF16)
        ag_grad.start_all(h)

    def add_small(row, value):
        r.small[row : row + 1, :] = r.small[row : row + 1, :] + jnp.sum(value, axis=0, keepdims=True)

    for h in range(H):
        add_small(1, own[h] * r.h2[rows_of(t, h), :])
        add_small(3, own[h])
    ag_grad.wait_all()
    grad_hidden = r.g[...] + r.t3[...].reshape(RP, D).astype(F32)
    r.g[...] = grad_hidden

    @pl.when(at_second)
    def _():
        resid_copy(r.g).start()

    for h in range(H):
        add_small(4, r.g[rows_of(t, h), :])
    grad_hidden_b = grad_hidden.astype(BF16)
    grad_mixed = nt(grad_hidden_b, r.attn_weight[...]).astype(BF16)
    r.w_part[...] = jnp.zeros((E * WC, D), BF16)
    r.w_part[0:W, :] = tn(r.mixed[...], grad_hidden_b).astype(BF16)
    rs_weight.start_all()
    found = [[], [], []]
    for h in range(heads):
        cols = slice(h * HEAD_DIM, (h + 1) * HEAD_DIM)
        query, key, value = r.qkv[0][:, cols], r.qkv[1][:, cols], r.qkv[2][:, cols]
        grad_mixed_h = grad_mixed[:, cols]
        probs = r.probs[h]
        grad_values = tn(probs.astype(BF16), grad_mixed_h)
        grad_probs = nt(grad_mixed_h, value)
        row_delta = jnp.sum(
            grad_mixed_h.astype(F32) * r.mixed[...][:, cols].astype(F32), axis=-1, keepdims=True
        )
        grad_scores = (probs * (grad_probs - row_delta) * scale_factor).astype(BF16)
        found[0].append(nn(grad_scores, key))
        found[1].append(tn(grad_scores, query))
        found[2].append(grad_values)
    for j in (0, 2):
        row = 5 + j // 2
        r.small[row : row + 1, 0:W] = jnp.concatenate(
            [jnp.sum(columns, axis=0, keepdims=True) for columns in found[j]], axis=1
        )
    flat = jnp.concatenate(found[0] + found[1] + found[2], axis=1).astype(BF16)
    r.grad_flat[...] = flat
    r.gp[e] = flat[0:RG]

    def proj_chunk(rows):
        return nn(r.grad_flat[rows, :], r.proj_weight[...].reshape(3 * W, D))

    own = scatter_chunks(rs_proj, r.p4, proj_chunk)
    all_proj.start_all()
    normed_first, inv_first = standardize(r.x[...])
    for h in range(H):
        r.p4[t, piece(h)] = own[h].astype(BF16)
    partial_rows = r.p4[...].reshape(RP, D).astype(F32)
    add_small(0, partial_rows * normed_first)
    add_small(2, partial_rows)
    small_t.start_all()
    r.h1[...] = normed_first
    r.r1[...] = inv_first
    for h in range(H):
        rows = rows_of(t, h)
        own[h] = collect(rs_proj, r.l4, own, h)
        r.t4[t, piece(h)] = norm_back(own[h], r.h1[rows, :], r.r1[rows, :], scale0).astype(BF16)

        @pl.when(at_second)
        def _():
            cross(r.t4, h)

        @pl.when(at_first)
        def _():
            ag_proj.start_all(h)

    @pl.when(at_second)
    def _():
        for h in range(H):
            ag_proj.start_all(h)

    small_t.wait_all()
    total = r.small[...]
    summed = total
    for k in range(1, T):
        summed = summed + r.small_t[k - 1]
    r.small2[...] = jnp.where(iota((8, D), 0) < 5, summed, total)
    small_e.start_all()
    rs_weight.wait_all()
    total = r.w_part[weight_rows(e), :].astype(F32)
    for k in range(1, E):
        total = total + r.w_land[k - 1].astype(F32)
    r.w_sum[weight_rows(e), :] = total.astype(BF16)
    ag_weight.start_all()

    @pl.when(at_second)
    def _():
        finish_forward(False)

    all_normed.wait_all()
    all_proj.wait_all()
    tokens = E * RG
    grad_proj = tn(r.gp[...].reshape(tokens, 3 * W), r.na[...].reshape(tokens, D))
    r.grad_proj[...] = grad_proj.reshape(3, W, D)
    small_e.wait_all()
    total = r.small2[...]
    for k in range(1, E):
        total = total + r.small_e[k - 1]
    r.grad_norm_scale[...] = total[0:2]
    r.grad_norm_shift[...] = total[2:4]
    r.grad_attn_bias[...] = total[4:5]
    r.grad_proj_bias[...] = total[5:7, 0:W]
    ag_weight.wait_all()
    r.grad_attn_weight[...] = r.w_sum[0:W, :].astype(F32)
    ag_proj.wait_all()
    grad_in = r.g[...] + r.t4[...].reshape(RP, D).astype(F32)
    r.section_in_grad[...] = grad_in[0:R]

    for swapped in (
        rs_attn, ag_attn, rs_moe, ag_moe, rs_grad, ag_grad, rs_proj, ag_proj,
        dispatch, parts, grads, grad_parts,
        all_normed, all_proj, rs_weight, ag_weight, small_e, small_t,
    ):
        swapped.drain()
    resid_copy(r.resid_in).wait_send()
    for h in range(H):
        for k in range(T):
            cross_copy(r.t4, k, h).wait_send()


def write_kernel(count, *refs):
    sems = refs[-1]
    copies = []
    for k in range(count):
        source, target = refs[k], refs[count + k]
        if len(target.shape) > len(source.shape):
            target = target.at[:, 0, :]
        copies.append(pltpu.make_async_copy(source, target, sems.at[k]))
    for copy in copies:
        copy.start()
    for copy in copies:
        copy.wait()


def slot_count(row_count, experts):
    return max(2, (3 * TOPK * row_count + 2 * experts - 1) // (2 * experts))


def round_up(value, unit):
    return -(-value // unit) * unit


def on_device(
    inputs,
    cotangent,
    norm_scale,
    norm_shift,
    proj_weight,
    proj_bias,
    attn_weight,
    attn_bias,
    expert_in,
    expert_in_bias,
    expert_out,
    expert_out_bias,
    routes,
    gate_weights,
):
    E, T = lax.axis_size("expert"), lax.axis_size("tensor")
    R, D = inputs.shape[1:]
    W, HW = proj_weight.shape[3], expert_in.shape[3]
    CH = round_up(-(-R // T), ROW_TILE)
    RP = T * CH
    CAP = round_up(slot_count(R, E), ROW_TILE)
    RG = round_up(R, ROW_TILE)
    H = 2 if CH % (2 * ROW_TILE) == 0 else 1
    EP = round_up(E, ROW_TILE)
    WC = round_up(-(-W // E), ROW_TILE)
    d = types.SimpleNamespace(
        E=E, T=T, R=R, RG=RG, RP=RP, CH=CH, CAP=CAP, D=D, W=W, HW=HW, H=H, EP=EP, WC=WC
    )
    heads = W // HEAD_DIM

    operands = dict(
        inputs=jnp.transpose(inputs, (1, 0, 2)),
        cotangent=jnp.transpose(cotangent, (1, 0, 2)),
        norm_scale=norm_scale[0],
        norm_shift=norm_shift[0],
        proj_weight=jnp.transpose(proj_weight[0], (1, 2, 0)),
        proj_bias=proj_bias[0],
        attn_weight=attn_weight[0],
        attn_bias=attn_bias,
        expert_in=expert_in[0, 0],
        expert_in_bias=expert_in_bias[0],
        expert_out=expert_out[0, 0],
        expert_out_bias=expert_out_bias[0],
        routes=routes[0, 0].T,
        gate_weights=gate_weights[0, 0].T,
    )
    results = dict(
        section_out=(R, D),
        section_in_grad=(R, D),
        grad_norm_scale=(2, D),
        grad_norm_shift=(2, D),
        grad_proj_bias=(2, W),
        grad_attn_bias=(1, D),
        grad_proj=(3, W, D),
        grad_attn_weight=(W, D),
        grad_expert_in=(D, HW),
        grad_expert_in_bias=(1, HW),
        grad_expert_out=(HW, D),
        grad_expert_out_bias=(1, D),
    )
    scratch = dict(
        x=((RP, D), F32),
        rows_in=((R, D), F32),
        g=((RP, D), F32),
        hidden=((RP, D), F32),
        h2=((RP, D), F32),
        r2=((RP, 1), F32),
        nb=((RP, D), BF16),
        resid_in=((RP, D), F32),
        delta_in=((T, CH, D), BF16),
        qkv=((3, RP, W), BF16),
        probs=((heads, RP, RP), F32),
        na=((E, RG, D), BF16),
        mixed=((RP, W), BF16),
        gp=((E, RG, 3 * W), BF16),
        grad_flat=((RP, 3 * W), BF16),
        h1=((RP, D), F32),
        r1=((RP, 1), F32),
        w_part=((E * WC, D), BF16),
        w_land=((E - 1, WC, D), BF16),
        w_sum=((E * WC, D), BF16),
        rt=((RP, 8), F32),
        gt=((RP, 8), F32),
        rt_t=((8, RP), F32),
        gt_t=((8, RP), F32),
        w_in=((D, HW), BF16),
        w_out=((HW, D), BF16),
        pick=((E, RP, CAP), BF16),
        place=((E, CAP, RP), BF16),
        act=((E, CAP, HW), BF16),
        gpb=((E, CAP, HW), BF16),
        slope=((E, CAP, HW), F32),
        raw=((E, CAP, HW), F32),
        in_bias=((1, HW), F32),
        small=((8, D), F32),
        small2=((8, D), F32),
        small_e=((E - 1, 8, D), F32),
        small_t=((T - 1, 8, D), F32),
    )
    for k in range(1, 5):
        scratch[f"p{k}"] = ((T, CH, D), BF16)
        scratch[f"l{k}"] = ((T - 1, CH, D), BF16)
        scratch[f"t{k}"] = ((T, CH, D), BF16)
        scratch[f"o{k}"] = ((E, CAP, D), BF16)
        scratch[f"b{k}"] = ((E, CAP, D), BF16)
    sems = pltpu.SemaphoreType.DMA((PHASES, max(E, T), H))
    names = list(operands) + list(results) + list(scratch) + ["load_sem", "send_sem", "recv_sem"]
    in_vmem, in_place = pl.BlockSpec(memory_space=pltpu.VMEM), pl.BlockSpec(memory_space=pl.ANY)
    loaded = ("inputs", "cotangent", "expert_in", "expert_out")
    found = pl.pallas_call(
        functools.partial(relay_kernel, names, d),
        out_shape=[pltpu.VMEM(shape, F32) for shape in results.values()],
        in_specs=[in_place if name in loaded else in_vmem for name in operands],
        out_specs=[in_vmem] * len(results),
        scratch_shapes=[pltpu.VMEM(shape, dtype) for shape, dtype in scratch.values()]
        + [pltpu.SemaphoreType.DMA((len(loaded),)), sems, sems],
        compiler_params=pltpu.CompilerParams(
            collective_id=0, has_side_effects=True, vmem_limit_bytes=52 * 2**20
        ),
        name="relay",
    )(*operands.values())
    shapes = [
        (R, 1, D) if name.startswith("section") else shape for name, shape in results.items()
    ]
    written = pl.pallas_call(
        functools.partial(write_kernel, len(results)),
        out_shape=[jax.ShapeDtypeStruct(shape, F32) for shape in shapes],
        in_specs=[in_vmem] * len(results),
        out_specs=[in_place] * len(results),
        scratch_shapes=[pltpu.SemaphoreType.DMA((len(results),))],
        compiler_params=pltpu.CompilerParams(vmem_limit_bytes=2**20),
        name="write",
    )(*[pltpu.with_memory_space_constraint(array, pltpu.VMEM) for array in found])
    found = types.SimpleNamespace(**dict(zip(results, written)))
    return (
        jnp.transpose(found.section_out, (1, 0, 2))[None],
        jnp.transpose(found.section_in_grad, (1, 0, 2))[None],
        found.grad_norm_scale[None],
        found.grad_norm_shift[None],
        jnp.transpose(found.grad_proj, (2, 0, 1))[None],
        found.grad_proj_bias[None],
        found.grad_attn_weight[None],
        found.grad_attn_bias,
        found.grad_expert_in[None, None],
        found.grad_expert_in_bias[None],
        found.grad_expert_out[None, None],
        found.grad_expert_out_bias[None],
    )


def solution(mesh):
    in_specs = (
        P(None, "expert", None),
        P(None, "expert", None),
        P("section", None, None),
        P("section", None, None),
        P("section", None, None, "tensor"),
        P("section", None, "tensor"),
        P("section", "tensor", None),
        P("section", None),
        P("section", "expert", None, "tensor"),
        P("section", "expert", "tensor"),
        P("section", "expert", "tensor", None),
        P("section", "expert", None),
        P("section", None, "expert", None),
        P("section", None, "expert", None),
    )
    out_specs = (
        P("section", None, "expert", None),
        P("section", None, "expert", None),
        P("section", None, None),
        P("section", None, None),
        P("section", None, None, "tensor"),
        P("section", None, "tensor"),
        P("section", "tensor", None),
        P("section", None),
        P("section", "expert", None, "tensor"),
        P("section", "expert", "tensor"),
        P("section", "expert", "tensor", None),
        P("section", "expert", None),
    )
    return jax.shard_map(
        on_device, mesh=mesh, in_specs=in_specs, out_specs=out_specs, check_vma=False
    )
```

```python
import functools
import math
import types

import jax
import jax.numpy as jnp
from jax import lax
from jax.experimental import pallas as pl
from jax.experimental.pallas import tpu as pltpu
from jax.sharding import PartitionSpec as P

HEAD_DIM = 64
TOPK = 2

NORM_EPSILON = 1e-06
GELU_FACTOR = 0.7978845608028654
CUBIC_TERM = 0.044715

MESH = pl.DeviceIdType.MESH
ROW_TILE = 16
BF16 = jnp.bfloat16
F32 = jnp.float32

(
    RS_ATTN,
    AG_ATTN,
    DISPATCH,
    PARTS,
    RS_MOE,
    AG_MOE,
    CROSS,
    RESID,
    GRADS,
    GRAD_PARTS,
    RS_GRAD,
    AG_GRAD,
    RS_PROJ,
    AG_PROJ,
    ALL_NORMED,
    RS_WEIGHT,
    AG_WEIGHT,
    ALL_PROJ,
    SMALL_E,
    SMALL_T,
    PHASES,
) = range(21)


def nn(left, right):
    return jnp.dot(left, right, preferred_element_type=F32)


def nt(left, right):
    return lax.dot_general(left, right, (((1,), (1,)), ((), ())), preferred_element_type=F32)


def tn(left, right):
    return lax.dot_general(left, right, (((0,), (0,)), ((), ())), preferred_element_type=F32)


def standardize(values):
    average = jnp.mean(values, axis=-1, keepdims=True)
    centred = values - average
    variance = jnp.mean(centred * centred, axis=-1, keepdims=True)
    inv_std = lax.rsqrt(variance + NORM_EPSILON)
    return centred * inv_std, inv_std


def norm_back(grad_normed, normed, inv_std, scale_row):
    scaled = grad_normed * scale_row
    return (
        scaled
        - jnp.mean(scaled, axis=-1, keepdims=True)
        - normed * jnp.mean(scaled * normed, axis=-1, keepdims=True)
    ) * inv_std


def iota(shape, axis):
    return lax.broadcasted_iota(jnp.int32, shape, axis)


def always(k, h, body):
    body()


class Swap:
    def __init__(self, r, phase, axis, pieces, source, landing, sends=None, comes=None):
        self.r, self.phase, self.axis, self.pieces = r, phase, axis, pieces
        self.sends, self.comes = sends or always, comes or always
        self.size = lax.axis_size(axis)
        self.me = lax.axis_index(axis)
        side = math.isqrt(self.size)
        self.q = side if axis == "expert" and side * side == self.size else 1
        self.source, self.landing = source, landing

    def walk(self, high, low):
        return lax.rem(high, self.size // self.q) * self.q + lax.rem(low, self.q)

    def ahead(self, k):
        q = self.q
        return self.walk(self.me // q + k // q, self.me % q + k % q)

    def behind(self, k):
        q = self.q
        return self.walk(self.me // q + self.size // q - k // q, self.me % q + q - k % q)

    def back(self, k):
        q = self.q
        return self.walk(self.size // q - k // q, q - k % q)

    def copy(self, k, h):
        there = self.ahead(k)
        return pltpu.make_async_remote_copy(
            src_ref=self.source(there, h),
            dst_ref=self.landing(k, h),
            send_sem=self.r.send_sem.at[self.phase, k * self.pieces + h],
            recv_sem=self.r.recv_sem.at[self.phase, k * self.pieces + h],
            device_id={self.axis: there},
            device_id_type=MESH,
        )

    def start(self, k, h=0):
        self.sends(k, h, lambda: self.copy(k, h).start())

    def start_all(self, h=0):
        for k in range(1, self.size):
            self.start(k, h)

    def wait(self, k, h=0):
        self.comes(k, h, lambda: self.copy(k, h).wait_recv())

    def wait_all(self):
        for h in range(self.pieces):
            for k in range(1, self.size):
                self.wait(k, h)

    def drain(self):
        for h in range(self.pieces):
            for k in range(1, self.size):
                self.sends(k, h, lambda: self.copy(k, h).wait_send())


def relay_kernel(names, d, *refs):
    r = types.SimpleNamespace(**dict(zip(names, refs)))
    E, T, R, RG, RP, H, EP = d.E, d.T, d.R, d.RG, d.RP, d.H, d.EP
    WC, LAST = d.WC, d.LAST
    CAP, D, W, HW = d.CAP, d.D, d.W, d.HW
    heads = W // HEAD_DIM
    scale_factor = HEAD_DIM ** (-0.5)
    s, e, t = [lax.axis_index(name) for name in ("section", "expert", "tensor")]
    other = 1 - s
    at_first, at_second = s == 0, s == 1

    def owned(h, owner, body):
        if h == H - 1 and LAST < T:
            pl.when(owner < LAST)(body)
        else:
            body()

    def piece(h):
        return pl.ds(h * ROW_TILE, ROW_TILE)

    def piece_rows(h):
        count = LAST if h == H - 1 else T
        return pl.ds(h * T * ROW_TILE, count * ROW_TILE)

    def rows_of(owner, h):
        return pl.ds(pl.multiple_of((h * T + owner) * ROW_TILE, ROW_TILE), ROW_TILE)

    def z_ahead(k):
        return lax.rem(t + k, T)

    def z_behind(k):
        return lax.rem(t + T - k, T)

    def gather(phase, ref):
        return Swap(r, phase, "expert", 1, lambda there, h: ref.at[e], lambda k, h: ref.at[e])

    def gather_rows(phase, ref):
        return Swap(
            r, phase, "tensor", H,
            lambda there, h: ref.at[rows_of(t, h)],
            lambda k, h: ref.at[rows_of(t, h)],
            lambda k, h, body: owned(h, t, body),
            lambda k, h, body: owned(h, z_behind(k), body),
        )

    def scatter_rows(phase, source, landing):
        return Swap(
            r, phase, "tensor", H,
            lambda there, h: source.at[rows_of(there, h)],
            lambda k, h: landing.at[k - 1, piece(h)],
            lambda k, h, body: owned(h, z_ahead(k), body),
        )

    rs_attn = scatter_rows(RS_ATTN, r.p1, r.l1)
    ag_attn = gather_rows(AG_ATTN, r.t1)
    rs_moe = scatter_rows(RS_MOE, r.p2, r.l2)
    ag_moe = gather_rows(AG_MOE, r.t2)
    rs_grad = scatter_rows(RS_GRAD, r.p3, r.l3)
    ag_grad = gather_rows(AG_GRAD, r.t3)
    rs_proj = scatter_rows(RS_PROJ, r.p4, r.l4)
    ag_proj = gather_rows(AG_PROJ, r.t4)

    def routed(phase, source, landing):
        return Swap(
            r, phase, "expert", 1, lambda there, h: source.at[there], lambda k, h: landing.at[e]
        )

    dispatch = routed(DISPATCH, r.o1, r.b1)
    parts = routed(PARTS, r.o2, r.b2)
    grads = routed(GRADS, r.o3, r.b3)
    grad_parts = routed(GRAD_PARTS, r.o4, r.b4)
    all_normed = gather(ALL_NORMED, r.na)

    def weight_rows(owner):
        return pl.ds(pl.multiple_of(owner * WC, WC), WC)

    rs_weight = Swap(
        r, RS_WEIGHT, "expert", 1,
        lambda there, h: r.w_part.at[weight_rows(there)],
        lambda k, h: r.w_land.at[k - 1],
    )
    ag_weight = Swap(
        r, AG_WEIGHT, "expert", 1,
        lambda there, h: r.w_sum.at[weight_rows(e)],
        lambda k, h: r.w_sum.at[weight_rows(e)],
    )
    all_proj = gather(ALL_PROJ, r.gp)
    small_e = Swap(
        r, SMALL_E, "expert", 1, lambda there, h: r.small2, lambda k, h: r.small_e.at[k - 1]
    )
    small_t = Swap(
        r, SMALL_T, "tensor", 1, lambda there, h: r.small, lambda k, h: r.small_t.at[k - 1]
    )

    def cross_copy(source, k, h):
        return pltpu.make_async_remote_copy(
            src_ref=source.at[rows_of(t, h)],
            dst_ref=r.delta_in.at[rows_of(t, h)],
            send_sem=r.send_sem.at[CROSS, k * H + h],
            recv_sem=r.recv_sem.at[CROSS, k * H + h],
            device_id={"section": other, "tensor": z_ahead(k)},
            device_id_type=MESH,
        )

    def resid_copy(source):
        return pltpu.make_async_remote_copy(
            src_ref=source,
            dst_ref=r.resid_in,
            send_sem=r.send_sem.at[RESID, 0],
            recv_sem=r.recv_sem.at[RESID, 0],
            device_id={"section": other},
            device_id_type=MESH,
        )

    def load(k):
        source, target = (
            (r.expert_in, r.w_in), (r.expert_out, r.w_out),
            (r.inputs.at[:, 0, :], r.rows_in), (r.cotangent.at[:, 0, :], r.rows_in),
        )[k]
        return pltpu.make_async_copy(source, target, r.load_sem.at[k])

    def from_other_section():
        resid_copy(r.resid_in).wait_recv()
        for h in range(H):
            for k in range(T):
                owned(h, z_behind(k), lambda: cross_copy(r.delta_in, k, h).wait_recv())
        return r.resid_in[...] + r.delta_in[...].astype(F32)

    r.x[...] = jnp.zeros((RP, D), F32)
    r.g[...] = jnp.zeros((RP, D), F32)
    if RG < RP:
        for ref in (r.t1, r.t2, r.t3, r.t4, r.p4, r.delta_in):
            ref[RG:RP, :] = jnp.zeros((RP - RG, D), BF16)

    @pl.when(at_first)
    def _():
        load(2).start()

    @pl.when(at_second)
    def _():
        load(3).start()

    load(1).start()
    load(0).start()

    barrier = pltpu.get_barrier_semaphore()
    friends = [{"tensor": lax.rem(t + k, T)} for k in range(1, T)]
    friends += [{"expert": lax.rem(e + k, E)} for k in range(1, E)]
    friends += [{"section": other, "tensor": lax.rem(t + k, T)} for k in range(T)]
    for device in friends:
        pl.semaphore_signal(barrier, inc=1, device_id=device, device_id_type=MESH)

    def all_are_here():
        pl.semaphore_wait(barrier, len(friends))

    def gate_of(expert, rows=slice(None)):
        ids, gates = r.rt[rows, :], r.gt[rows, :]
        named = lax.convert_element_type(expert, F32)
        return jnp.sum(jnp.where(ids == named, gates, 0.0), axis=-1, keepdims=True)

    def routing():
        r.rt_t[...] = jnp.full((8, RP), -1.0, F32)
        r.gt_t[...] = jnp.zeros((8, RP), F32)
        r.rt_t[0:TOPK, 0:R] = r.routes[...].astype(F32)
        r.gt_t[0:TOPK, 0:R] = r.gate_weights[...]
        ids = r.rt_t[...]
        r.rt[...] = jnp.transpose(ids)
        r.gt[...] = jnp.transpose(r.gt_t[...])
        expert = iota((EP, RP), 0).astype(F32)
        named = jnp.where((ids[0:1] == expert) | (ids[1:2] == expert), 1.0, 0.0)
        later = jnp.where(iota((RP, RP), 0) < iota((RP, RP), 1), 1.0, 0.0)
        slot_t = jnp.where(named > 0.5, nn(named.astype(BF16), later.astype(BF16)), -1.0)
        slot = jnp.transpose(slot_t)
        wide = iota((RP, CAP), 1).astype(F32)
        tall = iota((CAP, RP), 0).astype(F32)
        for k in range(E):
            r.pick[k] = jnp.where(slot[:, k : k + 1] == wide, 1.0, 0.0).astype(BF16)
            r.place[k] = jnp.where(slot_t[k : k + 1, :] == tall, 1.0, 0.0).astype(BF16)

    def dispatch_grads():
        def outgoing(expert):
            weighted = (gate_of(expert) * r.g[...]).astype(BF16)
            return nn(r.place[expert], weighted).astype(BF16)

        def one(k, carry):
            there = grads.ahead(k)
            r.o3[there] = outgoing(there)
            grads.start(k)
            return carry

        lax.fori_loop(1, E, one, 0)
        r.b3[e] = outgoing(e)

    def each_block(swapped, body):
        body(e, 0)

        def one(k, carry):
            swapped.wait(k)
            body(swapped.behind(k), k)
            return carry

        lax.fori_loop(1, E, one, 0)

    def send_part(swapped, outgoing, landing, image, k, value):
        if isinstance(k, int):
            landing[image] = value
        else:
            outgoing[image] = value
            swapped.start(swapped.back(k))

    def raw_block(image):
        r.raw[image] = nt(r.b3[image], r.w_out[...])

    def backward_part(image, k):
        grad_pre = r.raw[image] * r.slope[image]
        r.in_bias[...] = r.in_bias[...] + jnp.sum(grad_pre, axis=0, keepdims=True)
        grad_pre_b = grad_pre.astype(BF16)
        r.gpb[image] = grad_pre_b
        value = nt(grad_pre_b, r.w_in[...]).astype(BF16)
        send_part(grad_parts, r.o4, r.b4, image, k, value)

    def forward_part(image, k):
        bias = jnp.where(t == 0, r.expert_out_bias[...], 0.0)
        value = (nn(r.act[image], r.w_out[...]) + bias).astype(BF16)
        send_part(parts, r.o2, r.b2, image, k, value)

    def expert_block(image):
        pre = nn(r.b1[image], r.w_in[...]) + r.expert_in_bias[...]
        square = pre * pre
        tangent = jnp.tanh(GELU_FACTOR * (pre + CUBIC_TERM * square * pre))
        half = 0.5 * (1.0 + tangent)
        r.act[image] = (pre * half).astype(BF16)
        r.slope[image] = half + 0.5 * pre * (1.0 - tangent * tangent) * GELU_FACTOR * (
            1.0 + 3.0 * CUBIC_TERM * square
        )

    def scatter_chunks(swapped, part, chunk_of):
        for h in range(H):
            rows = piece_rows(h)
            part[rows, :] = chunk_of(rows).astype(BF16)
            swapped.start_all(h)

    def collect(swapped, part, landing, h):
        total = part[rows_of(t, h), :].astype(F32)
        for k in range(1, T):
            swapped.wait(k, h)
            total = total + landing[k - 1, piece(h)].astype(F32)
        return total

    def each_owned(body):
        for h in range(H):
            owned(h, t, functools.partial(body, h))

    def cross(ref, h):
        for k in range(T):
            owned(h, t, lambda: cross_copy(ref, k, h).start())

    def combined(landed, gated, rows):
        total = None
        for k in range(E):
            term = nn(r.pick[k, rows, :], landed[k])
            if gated:
                term = gate_of(k, rows) * term
            total = term if total is None else total + term
        return total

    def finish_forward(crossing):
        parts.wait_all()
        scatter_chunks(rs_moe, r.p2, lambda rows: combined(r.b2, True, rows))

        def hand_on(h):
            r.t2[rows_of(t, h), :] = collect(rs_moe, r.p2, r.l2, h).astype(BF16)
            if crossing:
                cross(r.t2, h)

        each_owned(hand_on)
        for h in range(H):
            ag_moe.start_all(h)
        ag_moe.wait_all()
        out = r.hidden[...] + r.t2[...].astype(F32)
        r.section_out[...] = out[0:R]

    r.in_bias[...] = jnp.zeros((1, HW), F32)
    r.small[...] = jnp.zeros((8, D), F32)

    @pl.when(at_first)
    def _():
        load(2).wait()
        r.x[0:R, :] = r.rows_in[...]

    @pl.when(at_second)
    def _():
        routing()
        load(3).wait()
        all_are_here()
        r.g[0:R, :] = r.rows_in[...]
        dispatch_grads()
        load(1).wait()
        each_block(grads, lambda image, k: raw_block(image))
        r.x[...] = from_other_section()

    inside = iota((RP, 1), 0) < R
    scale0, scale1 = r.norm_scale[0:1, :], r.norm_scale[1:2, :]
    shift0, shift1 = r.norm_shift[0:1, :], r.norm_shift[1:2, :]
    normed_first, _ = standardize(r.x[...])
    normed_a = jnp.where(inside, normed_first * scale0 + shift0, 0.0).astype(BF16)
    r.na[e] = normed_a[0:RG]
    query = nt(normed_a, r.proj_weight[0]) + r.proj_bias[0:1, :]
    r.qkv[0] = jnp.where(inside, query, 0.0).astype(BF16)
    r.qkv[1] = nt(normed_a, r.proj_weight[1]).astype(BF16)
    value = nt(normed_a, r.proj_weight[2]) + r.proj_bias[1:2, :]
    r.qkv[2] = jnp.where(inside, value, 0.0).astype(BF16)
    real_key = iota((RP, RP), 1) < R
    mixed = []
    for h in range(heads):
        cols = slice(h * HEAD_DIM, (h + 1) * HEAD_DIM)
        scores = nt(r.qkv[0][:, cols], r.qkv[1][:, cols]) * scale_factor
        powers = jnp.where(real_key, jnp.exp(scores), 0.0)
        probs = powers / jnp.sum(powers, axis=-1, keepdims=True)
        r.probs[h] = probs
        mixed.append(nn(probs.astype(BF16), r.qkv[2][:, cols]))
    r.mixed[...] = jnp.concatenate(mixed, axis=1).astype(BF16)

    @pl.when(at_first)
    def _():
        all_are_here()

    scatter_chunks(
        rs_attn, r.p1, lambda rows: nn(r.mixed[rows, :], r.attn_weight[...])
    )
    all_normed.start_all()

    @pl.when(at_first)
    def _():
        routing()

    def hand_on_mixed(h):
        r.t1[rows_of(t, h), :] = collect(rs_attn, r.p1, r.l1, h).astype(BF16)
        ag_attn.start_all(h)

    each_owned(hand_on_mixed)
    ag_attn.wait_all()
    hidden = r.x[...] + (r.t1[...].astype(F32) + r.attn_bias[...])
    r.hidden[...] = hidden

    @pl.when(at_first)
    def _():
        resid_copy(r.hidden).start()

    normed_second, inv_second = standardize(hidden)
    r.h2[...] = normed_second
    r.r2[...] = inv_second
    r.nb[...] = (normed_second * scale1 + shift1).astype(BF16)

    def dispatch_one(k, carry):
        there = dispatch.ahead(k)
        r.o1[there] = nn(r.place[there], r.nb[...]).astype(BF16)
        dispatch.start(k)
        return carry

    lax.fori_loop(1, E, dispatch_one, 0)
    r.b1[e] = nn(r.place[e], r.nb[...]).astype(BF16)

    @pl.when(at_first)
    def _():
        load(0).wait()
        load(1).wait()

        def both(image, k):
            expert_block(image)
            forward_part(image, k)

        each_block(dispatch, both)
        finish_forward(True)
        r.g[...] = from_other_section()
        dispatch_grads()

        def back(image, k):
            raw_block(image)
            backward_part(image, k)

        each_block(grads, back)

    @pl.when(at_second)
    def _():
        load(0).wait()

        def both(image, k):
            expert_block(image)
            backward_part(image, k)

        each_block(dispatch, both)
        forward_part(e, 0)

        def one(k, carry):
            forward_part(parts.behind(k), k)
            return carry

        lax.fori_loop(1, E, one, 0)

    slots = E * CAP
    r.grad_expert_out[...] = tn(
        r.act[...].reshape(slots, HW), r.b3[...].reshape(slots, D)
    )
    r.grad_expert_out_bias[...] = jnp.sum(
        r.b3[...].reshape(slots, D).astype(F32), axis=0, keepdims=True
    )
    grad_parts.wait_all()
    scatter_chunks(rs_grad, r.p3, lambda rows: combined(r.b4, False, rows))
    r.grad_expert_in[...] = tn(
        r.b1[...].reshape(slots, D), r.gpb[...].reshape(slots, HW)
    )
    r.grad_expert_in_bias[...] = r.in_bias[...]
    r.summed[...] = jnp.zeros((H * ROW_TILE, D), F32)

    def hand_on_grad(h):
        rows = rows_of(t, h)
        total = collect(rs_grad, r.p3, r.l3, h)
        delta = norm_back(total, r.h2[rows, :], r.r2[rows, :], scale1)
        r.t3[rows, :] = delta.astype(BF16)
        ag_grad.start_all(h)
        r.summed[piece(h), :] = total

    each_owned(hand_on_grad)

    def add_small(row, value):
        r.small[row : row + 1, :] = r.small[row : row + 1, :] + jnp.sum(value, axis=0, keepdims=True)

    for h in range(H):
        add_small(1, r.summed[piece(h), :] * r.h2[rows_of(t, h), :])
    add_small(3, r.summed[...])
    ag_grad.wait_all()
    grad_hidden = r.g[...] + r.t3[...].astype(F32)
    r.g[...] = grad_hidden

    @pl.when(at_second)
    def _():
        resid_copy(r.g).start()

    for h in range(H):
        add_small(4, r.g[rows_of(t, h), :])
    grad_hidden_b = grad_hidden.astype(BF16)
    grad_mixed = nt(grad_hidden_b, r.attn_weight[...]).astype(BF16)
    r.w_part[...] = jnp.zeros((E * WC, D), BF16)
    r.w_part[0:W, :] = tn(r.mixed[...], grad_hidden_b).astype(BF16)
    rs_weight.start_all()
    found = [[], [], []]
    for h in range(heads):
        cols = slice(h * HEAD_DIM, (h + 1) * HEAD_DIM)
        query, key, value = r.qkv[0][:, cols], r.qkv[1][:, cols], r.qkv[2][:, cols]
        grad_mixed_h = grad_mixed[:, cols]
        probs = r.probs[h]
        grad_values = tn(probs.astype(BF16), grad_mixed_h)
        grad_probs = nt(grad_mixed_h, value)
        row_delta = jnp.sum(
            grad_mixed_h.astype(F32) * r.mixed[...][:, cols].astype(F32), axis=-1, keepdims=True
        )
        grad_scores = (probs * (grad_probs - row_delta) * scale_factor).astype(BF16)
        found[0].append(nn(grad_scores, key))
        found[1].append(tn(grad_scores, query))
        found[2].append(grad_values)
    for j in (0, 2):
        row = 5 + j // 2
        r.small[row : row + 1, 0:W] = jnp.concatenate(
            [jnp.sum(columns, axis=0, keepdims=True) for columns in found[j]], axis=1
        )
    flat = jnp.concatenate(found[0] + found[1] + found[2], axis=1).astype(BF16)
    r.grad_flat[...] = flat
    r.gp[e] = flat[0:RG]

    def proj_chunk(rows):
        return nn(r.grad_flat[rows, :], r.proj_weight[...].reshape(3 * W, D))

    scatter_chunks(rs_proj, r.p4, proj_chunk)
    all_proj.start_all()
    normed_first, inv_first = standardize(r.x[...])
    partial_rows = r.p4[...].astype(F32)
    add_small(0, partial_rows * normed_first)
    add_small(2, partial_rows)
    small_t.start_all()
    r.h1[...] = normed_first
    r.r1[...] = inv_first

    def hand_on_proj(h):
        rows = rows_of(t, h)
        total = collect(rs_proj, r.p4, r.l4, h)
        r.t4[rows, :] = norm_back(total, r.h1[rows, :], r.r1[rows, :], scale0).astype(BF16)

        @pl.when(at_second)
        def _():
            cross(r.t4, h)

        @pl.when(at_first)
        def _():
            ag_proj.start_all(h)

    each_owned(hand_on_proj)

    @pl.when(at_second)
    def _():
        for h in range(H):
            ag_proj.start_all(h)

    small_t.wait_all()
    total = r.small[...]
    summed = total
    for k in range(1, T):
        summed = summed + r.small_t[k - 1]
    r.small2[...] = jnp.where(iota((8, D), 0) < 5, summed, total)
    small_e.start_all()
    rs_weight.wait_all()
    total = r.w_part[weight_rows(e), :].astype(F32)
    for k in range(1, E):
        total = total + r.w_land[k - 1].astype(F32)
    r.w_sum[weight_rows(e), :] = total.astype(BF16)
    ag_weight.start_all()

    @pl.when(at_second)
    def _():
        finish_forward(False)

    all_normed.wait_all()
    all_proj.wait_all()
    tokens = E * RG
    grad_proj = tn(r.gp[...].reshape(tokens, 3 * W), r.na[...].reshape(tokens, D))
    r.grad_proj[...] = grad_proj.reshape(3, W, D)
    small_e.wait_all()
    total = r.small2[...]
    for k in range(1, E):
        total = total + r.small_e[k - 1]
    r.grad_norm_scale[...] = total[0:2]
    r.grad_norm_shift[...] = total[2:4]
    r.grad_attn_bias[...] = total[4:5]
    r.grad_proj_bias[...] = total[5:7, 0:W]
    ag_weight.wait_all()
    r.grad_attn_weight[...] = r.w_sum[0:W, :].astype(F32)
    ag_proj.wait_all()
    grad_in = r.g[...] + r.t4[...].astype(F32)
    r.section_in_grad[...] = grad_in[0:R]

    for swapped in (
        rs_attn, ag_attn, rs_moe, ag_moe, rs_grad, ag_grad, rs_proj, ag_proj,
        dispatch, parts, grads, grad_parts,
        all_normed, all_proj, rs_weight, ag_weight, small_e, small_t,
    ):
        swapped.drain()
    resid_copy(r.resid_in).wait_send()
    for h in range(H):
        for k in range(T):
            owned(h, t, lambda: cross_copy(r.t4, k, h).wait_send())


def write_kernel(count, *refs):
    sems = refs[-1]
    copies = []
    for k in range(count):
        source, target = refs[k], refs[count + k]
        if len(target.shape) > len(source.shape):
            target = target.at[:, 0, :]
        copies.append(pltpu.make_async_copy(source, target, sems.at[k]))
    for copy in copies:
        copy.start()
    for copy in copies:
        copy.wait()


def slot_count(row_count, experts):
    return max(2, (3 * TOPK * row_count + 2 * experts - 1) // (2 * experts))


def round_up(value, unit):
    return -(-value // unit) * unit


def on_device(
    inputs,
    cotangent,
    norm_scale,
    norm_shift,
    proj_weight,
    proj_bias,
    attn_weight,
    attn_bias,
    expert_in,
    expert_in_bias,
    expert_out,
    expert_out_bias,
    routes,
    gate_weights,
):
    E, T = lax.axis_size("expert"), lax.axis_size("tensor")
    R, D = inputs.shape[1:]
    W, HW = proj_weight.shape[3], expert_in.shape[3]
    tiles = -(-R // ROW_TILE)
    H = -(-tiles // T)
    LAST = tiles - (H - 1) * T
    RP = H * T * ROW_TILE
    CAP = round_up(slot_count(R, E), ROW_TILE)
    RG = round_up(R, ROW_TILE)
    EP = round_up(E, ROW_TILE)
    WC = round_up(-(-W // E), ROW_TILE)
    d = types.SimpleNamespace(
        E=E, T=T, R=R, RG=RG, RP=RP, LAST=LAST, CAP=CAP, D=D, W=W, HW=HW, H=H, EP=EP, WC=WC
    )
    heads = W // HEAD_DIM

    operands = dict(
        inputs=jnp.transpose(inputs, (1, 0, 2)),
        cotangent=jnp.transpose(cotangent, (1, 0, 2)),
        norm_scale=norm_scale[0],
        norm_shift=norm_shift[0],
        proj_weight=jnp.transpose(proj_weight[0], (1, 2, 0)),
        proj_bias=proj_bias[0],
        attn_weight=attn_weight[0],
        attn_bias=attn_bias,
        expert_in=expert_in[0, 0],
        expert_in_bias=expert_in_bias[0],
        expert_out=expert_out[0, 0],
        expert_out_bias=expert_out_bias[0],
        routes=routes[0, 0].T,
        gate_weights=gate_weights[0, 0].T,
    )
    results = dict(
        section_out=(R, D),
        section_in_grad=(R, D),
        grad_norm_scale=(2, D),
        grad_norm_shift=(2, D),
        grad_proj_bias=(2, W),
        grad_attn_bias=(1, D),
        grad_proj=(3, W, D),
        grad_attn_weight=(W, D),
        grad_expert_in=(D, HW),
        grad_expert_in_bias=(1, HW),
        grad_expert_out=(HW, D),
        grad_expert_out_bias=(1, D),
    )
    scratch = dict(
        x=((RP, D), F32),
        rows_in=((R, D), F32),
        g=((RP, D), F32),
        hidden=((RP, D), F32),
        h2=((RP, D), F32),
        r2=((RP, 1), F32),
        nb=((RP, D), BF16),
        resid_in=((RP, D), F32),
        delta_in=((RP, D), BF16),
        qkv=((3, RP, W), BF16),
        probs=((heads, RP, RP), F32),
        na=((E, RG, D), BF16),
        mixed=((RP, W), BF16),
        gp=((E, RG, 3 * W), BF16),
        grad_flat=((RP, 3 * W), BF16),
        h1=((RP, D), F32),
        r1=((RP, 1), F32),
        summed=((H * ROW_TILE, D), F32),
        w_part=((E * WC, D), BF16),
        w_land=((E - 1, WC, D), BF16),
        w_sum=((E * WC, D), BF16),
        rt=((RP, 8), F32),
        gt=((RP, 8), F32),
        rt_t=((8, RP), F32),
        gt_t=((8, RP), F32),
        w_in=((D, HW), BF16),
        w_out=((HW, D), BF16),
        pick=((E, RP, CAP), BF16),
        place=((E, CAP, RP), BF16),
        act=((E, CAP, HW), BF16),
        gpb=((E, CAP, HW), BF16),
        slope=((E, CAP, HW), F32),
        raw=((E, CAP, HW), F32),
        in_bias=((1, HW), F32),
        small=((8, D), F32),
        small2=((8, D), F32),
        small_e=((E - 1, 8, D), F32),
        small_t=((T - 1, 8, D), F32),
    )
    for k in range(1, 5):
        scratch[f"p{k}"] = ((RP, D), BF16)
        scratch[f"l{k}"] = ((T - 1, H * ROW_TILE, D), BF16)
        scratch[f"t{k}"] = ((RP, D), BF16)
        scratch[f"o{k}"] = ((E, CAP, D), BF16)
        scratch[f"b{k}"] = ((E, CAP, D), BF16)
    sems = pltpu.SemaphoreType.DMA((PHASES, max(E, T * H)))
    names = list(operands) + list(results) + list(scratch) + ["load_sem", "send_sem", "recv_sem"]
    in_vmem, in_place = pl.BlockSpec(memory_space=pltpu.VMEM), pl.BlockSpec(memory_space=pl.ANY)
    loaded = ("inputs", "cotangent", "expert_in", "expert_out")
    found = pl.pallas_call(
        functools.partial(relay_kernel, names, d),
        out_shape=[pltpu.VMEM(shape, F32) for shape in results.values()],
        in_specs=[in_place if name in loaded else in_vmem for name in operands],
        out_specs=[in_vmem] * len(results),
        scratch_shapes=[pltpu.VMEM(shape, dtype) for shape, dtype in scratch.values()]
        + [pltpu.SemaphoreType.DMA((len(loaded),)), sems, sems],
        compiler_params=pltpu.CompilerParams(
            collective_id=0, has_side_effects=True, vmem_limit_bytes=52 * 2**20
        ),
        name="relay",
    )(*operands.values())
    shapes = [
        (R, 1, D) if name.startswith("section") else shape for name, shape in results.items()
    ]
    written = pl.pallas_call(
        functools.partial(write_kernel, len(results)),
        out_shape=[jax.ShapeDtypeStruct(shape, F32) for shape in shapes],
        in_specs=[in_vmem] * len(results),
        out_specs=[in_place] * len(results),
        scratch_shapes=[pltpu.SemaphoreType.DMA((len(results),))],
        compiler_params=pltpu.CompilerParams(vmem_limit_bytes=2**20),
        name="write",
    )(*[pltpu.with_memory_space_constraint(array, pltpu.VMEM) for array in found])
    found = types.SimpleNamespace(**dict(zip(results, written)))
    return (
        jnp.transpose(found.section_out, (1, 0, 2))[None],
        jnp.transpose(found.section_in_grad, (1, 0, 2))[None],
        found.grad_norm_scale[None],
        found.grad_norm_shift[None],
        jnp.transpose(found.grad_proj, (2, 0, 1))[None],
        found.grad_proj_bias[None],
        found.grad_attn_weight[None],
        found.grad_attn_bias,
        found.grad_expert_in[None, None],
        found.grad_expert_in_bias[None],
        found.grad_expert_out[None, None],
        found.grad_expert_out_bias[None],
    )


def solution(mesh):
    in_specs = (
        P(None, "expert", None),
        P(None, "expert", None),
        P("section", None, None),
        P("section", None, None),
        P("section", None, None, "tensor"),
        P("section", None, "tensor"),
        P("section", "tensor", None),
        P("section", None),
        P("section", "expert", None, "tensor"),
        P("section", "expert", "tensor"),
        P("section", "expert", "tensor", None),
        P("section", "expert", None),
        P("section", None, "expert", None),
        P("section", None, "expert", None),
    )
    out_specs = (
        P("section", None, "expert", None),
        P("section", None, "expert", None),
        P("section", None, None),
        P("section", None, None),
        P("section", None, None, "tensor"),
        P("section", None, "tensor"),
        P("section", "tensor", None),
        P("section", None),
        P("section", "expert", None, "tensor"),
        P("section", "expert", "tensor"),
        P("section", "expert", "tensor", None),
        P("section", "expert", None),
    )
    return jax.shard_map(
        on_device, mesh=mesh, in_specs=in_specs, out_specs=out_specs, check_vma=False
    )
```

```python
import functools
import math
import types

import jax
import jax.numpy as jnp
from jax import lax
from jax.experimental import pallas as pl
from jax.experimental.pallas import tpu as pltpu
from jax.sharding import PartitionSpec as P

HEAD_DIM = 64
TOPK = 2

NORM_EPSILON = 1e-06
GELU_FACTOR = 0.7978845608028654
CUBIC_TERM = 0.044715

MESH = pl.DeviceIdType.MESH
ROW_TILE = 16
BF16 = jnp.bfloat16
F32 = jnp.float32

(
    RS_ATTN,
    AG_ATTN,
    DISPATCH,
    PARTS,
    RS_MOE,
    AG_MOE,
    CROSS,
    RESID,
    GRADS,
    GRAD_PARTS,
    RS_GRAD,
    AG_GRAD,
    RS_PROJ,
    AG_PROJ,
    ALL_NORMED,
    RS_WEIGHT,
    AG_WEIGHT,
    ALL_PROJ,
    SMALL_E,
    SMALL_T,
    PHASES,
) = range(21)


def nn(left, right):
    return jnp.dot(left, right, preferred_element_type=F32)


def nt(left, right):
    return lax.dot_general(left, right, (((1,), (1,)), ((), ())), preferred_element_type=F32)


def tn(left, right):
    return lax.dot_general(left, right, (((0,), (0,)), ((), ())), preferred_element_type=F32)


def standardize(values):
    average = jnp.mean(values, axis=-1, keepdims=True)
    centred = values - average
    variance = jnp.mean(centred * centred, axis=-1, keepdims=True)
    inv_std = lax.rsqrt(variance + NORM_EPSILON)
    return centred * inv_std, inv_std


def norm_back(grad_normed, normed, inv_std, scale_row):
    scaled = grad_normed * scale_row
    return (
        scaled
        - jnp.mean(scaled, axis=-1, keepdims=True)
        - normed * jnp.mean(scaled * normed, axis=-1, keepdims=True)
    ) * inv_std


def iota(shape, axis):
    return lax.broadcasted_iota(jnp.int32, shape, axis)


def always(k, h, body):
    body()


class Swap:
    def __init__(self, r, phase, axis, pieces, source, landing, sends=None, comes=None, blocks=False):
        self.r, self.phase, self.axis, self.pieces = r, phase, axis, pieces
        self.sends, self.comes = sends or always, comes or always
        self.blocks = blocks
        self.size = lax.axis_size(axis)
        self.me = lax.axis_index(axis)
        side = math.isqrt(self.size)
        self.q = side if axis == "expert" and side * side == self.size else 1
        self.source, self.landing = source, landing

    def walk(self, high, low):
        return lax.rem(high, self.size // self.q) * self.q + lax.rem(low, self.q)

    def ahead(self, k):
        q = self.q
        return self.walk(self.me // q + k // q, self.me % q + k % q)

    def behind(self, k):
        q = self.q
        return self.walk(self.me // q + self.size // q - k // q, self.me % q + q - k % q)

    def back(self, k):
        q = self.q
        return self.walk(self.size // q - k // q, q - k % q)

    def copy(self, k, h):
        there = self.ahead(k)
        return pltpu.make_async_remote_copy(
            src_ref=self.source(there, h, k) if self.blocks else self.source(there, h),
            dst_ref=self.landing(k, h),
            send_sem=self.r.send_sem.at[self.phase, k * self.pieces + h],
            recv_sem=self.r.recv_sem.at[self.phase, k * self.pieces + h],
            device_id={self.axis: there},
            device_id_type=MESH,
        )

    def start(self, k, h=0):
        self.sends(k, h, lambda: self.copy(k, h).start())

    def start_all(self, h=0):
        for k in range(1, self.size):
            self.start(k, h)

    def wait(self, k, h=0):
        self.comes(k, h, lambda: self.copy(k, h).wait_recv())

    def pieces_of(self, k):
        return self.pieces if not self.blocks or k == self.size - 1 else 1

    def wait_all(self):
        for k in range(1, self.size):
            for h in range(self.pieces_of(k)):
                self.wait(k, h)

    def drain(self):
        for k in range(1, self.size):
            for h in range(self.pieces_of(k)):
                self.sends(k, h, lambda: self.copy(k, h).wait_send())


def relay_kernel(names, d, *refs):
    r = types.SimpleNamespace(**dict(zip(names, refs)))
    E, T, R, RG, RP, H, EP = d.E, d.T, d.R, d.RG, d.RP, d.H, d.EP
    WC, LAST = d.WC, d.LAST
    PARTED = 2 if E == 4 and d.CAP % (2 * ROW_TILE) == 0 else 1
    WHOLE = E - 1 if PARTED > 1 else E
    CAP, D, W, HW = d.CAP, d.D, d.W, d.HW
    heads = W // HEAD_DIM
    scale_factor = HEAD_DIM ** (-0.5)
    s, e, t = [lax.axis_index(name) for name in ("section", "expert", "tensor")]
    other = 1 - s
    at_first, at_second = s == 0, s == 1

    def owned(h, owner, body):
        if h == H - 1 and LAST < T:
            pl.when(owner < LAST)(body)
        else:
            body()

    def piece(h):
        return pl.ds(h * ROW_TILE, ROW_TILE)

    def piece_rows(h):
        count = LAST if h == H - 1 else T
        return pl.ds(h * T * ROW_TILE, count * ROW_TILE)

    def rows_of(owner, h):
        return pl.ds(pl.multiple_of((h * T + owner) * ROW_TILE, ROW_TILE), ROW_TILE)

    def z_ahead(k):
        return lax.rem(t + k, T)

    def z_behind(k):
        return lax.rem(t + T - k, T)

    def gather(phase, ref):
        return Swap(r, phase, "expert", 1, lambda there, h: ref.at[e], lambda k, h: ref.at[e])

    def gather_rows(phase, ref):
        return Swap(
            r, phase, "tensor", H,
            lambda there, h: ref.at[rows_of(t, h)],
            lambda k, h: ref.at[rows_of(t, h)],
            lambda k, h, body: owned(h, t, body),
            lambda k, h, body: owned(h, z_behind(k), body),
        )

    def scatter_rows(phase, source, landing):
        return Swap(
            r, phase, "tensor", H,
            lambda there, h: source.at[rows_of(there, h)],
            lambda k, h: landing.at[k - 1, piece(h)],
            lambda k, h, body: owned(h, z_ahead(k), body),
        )

    rs_attn = scatter_rows(RS_ATTN, r.p1, r.l1)
    ag_attn = gather_rows(AG_ATTN, r.t1)
    rs_moe = scatter_rows(RS_MOE, r.p2, r.l2)
    ag_moe = gather_rows(AG_MOE, r.t2)
    rs_grad = scatter_rows(RS_GRAD, r.p3, r.l3)
    ag_grad = gather_rows(AG_GRAD, r.t3)
    rs_proj = scatter_rows(RS_PROJ, r.p4, r.l4)
    ag_proj = gather_rows(AG_PROJ, r.t4)

    def is_last(k):
        return PARTED > 1 and isinstance(k, int) and k == E - 1

    def half(h):
        return pl.ds(h * (CAP // PARTED), CAP // PARTED)

    def routed(phase, source, landing):
        def part(ref, k, block, h):
            return ref.at[block, half(h)] if is_last(k) else ref.at[block]

        return Swap(
            r, phase, "expert", PARTED,
            lambda there, h, k: part(source, k, there, h),
            lambda k, h: part(landing, k, e, h),
            blocks=True,
        )

    dispatch = routed(DISPATCH, r.o1, r.b1)
    parts = routed(PARTS, r.o2, r.b2)
    grads = routed(GRADS, r.o3, r.b3)
    grad_parts = routed(GRAD_PARTS, r.o4, r.b4)
    all_normed = gather(ALL_NORMED, r.na)

    def weight_rows(owner):
        return pl.ds(pl.multiple_of(owner * WC, WC), WC)

    rs_weight = Swap(
        r, RS_WEIGHT, "expert", 1,
        lambda there, h: r.w_part.at[weight_rows(there)],
        lambda k, h: r.w_land.at[k - 1],
    )
    ag_weight = Swap(
        r, AG_WEIGHT, "expert", 1,
        lambda there, h: r.w_sum.at[weight_rows(e)],
        lambda k, h: r.w_sum.at[weight_rows(e)],
    )
    all_proj = gather(ALL_PROJ, r.gp)
    small_e = Swap(
        r, SMALL_E, "expert", 1, lambda there, h: r.small2, lambda k, h: r.small_e.at[k - 1]
    )
    small_t = Swap(
        r, SMALL_T, "tensor", 1, lambda there, h: r.small, lambda k, h: r.small_t.at[k - 1]
    )

    def cross_copy(source, k, h):
        return pltpu.make_async_remote_copy(
            src_ref=source.at[rows_of(t, h)],
            dst_ref=r.delta_in.at[rows_of(t, h)],
            send_sem=r.send_sem.at[CROSS, k * H + h],
            recv_sem=r.recv_sem.at[CROSS, k * H + h],
            device_id={"section": other, "tensor": z_ahead(k)},
            device_id_type=MESH,
        )

    def resid_copy(source):
        return pltpu.make_async_remote_copy(
            src_ref=source,
            dst_ref=r.resid_in,
            send_sem=r.send_sem.at[RESID, 0],
            recv_sem=r.recv_sem.at[RESID, 0],
            device_id={"section": other},
            device_id_type=MESH,
        )

    def load(k):
        source, target = (
            (r.expert_in, r.w_in), (r.expert_out, r.w_out),
            (r.inputs.at[:, 0, :], r.rows_in), (r.cotangent.at[:, 0, :], r.rows_in),
        )[k]
        return pltpu.make_async_copy(source, target, r.load_sem.at[k])

    def from_other_section():
        resid_copy(r.resid_in).wait_recv()
        for h in range(H):
            for k in range(T):
                owned(h, z_behind(k), lambda: cross_copy(r.delta_in, k, h).wait_recv())
        return r.resid_in[...] + r.delta_in[...].astype(F32)

    r.x[...] = jnp.zeros((RP, D), F32)
    r.g[...] = jnp.zeros((RP, D), F32)
    if RG < RP:
        for ref in (r.t1, r.t2, r.t3, r.t4, r.p4, r.delta_in):
            ref[RG:RP, :] = jnp.zeros((RP - RG, D), BF16)

    @pl.when(at_first)
    def _():
        load(2).start()

    @pl.when(at_second)
    def _():
        load(3).start()

    load(1).start()
    load(0).start()

    barrier = pltpu.get_barrier_semaphore()
    friends = [{"tensor": lax.rem(t + k, T)} for k in range(1, T)]
    friends += [{"expert": lax.rem(e + k, E)} for k in range(1, E)]
    friends += [{"section": other, "tensor": lax.rem(t + k, T)} for k in range(T)]
    for device in friends:
        pl.semaphore_signal(barrier, inc=1, device_id=device, device_id_type=MESH)

    def all_are_here():
        pl.semaphore_wait(barrier, len(friends))

    def gate_of(expert, rows=slice(None)):
        ids, gates = r.rt[rows, :], r.gt[rows, :]
        named = lax.convert_element_type(expert, F32)
        return jnp.sum(jnp.where(ids == named, gates, 0.0), axis=-1, keepdims=True)

    def routing():
        r.rt_t[...] = jnp.full((8, RP), -1.0, F32)
        r.gt_t[...] = jnp.zeros((8, RP), F32)
        r.rt_t[0:TOPK, 0:R] = r.routes[...].astype(F32)
        r.gt_t[0:TOPK, 0:R] = r.gate_weights[...]
        ids = r.rt_t[...]
        r.rt[...] = jnp.transpose(ids)
        r.gt[...] = jnp.transpose(r.gt_t[...])
        expert = iota((EP, RP), 0).astype(F32)
        named = jnp.where((ids[0:1] == expert) | (ids[1:2] == expert), 1.0, 0.0)
        later = jnp.where(iota((RP, RP), 0) < iota((RP, RP), 1), 1.0, 0.0)
        slot_t = jnp.where(named > 0.5, nn(named.astype(BF16), later.astype(BF16)), -1.0)
        slot = jnp.transpose(slot_t)
        wide = iota((RP, CAP), 1).astype(F32)
        tall = iota((CAP, RP), 0).astype(F32)
        for k in range(E):
            r.pick[k] = jnp.where(slot[:, k : k + 1] == wide, 1.0, 0.0).astype(BF16)
            r.place[k] = jnp.where(slot_t[k : k + 1, :] == tall, 1.0, 0.0).astype(BF16)

    def dispatch_grads():
        def outgoing(expert):
            weighted = (gate_of(expert) * r.g[...]).astype(BF16)
            return nn(r.place[expert], weighted).astype(BF16)

        def one(k, carry):
            there = grads.ahead(k)
            r.o3[there] = outgoing(there)
            grads.start(k)
            return carry

        lax.fori_loop(1, WHOLE, one, 0)
        if PARTED > 1:
            r.o3[grads.ahead(E - 1)] = outgoing(grads.ahead(E - 1))
            for h in range(PARTED):
                grads.start(E - 1, h)
        r.b3[e] = outgoing(e)

    def each_block(swapped, body):
        body(e, 0, slice(None))

        def one(k, carry):
            if swapped is not None:
                swapped.wait(k)
            body(dispatch.behind(k), k, slice(None))
            return carry

        lax.fori_loop(1, WHOLE, one, 0)
        if PARTED > 1:
            for h in range(PARTED):
                if swapped is not None:
                    swapped.wait(E - 1, h)
                body(dispatch.behind(E - 1), (E - 1, h), half(h))

    def send_part(swapped, outgoing, landing, image, k, rows, value):
        if isinstance(k, int):
            landing[image] = value
            return
        outgoing[image, rows, :] = value
        if isinstance(k, tuple):
            swapped.start(*k)
        else:
            swapped.start(swapped.back(k))

    def raw_block(image, rows):
        r.raw[image, rows, :] = nt(r.b3[image, rows, :], r.w_out[...])

    def backward_part(image, k, rows):
        grad_pre = r.raw[image, rows, :] * r.slope[image, rows, :]
        r.in_bias[...] = r.in_bias[...] + jnp.sum(grad_pre, axis=0, keepdims=True)
        grad_pre_b = grad_pre.astype(BF16)
        r.gpb[image, rows, :] = grad_pre_b
        value = nt(grad_pre_b, r.w_in[...]).astype(BF16)
        send_part(grad_parts, r.o4, r.b4, image, k, rows, value)

    def forward_part(image, k, rows):
        bias = jnp.where(t == 0, r.expert_out_bias[...], 0.0)
        value = (nn(r.act[image, rows, :], r.w_out[...]) + bias).astype(BF16)
        send_part(parts, r.o2, r.b2, image, k, rows, value)

    def expert_block(image, rows):
        pre = nn(r.b1[image, rows, :], r.w_in[...]) + r.expert_in_bias[...]
        square = pre * pre
        tangent = jnp.tanh(GELU_FACTOR * (pre + CUBIC_TERM * square * pre))
        rise = 0.5 * (1.0 + tangent)
        r.act[image, rows, :] = (pre * rise).astype(BF16)
        r.slope[image, rows, :] = rise + 0.5 * pre * (1.0 - tangent * tangent) * GELU_FACTOR * (
            1.0 + 3.0 * CUBIC_TERM * square
        )

    def scatter_chunks(swapped, part, chunk_of):
        for h in range(H):
            rows = piece_rows(h)
            part[rows, :] = chunk_of(rows).astype(BF16)
            swapped.start_all(h)

    def collect(swapped, part, landing, h):
        total = part[rows_of(t, h), :].astype(F32)
        for k in range(1, T):
            swapped.wait(k, h)
            total = total + landing[k - 1, piece(h)].astype(F32)
        return total

    def each_owned(body):
        for h in range(H):
            owned(h, t, functools.partial(body, h))

    def cross(ref, h):
        for k in range(T):
            owned(h, t, lambda: cross_copy(ref, k, h).start())

    def combined(landed, gated, rows):
        total = None
        for k in range(E):
            term = nn(r.pick[k, rows, :], landed[k])
            if gated:
                term = gate_of(k, rows) * term
            total = term if total is None else total + term
        return total

    def finish_forward(crossing):
        parts.wait_all()
        scatter_chunks(rs_moe, r.p2, lambda rows: combined(r.b2, True, rows))

        def hand_on(h):
            r.t2[rows_of(t, h), :] = collect(rs_moe, r.p2, r.l2, h).astype(BF16)
            if crossing:
                cross(r.t2, h)

        each_owned(hand_on)
        for h in range(H):
            ag_moe.start_all(h)
        ag_moe.wait_all()
        out = r.hidden[...] + r.t2[...].astype(F32)
        r.section_out[...] = out[0:R]

    r.in_bias[...] = jnp.zeros((1, HW), F32)
    r.small[...] = jnp.zeros((8, D), F32)

    @pl.when(at_first)
    def _():
        load(2).wait()
        r.x[0:R, :] = r.rows_in[...]

    @pl.when(at_second)
    def _():
        routing()
        load(3).wait()
        all_are_here()
        r.g[0:R, :] = r.rows_in[...]
        dispatch_grads()
        load(1).wait()
        each_block(grads, lambda image, k, rows: raw_block(image, rows))
        r.x[...] = from_other_section()

    inside = iota((RP, 1), 0) < R
    scale0, scale1 = r.norm_scale[0:1, :], r.norm_scale[1:2, :]
    shift0, shift1 = r.norm_shift[0:1, :], r.norm_shift[1:2, :]
    normed_first, _ = standardize(r.x[...])
    normed_a = jnp.where(inside, normed_first * scale0 + shift0, 0.0).astype(BF16)
    r.na[e] = normed_a[0:RG]
    query = nt(normed_a, r.proj_weight[0]) + r.proj_bias[0:1, :]
    r.qkv[0] = jnp.where(inside, query, 0.0).astype(BF16)
    r.qkv[1] = nt(normed_a, r.proj_weight[1]).astype(BF16)
    value = nt(normed_a, r.proj_weight[2]) + r.proj_bias[1:2, :]
    r.qkv[2] = jnp.where(inside, value, 0.0).astype(BF16)
    real_key = iota((RP, RP), 1) < R
    mixed = []
    for h in range(heads):
        cols = slice(h * HEAD_DIM, (h + 1) * HEAD_DIM)
        scores = nt(r.qkv[0][:, cols], r.qkv[1][:, cols]) * scale_factor
        powers = jnp.where(real_key, jnp.exp(scores), 0.0)
        probs = powers / jnp.sum(powers, axis=-1, keepdims=True)
        r.probs[h] = probs
        mixed.append(nn(probs.astype(BF16), r.qkv[2][:, cols]))
    r.mixed[...] = jnp.concatenate(mixed, axis=1).astype(BF16)

    @pl.when(at_first)
    def _():
        all_are_here()

    scatter_chunks(
        rs_attn, r.p1, lambda rows: nn(r.mixed[rows, :], r.attn_weight[...])
    )
    all_normed.start_all()

    @pl.when(at_first)
    def _():
        routing()

    def hand_on_mixed(h):
        r.t1[rows_of(t, h), :] = collect(rs_attn, r.p1, r.l1, h).astype(BF16)
        ag_attn.start_all(h)

    each_owned(hand_on_mixed)
    ag_attn.wait_all()
    hidden = r.x[...] + (r.t1[...].astype(F32) + r.attn_bias[...])
    r.hidden[...] = hidden

    @pl.when(at_first)
    def _():
        resid_copy(r.hidden).start()

    normed_second, inv_second = standardize(hidden)
    r.h2[...] = normed_second
    r.r2[...] = inv_second
    r.nb[...] = (normed_second * scale1 + shift1).astype(BF16)

    def dispatch_one(k, carry):
        there = dispatch.ahead(k)
        r.o1[there] = nn(r.place[there], r.nb[...]).astype(BF16)
        dispatch.start(k)
        return carry

    lax.fori_loop(1, WHOLE, dispatch_one, 0)
    if PARTED > 1:
        there = dispatch.ahead(E - 1)
        r.o1[there] = nn(r.place[there], r.nb[...]).astype(BF16)
        for h in range(PARTED):
            dispatch.start(E - 1, h)
    r.b1[e] = nn(r.place[e], r.nb[...]).astype(BF16)

    @pl.when(at_first)
    def _():
        load(0).wait()
        load(1).wait()

        def both(image, k, rows):
            expert_block(image, rows)
            forward_part(image, k, rows)

        each_block(dispatch, both)
        finish_forward(True)
        r.g[...] = from_other_section()
        dispatch_grads()

        def back(image, k, rows):
            raw_block(image, rows)
            backward_part(image, k, rows)

        each_block(grads, back)

    @pl.when(at_second)
    def _():
        load(0).wait()

        def both(image, k, rows):
            expert_block(image, rows)
            backward_part(image, k, rows)

        each_block(dispatch, both)
        each_block(None, forward_part)

    slots = E * CAP
    r.grad_expert_out[...] = tn(
        r.act[...].reshape(slots, HW), r.b3[...].reshape(slots, D)
    )
    r.grad_expert_out_bias[...] = jnp.sum(
        r.b3[...].reshape(slots, D).astype(F32), axis=0, keepdims=True
    )
    grad_parts.wait_all()
    scatter_chunks(rs_grad, r.p3, lambda rows: combined(r.b4, False, rows))
    r.grad_expert_in[...] = tn(
        r.b1[...].reshape(slots, D), r.gpb[...].reshape(slots, HW)
    )
    r.grad_expert_in_bias[...] = r.in_bias[...]
    r.summed[...] = jnp.zeros((H * ROW_TILE, D), F32)

    def hand_on_grad(h):
        rows = rows_of(t, h)
        total = collect(rs_grad, r.p3, r.l3, h)
        delta = norm_back(total, r.h2[rows, :], r.r2[rows, :], scale1)
        r.t3[rows, :] = delta.astype(BF16)
        ag_grad.start_all(h)
        r.summed[piece(h), :] = total

    each_owned(hand_on_grad)

    def add_small(row, value):
        r.small[row : row + 1, :] = r.small[row : row + 1, :] + jnp.sum(value, axis=0, keepdims=True)

    for h in range(H):
        add_small(1, r.summed[piece(h), :] * r.h2[rows_of(t, h), :])
    add_small(3, r.summed[...])
    ag_grad.wait_all()
    grad_hidden = r.g[...] + r.t3[...].astype(F32)
    r.g[...] = grad_hidden

    @pl.when(at_second)
    def _():
        resid_copy(r.g).start()

    for h in range(H):
        add_small(4, r.g[rows_of(t, h), :])
    grad_hidden_b = grad_hidden.astype(BF16)
    grad_mixed = nt(grad_hidden_b, r.attn_weight[...]).astype(BF16)
    r.w_part[...] = jnp.zeros((E * WC, D), BF16)
    r.w_part[0:W, :] = tn(r.mixed[...], grad_hidden_b).astype(BF16)
    rs_weight.start_all()
    found = [[], [], []]
    for h in range(heads):
        cols = slice(h * HEAD_DIM, (h + 1) * HEAD_DIM)
        query, key, value = r.qkv[0][:, cols], r.qkv[1][:, cols], r.qkv[2][:, cols]
        grad_mixed_h = grad_mixed[:, cols]
        probs = r.probs[h]
        grad_values = tn(probs.astype(BF16), grad_mixed_h)
        grad_probs = nt(grad_mixed_h, value)
        row_delta = jnp.sum(
            grad_mixed_h.astype(F32) * r.mixed[...][:, cols].astype(F32), axis=-1, keepdims=True
        )
        grad_scores = (probs * (grad_probs - row_delta) * scale_factor).astype(BF16)
        found[0].append(nn(grad_scores, key))
        found[1].append(tn(grad_scores, query))
        found[2].append(grad_values)
    for j in (0, 2):
        row = 5 + j // 2
        r.small[row : row + 1, 0:W] = jnp.concatenate(
            [jnp.sum(columns, axis=0, keepdims=True) for columns in found[j]], axis=1
        )
    flat = jnp.concatenate(found[0] + found[1] + found[2], axis=1).astype(BF16)
    r.grad_flat[...] = flat
    r.gp[e] = flat[0:RG]

    def proj_chunk(rows):
        return nn(r.grad_flat[rows, :], r.proj_weight[...].reshape(3 * W, D))

    scatter_chunks(rs_proj, r.p4, proj_chunk)
    all_proj.start_all()
    normed_first, inv_first = standardize(r.x[...])
    partial_rows = r.p4[...].astype(F32)
    add_small(0, partial_rows * normed_first)
    add_small(2, partial_rows)
    small_t.start_all()
    r.h1[...] = normed_first
    r.r1[...] = inv_first

    def hand_on_proj(h):
        rows = rows_of(t, h)
        total = collect(rs_proj, r.p4, r.l4, h)
        r.t4[rows, :] = norm_back(total, r.h1[rows, :], r.r1[rows, :], scale0).astype(BF16)

        @pl.when(at_second)
        def _():
            cross(r.t4, h)

        @pl.when(at_first)
        def _():
            ag_proj.start_all(h)

    each_owned(hand_on_proj)

    @pl.when(at_second)
    def _():
        for h in range(H):
            ag_proj.start_all(h)

    small_t.wait_all()
    total = r.small[...]
    summed = total
    for k in range(1, T):
        summed = summed + r.small_t[k - 1]
    r.small2[...] = jnp.where(iota((8, D), 0) < 5, summed, total)
    small_e.start_all()
    rs_weight.wait_all()
    total = r.w_part[weight_rows(e), :].astype(F32)
    for k in range(1, E):
        total = total + r.w_land[k - 1].astype(F32)
    r.w_sum[weight_rows(e), :] = total.astype(BF16)
    ag_weight.start_all()

    @pl.when(at_second)
    def _():
        finish_forward(False)

    all_normed.wait_all()
    all_proj.wait_all()
    tokens = E * RG
    grad_proj = tn(r.gp[...].reshape(tokens, 3 * W), r.na[...].reshape(tokens, D))
    r.grad_proj[...] = grad_proj.reshape(3, W, D)
    small_e.wait_all()
    total = r.small2[...]
    for k in range(1, E):
        total = total + r.small_e[k - 1]
    r.grad_norm_scale[...] = total[0:2]
    r.grad_norm_shift[...] = total[2:4]
    r.grad_attn_bias[...] = total[4:5]
    r.grad_proj_bias[...] = total[5:7, 0:W]
    ag_weight.wait_all()
    r.grad_attn_weight[...] = r.w_sum[0:W, :].astype(F32)
    ag_proj.wait_all()
    grad_in = r.g[...] + r.t4[...].astype(F32)
    r.section_in_grad[...] = grad_in[0:R]

    for swapped in (
        rs_attn, ag_attn, rs_moe, ag_moe, rs_grad, ag_grad, rs_proj, ag_proj,
        dispatch, parts, grads, grad_parts,
        all_normed, all_proj, rs_weight, ag_weight, small_e, small_t,
    ):
        swapped.drain()
    resid_copy(r.resid_in).wait_send()
    for h in range(H):
        for k in range(T):
            owned(h, t, lambda: cross_copy(r.t4, k, h).wait_send())


def write_kernel(count, *refs):
    sems = refs[-1]
    copies = []
    for k in range(count):
        source, target = refs[k], refs[count + k]
        if len(target.shape) > len(source.shape):
            target = target.at[:, 0, :]
        copies.append(pltpu.make_async_copy(source, target, sems.at[k]))
    for copy in copies:
        copy.start()
    for copy in copies:
        copy.wait()


def slot_count(row_count, experts):
    return max(2, (3 * TOPK * row_count + 2 * experts - 1) // (2 * experts))


def round_up(value, unit):
    return -(-value // unit) * unit


def on_device(
    inputs,
    cotangent,
    norm_scale,
    norm_shift,
    proj_weight,
    proj_bias,
    attn_weight,
    attn_bias,
    expert_in,
    expert_in_bias,
    expert_out,
    expert_out_bias,
    routes,
    gate_weights,
):
    E, T = lax.axis_size("expert"), lax.axis_size("tensor")
    R, D = inputs.shape[1:]
    W, HW = proj_weight.shape[3], expert_in.shape[3]
    tiles = -(-R // ROW_TILE)
    H = -(-tiles // T)
    LAST = tiles - (H - 1) * T
    RP = H * T * ROW_TILE
    CAP = round_up(slot_count(R, E), ROW_TILE)
    RG = round_up(R, ROW_TILE)
    EP = round_up(E, ROW_TILE)
    WC = round_up(-(-W // E), ROW_TILE)
    d = types.SimpleNamespace(
        E=E, T=T, R=R, RG=RG, RP=RP, LAST=LAST, CAP=CAP, D=D, W=W, HW=HW, H=H, EP=EP, WC=WC
    )
    heads = W // HEAD_DIM

    operands = dict(
        inputs=jnp.transpose(inputs, (1, 0, 2)),
        cotangent=jnp.transpose(cotangent, (1, 0, 2)),
        norm_scale=norm_scale[0],
        norm_shift=norm_shift[0],
        proj_weight=jnp.transpose(proj_weight[0], (1, 2, 0)),
        proj_bias=proj_bias[0],
        attn_weight=attn_weight[0],
        attn_bias=attn_bias,
        expert_in=expert_in[0, 0],
        expert_in_bias=expert_in_bias[0],
        expert_out=expert_out[0, 0],
        expert_out_bias=expert_out_bias[0],
        routes=routes[0, 0].T,
        gate_weights=gate_weights[0, 0].T,
    )
    results = dict(
        section_out=(R, D),
        section_in_grad=(R, D),
        grad_norm_scale=(2, D),
        grad_norm_shift=(2, D),
        grad_proj_bias=(2, W),
        grad_attn_bias=(1, D),
        grad_proj=(3, W, D),
        grad_attn_weight=(W, D),
        grad_expert_in=(D, HW),
        grad_expert_in_bias=(1, HW),
        grad_expert_out=(HW, D),
        grad_expert_out_bias=(1, D),
    )
    scratch = dict(
        x=((RP, D), F32),
        rows_in=((R, D), F32),
        g=((RP, D), F32),
        hidden=((RP, D), F32),
        h2=((RP, D), F32),
        r2=((RP, 1), F32),
        nb=((RP, D), BF16),
        resid_in=((RP, D), F32),
        delta_in=((RP, D), BF16),
        qkv=((3, RP, W), BF16),
        probs=((heads, RP, RP), F32),
        na=((E, RG, D), BF16),
        mixed=((RP, W), BF16),
        gp=((E, RG, 3 * W), BF16),
        grad_flat=((RP, 3 * W), BF16),
        h1=((RP, D), F32),
        r1=((RP, 1), F32),
        summed=((H * ROW_TILE, D), F32),
        w_part=((E * WC, D), BF16),
        w_land=((E - 1, WC, D), BF16),
        w_sum=((E * WC, D), BF16),
        rt=((RP, 8), F32),
        gt=((RP, 8), F32),
        rt_t=((8, RP), F32),
        gt_t=((8, RP), F32),
        w_in=((D, HW), BF16),
        w_out=((HW, D), BF16),
        pick=((E, RP, CAP), BF16),
        place=((E, CAP, RP), BF16),
        act=((E, CAP, HW), BF16),
        gpb=((E, CAP, HW), BF16),
        slope=((E, CAP, HW), F32),
        raw=((E, CAP, HW), F32),
        in_bias=((1, HW), F32),
        small=((8, D), F32),
        small2=((8, D), F32),
        small_e=((E - 1, 8, D), F32),
        small_t=((T - 1, 8, D), F32),
    )
    for k in range(1, 5):
        scratch[f"p{k}"] = ((RP, D), BF16)
        scratch[f"l{k}"] = ((T - 1, H * ROW_TILE, D), BF16)
        scratch[f"t{k}"] = ((RP, D), BF16)
        scratch[f"o{k}"] = ((E, CAP, D), BF16)
        scratch[f"b{k}"] = ((E, CAP, D), BF16)
    sems = pltpu.SemaphoreType.DMA((PHASES, max(2 * E, T * H)))
    names = list(operands) + list(results) + list(scratch) + ["load_sem", "send_sem", "recv_sem"]
    in_vmem, in_place = pl.BlockSpec(memory_space=pltpu.VMEM), pl.BlockSpec(memory_space=pl.ANY)
    loaded = ("inputs", "cotangent", "expert_in", "expert_out")
    found = pl.pallas_call(
        functools.partial(relay_kernel, names, d),
        out_shape=[pltpu.VMEM(shape, F32) for shape in results.values()],
        in_specs=[in_place if name in loaded else in_vmem for name in operands],
        out_specs=[in_vmem] * len(results),
        scratch_shapes=[pltpu.VMEM(shape, dtype) for shape, dtype in scratch.values()]
        + [pltpu.SemaphoreType.DMA((len(loaded),)), sems, sems],
        compiler_params=pltpu.CompilerParams(
            collective_id=0, has_side_effects=True, vmem_limit_bytes=52 * 2**20
        ),
        name="relay",
    )(*operands.values())
    shapes = [
        (R, 1, D) if name.startswith("section") else shape for name, shape in results.items()
    ]
    written = pl.pallas_call(
        functools.partial(write_kernel, len(results)),
        out_shape=[jax.ShapeDtypeStruct(shape, F32) for shape in shapes],
        in_specs=[in_vmem] * len(results),
        out_specs=[in_place] * len(results),
        scratch_shapes=[pltpu.SemaphoreType.DMA((len(results),))],
        compiler_params=pltpu.CompilerParams(vmem_limit_bytes=2**20),
        name="write",
    )(*[pltpu.with_memory_space_constraint(array, pltpu.VMEM) for array in found])
    found = types.SimpleNamespace(**dict(zip(results, written)))
    return (
        jnp.transpose(found.section_out, (1, 0, 2))[None],
        jnp.transpose(found.section_in_grad, (1, 0, 2))[None],
        found.grad_norm_scale[None],
        found.grad_norm_shift[None],
        jnp.transpose(found.grad_proj, (2, 0, 1))[None],
        found.grad_proj_bias[None],
        found.grad_attn_weight[None],
        found.grad_attn_bias,
        found.grad_expert_in[None, None],
        found.grad_expert_in_bias[None],
        found.grad_expert_out[None, None],
        found.grad_expert_out_bias[None],
    )


def solution(mesh):
    in_specs = (
        P(None, "expert", None),
        P(None, "expert", None),
        P("section", None, None),
        P("section", None, None),
        P("section", None, None, "tensor"),
        P("section", None, "tensor"),
        P("section", "tensor", None),
        P("section", None),
        P("section", "expert", None, "tensor"),
        P("section", "expert", "tensor"),
        P("section", "expert", "tensor", None),
        P("section", "expert", None),
        P("section", None, "expert", None),
        P("section", None, "expert", None),
    )
    out_specs = (
        P("section", None, "expert", None),
        P("section", None, "expert", None),
        P("section", None, None),
        P("section", None, None),
        P("section", None, None, "tensor"),
        P("section", None, "tensor"),
        P("section", "tensor", None),
        P("section", None),
        P("section", "expert", None, "tensor"),
        P("section", "expert", "tensor"),
        P("section", "expert", "tensor", None),
        P("section", "expert", None),
    )
    return jax.shard_map(
        on_device, mesh=mesh, in_specs=in_specs, out_specs=out_specs, check_vma=False
    )
```

```python
import functools
import math
import types

import jax
import jax.numpy as jnp
from jax import lax
from jax.experimental import pallas as pl
from jax.experimental.pallas import tpu as pltpu
from jax.sharding import PartitionSpec as P

HEAD_DIM = 64
TOPK = 2

NORM_EPSILON = 1e-06
GELU_FACTOR = 0.7978845608028654
CUBIC_TERM = 0.044715

MESH = pl.DeviceIdType.MESH
ROW_TILE = 16
BF16 = jnp.bfloat16
F32 = jnp.float32

(
    RS_ATTN,
    AG_ATTN,
    DISPATCH,
    PARTS,
    RS_MOE,
    AG_MOE,
    CROSS,
    RESID,
    GRADS,
    GRAD_PARTS,
    RS_GRAD,
    AG_GRAD,
    RS_PROJ,
    AG_PROJ,
    ALL_NORMED,
    RS_WEIGHT,
    AG_WEIGHT,
    ALL_PROJ,
    SMALL_E,
    SMALL_T,
    PHASES,
) = range(21)


def nn(left, right):
    return jnp.dot(left, right, preferred_element_type=F32)


def nt(left, right):
    return lax.dot_general(left, right, (((1,), (1,)), ((), ())), preferred_element_type=F32)


def tn(left, right):
    return lax.dot_general(left, right, (((0,), (0,)), ((), ())), preferred_element_type=F32)


def standardize(values):
    average = jnp.mean(values, axis=-1, keepdims=True)
    centred = values - average
    variance = jnp.mean(centred * centred, axis=-1, keepdims=True)
    inv_std = lax.rsqrt(variance + NORM_EPSILON)
    return centred * inv_std, inv_std


def norm_back(grad_normed, normed, inv_std, scale_row):
    scaled = grad_normed * scale_row
    return (
        scaled
        - jnp.mean(scaled, axis=-1, keepdims=True)
        - normed * jnp.mean(scaled * normed, axis=-1, keepdims=True)
    ) * inv_std


def iota(shape, axis):
    return lax.broadcasted_iota(jnp.int32, shape, axis)


def always(k, h, body):
    body()


class Swap:
    def __init__(self, r, phase, axis, pieces, source, landing, sends=None, comes=None, blocks=False):
        self.r, self.phase, self.axis, self.pieces = r, phase, axis, pieces
        self.sends, self.comes = sends or always, comes or always
        self.blocks = blocks
        self.size = lax.axis_size(axis)
        self.me = lax.axis_index(axis)
        side = math.isqrt(self.size)
        self.q = side if axis == "expert" and side * side == self.size else 1
        self.source, self.landing = source, landing

    def walk(self, high, low):
        return lax.rem(high, self.size // self.q) * self.q + lax.rem(low, self.q)

    def ahead(self, k):
        q = self.q
        return self.walk(self.me // q + k // q, self.me % q + k % q)

    def behind(self, k):
        q = self.q
        return self.walk(self.me // q + self.size // q - k // q, self.me % q + q - k % q)

    def back(self, k):
        q = self.q
        return self.walk(self.size // q - k // q, q - k % q)

    def copy(self, k, h):
        there = self.ahead(k)
        return pltpu.make_async_remote_copy(
            src_ref=self.source(there, h, k) if self.blocks else self.source(there, h),
            dst_ref=self.landing(k, h),
            send_sem=self.r.send_sem.at[self.phase, k * self.pieces + h],
            recv_sem=self.r.recv_sem.at[self.phase, k * self.pieces + h],
            device_id={self.axis: there},
            device_id_type=MESH,
        )

    def start(self, k, h=0):
        self.sends(k, h, lambda: self.copy(k, h).start())

    def start_all(self, h=0):
        for k in range(1, self.size):
            self.start(k, h)

    def wait(self, k, h=0):
        self.comes(k, h, lambda: self.copy(k, h).wait_recv())

    def pieces_of(self, k):
        return self.pieces if not self.blocks or k == self.size - 1 else 1

    def wait_all(self):
        for k in range(1, self.size):
            for h in range(self.pieces_of(k)):
                self.wait(k, h)

    def drain(self):
        for k in range(1, self.size):
            for h in range(self.pieces_of(k)):
                self.sends(k, h, lambda: self.copy(k, h).wait_send())


def relay_kernel(names, d, *refs):
    r = types.SimpleNamespace(**dict(zip(names, refs)))
    E, T, R, RG, RP, H, EP = d.E, d.T, d.R, d.RG, d.RP, d.H, d.EP
    WC, LAST = d.WC, d.LAST
    PARTED = 2 if E == 4 and d.CAP % (2 * ROW_TILE) == 0 else 1
    WHOLE = E - 1 if PARTED > 1 else E
    CAP, D, W, HW = d.CAP, d.D, d.W, d.HW
    heads = W // HEAD_DIM
    scale_factor = HEAD_DIM ** (-0.5)
    s, e, t = [lax.axis_index(name) for name in ("section", "expert", "tensor")]
    other = 1 - s
    at_first, at_second = s == 0, s == 1

    def owned(h, owner, body):
        if h == H - 1 and LAST < T:
            pl.when(owner < LAST)(body)
        else:
            body()

    def piece(h):
        return pl.ds(h * ROW_TILE, ROW_TILE)

    def piece_rows(h):
        count = LAST if h == H - 1 else T
        return pl.ds(h * T * ROW_TILE, count * ROW_TILE)

    def rows_of(owner, h):
        return pl.ds(pl.multiple_of((h * T + owner) * ROW_TILE, ROW_TILE), ROW_TILE)

    def z_ahead(k):
        return lax.rem(t + k, T)

    def z_behind(k):
        return lax.rem(t + T - k, T)

    def gather(phase, ref):
        return Swap(r, phase, "expert", 1, lambda there, h: ref.at[e], lambda k, h: ref.at[e])

    def gather_rows(phase, ref):
        return Swap(
            r, phase, "tensor", H,
            lambda there, h: ref.at[rows_of(t, h)],
            lambda k, h: ref.at[rows_of(t, h)],
            lambda k, h, body: owned(h, t, body),
            lambda k, h, body: owned(h, z_behind(k), body),
        )

    def scatter_rows(phase, source, landing):
        return Swap(
            r, phase, "tensor", H,
            lambda there, h: source.at[rows_of(there, h)],
            lambda k, h: landing.at[k - 1, piece(h)],
            lambda k, h, body: owned(h, z_ahead(k), body),
        )

    rs_attn = scatter_rows(RS_ATTN, r.p1, r.l1)
    ag_attn = gather_rows(AG_ATTN, r.t1)
    rs_moe = scatter_rows(RS_MOE, r.p2, r.l2)
    ag_moe = gather_rows(AG_MOE, r.t2)
    rs_grad = scatter_rows(RS_GRAD, r.p3, r.l3)
    ag_grad = gather_rows(AG_GRAD, r.t3)
    rs_proj = scatter_rows(RS_PROJ, r.p4, r.l4)
    ag_proj = gather_rows(AG_PROJ, r.t4)

    def is_last(k):
        return PARTED > 1 and isinstance(k, int) and k == E - 1

    def half(h):
        return pl.ds(h * (CAP // PARTED), CAP // PARTED)

    def routed(phase, source, landing):
        def part(ref, k, block, h):
            return ref.at[block, half(h)] if is_last(k) else ref.at[block]

        return Swap(
            r, phase, "expert", PARTED,
            lambda there, h, k: part(source, k, there, h),
            lambda k, h: part(landing, k, e, h),
            blocks=True,
        )

    dispatch = routed(DISPATCH, r.o1, r.b1)
    parts = routed(PARTS, r.o2, r.b2)
    grads = routed(GRADS, r.o3, r.b3)
    grad_parts = routed(GRAD_PARTS, r.o4, r.b4)
    all_normed = gather(ALL_NORMED, r.na)

    def weight_rows(owner):
        return pl.ds(pl.multiple_of(owner * WC, WC), WC)

    rs_weight = Swap(
        r, RS_WEIGHT, "expert", 1,
        lambda there, h: r.w_part.at[weight_rows(there)],
        lambda k, h: r.w_land.at[k - 1],
    )
    ag_weight = Swap(
        r, AG_WEIGHT, "expert", 1,
        lambda there, h: r.w_sum.at[weight_rows(e)],
        lambda k, h: r.w_sum.at[weight_rows(e)],
    )
    all_proj = gather(ALL_PROJ, r.gp)
    small_e = Swap(
        r, SMALL_E, "expert", 1, lambda there, h: r.small2, lambda k, h: r.small_e.at[k - 1]
    )
    small_t = Swap(
        r, SMALL_T, "tensor", 1, lambda there, h: r.small, lambda k, h: r.small_t.at[k - 1]
    )

    def cross_copy(source, k, h):
        return pltpu.make_async_remote_copy(
            src_ref=source.at[rows_of(t, h)],
            dst_ref=r.delta_in.at[rows_of(t, h)],
            send_sem=r.send_sem.at[CROSS, k * H + h],
            recv_sem=r.recv_sem.at[CROSS, k * H + h],
            device_id={"section": other, "tensor": z_ahead(k)},
            device_id_type=MESH,
        )

    def resid_copy(source):
        return pltpu.make_async_remote_copy(
            src_ref=source,
            dst_ref=r.resid_in,
            send_sem=r.send_sem.at[RESID, 0],
            recv_sem=r.recv_sem.at[RESID, 0],
            device_id={"section": other},
            device_id_type=MESH,
        )

    def load(k):
        source, target = (
            (r.expert_in, r.w_in), (r.expert_out, r.w_out),
            (r.inputs.at[:, 0, :], r.rows_in), (r.cotangent.at[:, 0, :], r.rows_in),
        )[k]
        return pltpu.make_async_copy(source, target, r.load_sem.at[k])

    def from_other_section():
        resid_copy(r.resid_in).wait_recv()
        for h in range(H):
            for k in range(T):
                owned(h, z_behind(k), lambda: cross_copy(r.delta_in, k, h).wait_recv())
        return r.resid_in[...] + r.delta_in[...].astype(F32)

    r.x[...] = jnp.zeros((RP, D), F32)
    r.g[...] = jnp.zeros((RP, D), F32)
    if RG < RP:
        for ref in (r.t1, r.t2, r.t3, r.t4, r.p4, r.delta_in):
            ref[RG:RP, :] = jnp.zeros((RP - RG, D), BF16)

    @pl.when(at_first)
    def _():
        load(2).start()

    @pl.when(at_second)
    def _():
        load(3).start()

    load(1).start()
    load(0).start()

    barrier = pltpu.get_barrier_semaphore()
    friends = [{"tensor": lax.rem(t + k, T)} for k in range(1, T)]
    friends += [{"expert": lax.rem(e + k, E)} for k in range(1, E)]
    friends += [{"section": other, "tensor": lax.rem(t + k, T)} for k in range(T)]
    for device in friends:
        pl.semaphore_signal(barrier, inc=1, device_id=device, device_id_type=MESH)

    def all_are_here():
        pl.semaphore_wait(barrier, len(friends))

    def gate_of(expert, rows=slice(None)):
        ids, gates = r.rt[rows, :], r.gt[rows, :]
        named = lax.convert_element_type(expert, F32)
        return jnp.sum(jnp.where(ids == named, gates, 0.0), axis=-1, keepdims=True)

    def routing():
        r.rt_t[...] = jnp.full((8, RP), -1.0, F32)
        r.gt_t[...] = jnp.zeros((8, RP), F32)
        r.rt_t[0:TOPK, 0:R] = r.routes[...].astype(F32)
        r.gt_t[0:TOPK, 0:R] = r.gate_weights[...]
        ids = r.rt_t[...]
        r.rt[...] = jnp.transpose(ids)
        r.gt[...] = jnp.transpose(r.gt_t[...])
        expert = iota((EP, RP), 0).astype(F32)
        named = jnp.where((ids[0:1] == expert) | (ids[1:2] == expert), 1.0, 0.0)
        later = jnp.where(iota((RP, RP), 0) < iota((RP, RP), 1), 1.0, 0.0)
        slot_t = jnp.where(named > 0.5, nn(named.astype(BF16), later.astype(BF16)), -1.0)
        slot = jnp.transpose(slot_t)
        wide = iota((RP, CAP), 1).astype(F32)
        tall = iota((CAP, RP), 0).astype(F32)
        for k in range(E):
            r.pick[k] = jnp.where(slot[:, k : k + 1] == wide, 1.0, 0.0).astype(BF16)
            r.place[k] = jnp.where(slot_t[k : k + 1, :] == tall, 1.0, 0.0).astype(BF16)

    def dispatch_grads():
        def outgoing(expert):
            weighted = (gate_of(expert) * r.g[...]).astype(BF16)
            return nn(r.place[expert], weighted).astype(BF16)

        def one(k, carry):
            there = grads.ahead(k)
            r.o3[there] = outgoing(there)
            grads.start(k)
            return carry

        lax.fori_loop(1, WHOLE, one, 0)
        if PARTED > 1:
            r.o3[grads.ahead(E - 1)] = outgoing(grads.ahead(E - 1))
            for h in range(PARTED):
                grads.start(E - 1, h)
        r.b3[e] = outgoing(e)

    def each_block(swapped, body):
        body(e, 0, slice(None))

        def one(k, carry):
            if swapped is not None:
                swapped.wait(k)
            body(dispatch.behind(k), k, slice(None))
            return carry

        lax.fori_loop(1, WHOLE, one, 0)
        if PARTED > 1:
            for h in range(PARTED):
                if swapped is not None:
                    swapped.wait(E - 1, h)
                body(dispatch.behind(E - 1), (E - 1, h), half(h))

    def send_part(swapped, outgoing, landing, image, k, rows, value):
        if isinstance(k, int):
            landing[image] = value
            return
        outgoing[image, rows, :] = value
        if isinstance(k, tuple):
            swapped.start(*k)
        else:
            swapped.start(swapped.back(k))

    def raw_block(image, rows):
        r.raw[image, rows, :] = nt(r.b3[image, rows, :], r.w_out[...])

    def backward_part(image, k, rows):
        grad_pre = r.raw[image, rows, :] * r.slope[image, rows, :]
        r.in_bias[...] = r.in_bias[...] + jnp.sum(grad_pre, axis=0, keepdims=True)
        grad_pre_b = grad_pre.astype(BF16)
        r.gpb[image, rows, :] = grad_pre_b
        value = nt(grad_pre_b, r.w_in[...]).astype(BF16)
        send_part(grad_parts, r.o4, r.b4, image, k, rows, value)

    def forward_part(image, k, rows):
        bias = jnp.where(t == 0, r.expert_out_bias[...], 0.0)
        value = (nn(r.act[image, rows, :], r.w_out[...]) + bias).astype(BF16)
        send_part(parts, r.o2, r.b2, image, k, rows, value)

    def expert_block(image, rows):
        pre = nn(r.b1[image, rows, :], r.w_in[...]) + r.expert_in_bias[...]
        square = pre * pre
        tangent = jnp.tanh(GELU_FACTOR * (pre + CUBIC_TERM * square * pre))
        rise = 0.5 * (1.0 + tangent)
        r.act[image, rows, :] = (pre * rise).astype(BF16)
        r.slope[image, rows, :] = rise + 0.5 * pre * (1.0 - tangent * tangent) * GELU_FACTOR * (
            1.0 + 3.0 * CUBIC_TERM * square
        )

    def scatter_chunks(swapped, part, chunk_of):
        for h in range(H):
            rows = piece_rows(h)
            part[rows, :] = chunk_of(rows).astype(BF16)
            swapped.start_all(h)

    def collect(swapped, part, landing, h):
        total = part[rows_of(t, h), :].astype(F32)
        for k in range(1, T):
            swapped.wait(k, h)
            total = total + landing[k - 1, piece(h)].astype(F32)
        return total

    def each_owned(body):
        for h in range(H):
            owned(h, t, functools.partial(body, h))

    def cross(ref, h):
        for k in range(T):
            owned(h, t, lambda: cross_copy(ref, k, h).start())

    def combined(landed, gated, rows):
        total = None
        for k in range(E):
            term = nn(r.pick[k, rows, :], landed[k])
            if gated:
                term = gate_of(k, rows) * term
            total = term if total is None else total + term
        return total

    def finish_forward(crossing):
        parts.wait_all()
        scatter_chunks(rs_moe, r.p2, lambda rows: combined(r.b2, True, rows))

        def hand_on(h):
            r.t2[rows_of(t, h), :] = collect(rs_moe, r.p2, r.l2, h).astype(BF16)
            if crossing:
                cross(r.t2, h)

        each_owned(hand_on)
        for h in range(H):
            ag_moe.start_all(h)
        ag_moe.wait_all()
        out = r.hidden[...] + r.t2[...].astype(F32)
        r.section_out[...] = out[0:R]

    r.in_bias[...] = jnp.zeros((1, HW), F32)
    r.small[...] = jnp.zeros((8, D), F32)

    @pl.when(at_first)
    def _():
        load(2).wait()
        r.x[0:R, :] = r.rows_in[...]

    @pl.when(at_second)
    def _():
        routing()
        load(3).wait()
        all_are_here()
        r.g[0:R, :] = r.rows_in[...]
        dispatch_grads()
        load(1).wait()
        each_block(grads, lambda image, k, rows: raw_block(image, rows))
        r.x[...] = from_other_section()

    inside = iota((RP, 1), 0) < R
    scale0, scale1 = r.norm_scale[0:1, :], r.norm_scale[1:2, :]
    shift0, shift1 = r.norm_shift[0:1, :], r.norm_shift[1:2, :]
    normed_first, _ = standardize(r.x[...])
    normed_a = jnp.where(inside, normed_first * scale0 + shift0, 0.0).astype(BF16)
    r.na[e] = normed_a[0:RG]
    query = nt(normed_a, r.proj_weight[0]) + r.proj_bias[0:1, :]
    r.qkv[0] = jnp.where(inside, query, 0.0).astype(BF16)
    r.qkv[1] = nt(normed_a, r.proj_weight[1]).astype(BF16)
    value = nt(normed_a, r.proj_weight[2]) + r.proj_bias[1:2, :]
    r.qkv[2] = jnp.where(inside, value, 0.0).astype(BF16)
    real_key = iota((RP, RP), 1) < R
    mixed = []
    for h in range(heads):
        cols = slice(h * HEAD_DIM, (h + 1) * HEAD_DIM)
        scores = nt(r.qkv[0][:, cols], r.qkv[1][:, cols]) * scale_factor
        powers = jnp.where(real_key, jnp.exp(scores), 0.0)
        probs = powers / jnp.sum(powers, axis=-1, keepdims=True)
        r.probs[h] = probs
        mixed.append(nn(probs.astype(BF16), r.qkv[2][:, cols]))
    r.mixed[...] = jnp.concatenate(mixed, axis=1).astype(BF16)

    @pl.when(at_first)
    def _():
        all_are_here()

    scatter_chunks(
        rs_attn, r.p1, lambda rows: nn(r.mixed[rows, :], r.attn_weight[...])
    )
    all_normed.start_all()

    @pl.when(at_first)
    def _():
        routing()

    def hand_on_mixed(h):
        r.t1[rows_of(t, h), :] = collect(rs_attn, r.p1, r.l1, h).astype(BF16)
        ag_attn.start_all(h)

    each_owned(hand_on_mixed)
    ag_attn.wait_all()
    hidden = r.x[...] + (r.t1[...].astype(F32) + r.attn_bias[...])
    r.hidden[...] = hidden

    @pl.when(at_first)
    def _():
        resid_copy(r.hidden).start()

    normed_second, inv_second = standardize(hidden)
    r.h2[...] = normed_second
    r.r2[...] = inv_second
    r.nb[...] = (normed_second * scale1 + shift1).astype(BF16)

    def dispatch_one(k, carry):
        there = dispatch.ahead(k)
        r.o1[there] = nn(r.place[there], r.nb[...]).astype(BF16)
        dispatch.start(k)
        return carry

    lax.fori_loop(1, WHOLE, dispatch_one, 0)
    if PARTED > 1:
        there = dispatch.ahead(E - 1)
        r.o1[there] = nn(r.place[there], r.nb[...]).astype(BF16)
        for h in range(PARTED):
            dispatch.start(E - 1, h)
    r.b1[e] = nn(r.place[e], r.nb[...]).astype(BF16)

    @pl.when(at_first)
    def _():
        load(0).wait()
        load(1).wait()

        def both(image, k, rows):
            expert_block(image, rows)
            forward_part(image, k, rows)

        each_block(dispatch, both)
        finish_forward(True)
        r.g[...] = from_other_section()
        dispatch_grads()

        def back(image, k, rows):
            raw_block(image, rows)
            backward_part(image, k, rows)

        each_block(grads, back)

    @pl.when(at_second)
    def _():
        load(0).wait()

        def both(image, k, rows):
            expert_block(image, rows)
            backward_part(image, k, rows)

        each_block(dispatch, both)
        each_block(None, forward_part)

    slots = E * CAP
    r.grad_expert_out[...] = tn(
        r.act[...].reshape(slots, HW), r.b3[...].reshape(slots, D)
    )
    r.grad_expert_out_bias[...] = jnp.sum(
        r.b3[...].reshape(slots, D).astype(F32), axis=0, keepdims=True
    )
    grad_parts.wait_all()
    scatter_chunks(rs_grad, r.p3, lambda rows: combined(r.b4, False, rows))
    r.grad_expert_in[...] = tn(
        r.b1[...].reshape(slots, D), r.gpb[...].reshape(slots, HW)
    )
    r.grad_expert_in_bias[...] = r.in_bias[...]
    r.summed[...] = jnp.zeros((H * ROW_TILE, D), F32)

    def hand_on_grad(h):
        rows = rows_of(t, h)
        total = collect(rs_grad, r.p3, r.l3, h)
        delta = norm_back(total, r.h2[rows, :], r.r2[rows, :], scale1)
        r.t3[rows, :] = delta.astype(BF16)
        ag_grad.start_all(h)
        r.summed[piece(h), :] = total

    each_owned(hand_on_grad)

    def add_small(row, value):
        r.small[row : row + 1, :] = r.small[row : row + 1, :] + jnp.sum(value, axis=0, keepdims=True)

    for h in range(H):
        add_small(1, r.summed[piece(h), :] * r.h2[rows_of(t, h), :])
    add_small(3, r.summed[...])
    ag_grad.wait_all()
    grad_hidden = r.g[...] + r.t3[...].astype(F32)
    r.g[...] = grad_hidden

    @pl.when(at_second)
    def _():
        resid_copy(r.g).start()

    for h in range(H):
        add_small(4, r.g[rows_of(t, h), :])
    grad_hidden_b = grad_hidden.astype(BF16)
    grad_mixed = nt(grad_hidden_b, r.attn_weight[...]).astype(BF16)
    r.w_part[...] = jnp.zeros((E * WC, D), BF16)
    r.w_part[0:W, :] = tn(r.mixed[...], grad_hidden_b).astype(BF16)
    rs_weight.start_all()
    found = [[], [], []]
    for h in range(heads):
        cols = slice(h * HEAD_DIM, (h + 1) * HEAD_DIM)
        query, key, value = r.qkv[0][:, cols], r.qkv[1][:, cols], r.qkv[2][:, cols]
        grad_mixed_h = grad_mixed[:, cols]
        probs = r.probs[h]
        grad_values = tn(probs.astype(BF16), grad_mixed_h)
        grad_probs = nt(grad_mixed_h, value)
        row_delta = jnp.sum(
            grad_mixed_h.astype(F32) * r.mixed[...][:, cols].astype(F32), axis=-1, keepdims=True
        )
        grad_scores = (probs * (grad_probs - row_delta) * scale_factor).astype(BF16)
        found[0].append(nn(grad_scores, key))
        found[1].append(tn(grad_scores, query))
        found[2].append(grad_values)
    for j in (0, 2):
        row = 5 + j // 2
        r.small[row : row + 1, 0:W] = jnp.concatenate(
            [jnp.sum(columns, axis=0, keepdims=True) for columns in found[j]], axis=1
        )
    flat = jnp.concatenate(found[0] + found[1] + found[2], axis=1).astype(BF16)
    r.grad_flat[...] = flat
    r.gp[e] = flat[0:RG]

    def proj_chunk(rows):
        return nn(r.grad_flat[rows, :], r.proj_weight[...].reshape(3 * W, D))

    scatter_chunks(rs_proj, r.p4, proj_chunk)
    all_proj.start_all()
    normed_first, inv_first = standardize(r.x[...])
    partial_rows = r.p4[...].astype(F32)
    add_small(0, partial_rows * normed_first)
    add_small(2, partial_rows)
    small_t.start_all()
    rs_weight.wait_all()
    total = r.w_part[weight_rows(e), :].astype(F32)
    for k in range(1, E):
        total = total + r.w_land[k - 1].astype(F32)
    r.w_sum[weight_rows(e), :] = total.astype(BF16)
    ag_weight.start_all()
    r.h1[...] = normed_first
    r.r1[...] = inv_first

    def hand_on_proj(h):
        rows = rows_of(t, h)
        total = collect(rs_proj, r.p4, r.l4, h)
        r.t4[rows, :] = norm_back(total, r.h1[rows, :], r.r1[rows, :], scale0).astype(BF16)

        @pl.when(at_second)
        def _():
            cross(r.t4, h)

        @pl.when(at_first)
        def _():
            ag_proj.start_all(h)

    each_owned(hand_on_proj)

    @pl.when(at_second)
    def _():
        for h in range(H):
            ag_proj.start_all(h)

    small_t.wait_all()
    total = r.small[...]
    summed = total
    for k in range(1, T):
        summed = summed + r.small_t[k - 1]
    r.small2[...] = jnp.where(iota((8, D), 0) < 5, summed, total)
    small_e.start_all()

    @pl.when(at_second)
    def _():
        finish_forward(False)

    all_normed.wait_all()
    all_proj.wait_all()
    tokens = E * RG
    grad_proj = tn(r.gp[...].reshape(tokens, 3 * W), r.na[...].reshape(tokens, D))
    r.grad_proj[...] = grad_proj.reshape(3, W, D)
    small_e.wait_all()
    total = r.small2[...]
    for k in range(1, E):
        total = total + r.small_e[k - 1]
    r.grad_norm_scale[...] = total[0:2]
    r.grad_norm_shift[...] = total[2:4]
    r.grad_attn_bias[...] = total[4:5]
    r.grad_proj_bias[...] = total[5:7, 0:W]
    ag_weight.wait_all()
    r.grad_attn_weight[...] = r.w_sum[0:W, :].astype(F32)
    ag_proj.wait_all()
    grad_in = r.g[...] + r.t4[...].astype(F32)
    r.section_in_grad[...] = grad_in[0:R]

    for swapped in (
        rs_attn, ag_attn, rs_moe, ag_moe, rs_grad, ag_grad, rs_proj, ag_proj,
        dispatch, parts, grads, grad_parts,
        all_normed, all_proj, rs_weight, ag_weight, small_e, small_t,
    ):
        swapped.drain()
    resid_copy(r.resid_in).wait_send()
    for h in range(H):
        for k in range(T):
            owned(h, t, lambda: cross_copy(r.t4, k, h).wait_send())


def write_kernel(count, *refs):
    sems = refs[-1]
    copies = []
    for k in range(count):
        source, target = refs[k], refs[count + k]
        if len(target.shape) > len(source.shape):
            target = target.at[:, 0, :]
        copies.append(pltpu.make_async_copy(source, target, sems.at[k]))
    for copy in copies:
        copy.start()
    for copy in copies:
        copy.wait()


def slot_count(row_count, experts):
    return max(2, (3 * TOPK * row_count + 2 * experts - 1) // (2 * experts))


def round_up(value, unit):
    return -(-value // unit) * unit


def on_device(
    inputs,
    cotangent,
    norm_scale,
    norm_shift,
    proj_weight,
    proj_bias,
    attn_weight,
    attn_bias,
    expert_in,
    expert_in_bias,
    expert_out,
    expert_out_bias,
    routes,
    gate_weights,
):
    E, T = lax.axis_size("expert"), lax.axis_size("tensor")
    R, D = inputs.shape[1:]
    W, HW = proj_weight.shape[3], expert_in.shape[3]
    tiles = -(-R // ROW_TILE)
    H = -(-tiles // T)
    LAST = tiles - (H - 1) * T
    RP = H * T * ROW_TILE
    CAP = round_up(slot_count(R, E), ROW_TILE)
    RG = round_up(R, ROW_TILE)
    EP = round_up(E, ROW_TILE)
    WC = round_up(-(-W // E), ROW_TILE)
    d = types.SimpleNamespace(
        E=E, T=T, R=R, RG=RG, RP=RP, LAST=LAST, CAP=CAP, D=D, W=W, HW=HW, H=H, EP=EP, WC=WC
    )
    heads = W // HEAD_DIM

    operands = dict(
        inputs=jnp.transpose(inputs, (1, 0, 2)),
        cotangent=jnp.transpose(cotangent, (1, 0, 2)),
        norm_scale=norm_scale[0],
        norm_shift=norm_shift[0],
        proj_weight=jnp.transpose(proj_weight[0], (1, 2, 0)),
        proj_bias=proj_bias[0],
        attn_weight=attn_weight[0],
        attn_bias=attn_bias,
        expert_in=expert_in[0, 0],
        expert_in_bias=expert_in_bias[0],
        expert_out=expert_out[0, 0],
        expert_out_bias=expert_out_bias[0],
        routes=routes[0, 0].T,
        gate_weights=gate_weights[0, 0].T,
    )
    results = dict(
        section_out=(R, D),
        section_in_grad=(R, D),
        grad_norm_scale=(2, D),
        grad_norm_shift=(2, D),
        grad_proj_bias=(2, W),
        grad_attn_bias=(1, D),
        grad_proj=(3, W, D),
        grad_attn_weight=(W, D),
        grad_expert_in=(D, HW),
        grad_expert_in_bias=(1, HW),
        grad_expert_out=(HW, D),
        grad_expert_out_bias=(1, D),
    )
    scratch = dict(
        x=((RP, D), F32),
        rows_in=((R, D), F32),
        g=((RP, D), F32),
        hidden=((RP, D), F32),
        h2=((RP, D), F32),
        r2=((RP, 1), F32),
        nb=((RP, D), BF16),
        resid_in=((RP, D), F32),
        delta_in=((RP, D), BF16),
        qkv=((3, RP, W), BF16),
        probs=((heads, RP, RP), F32),
        na=((E, RG, D), BF16),
        mixed=((RP, W), BF16),
        gp=((E, RG, 3 * W), BF16),
        grad_flat=((RP, 3 * W), BF16),
        h1=((RP, D), F32),
        r1=((RP, 1), F32),
        summed=((H * ROW_TILE, D), F32),
        w_part=((E * WC, D), BF16),
        w_land=((E - 1, WC, D), BF16),
        w_sum=((E * WC, D), BF16),
        rt=((RP, 8), F32),
        gt=((RP, 8), F32),
        rt_t=((8, RP), F32),
        gt_t=((8, RP), F32),
        w_in=((D, HW), BF16),
        w_out=((HW, D), BF16),
        pick=((E, RP, CAP), BF16),
        place=((E, CAP, RP), BF16),
        act=((E, CAP, HW), BF16),
        gpb=((E, CAP, HW), BF16),
        slope=((E, CAP, HW), F32),
        raw=((E, CAP, HW), F32),
        in_bias=((1, HW), F32),
        small=((8, D), F32),
        small2=((8, D), F32),
        small_e=((E - 1, 8, D), F32),
        small_t=((T - 1, 8, D), F32),
    )
    for k in range(1, 5):
        scratch[f"p{k}"] = ((RP, D), BF16)
        scratch[f"l{k}"] = ((T - 1, H * ROW_TILE, D), BF16)
        scratch[f"t{k}"] = ((RP, D), BF16)
        scratch[f"o{k}"] = ((E, CAP, D), BF16)
        scratch[f"b{k}"] = ((E, CAP, D), BF16)
    sems = pltpu.SemaphoreType.DMA((PHASES, max(2 * E, T * H)))
    names = list(operands) + list(results) + list(scratch) + ["load_sem", "send_sem", "recv_sem"]
    in_vmem, in_place = pl.BlockSpec(memory_space=pltpu.VMEM), pl.BlockSpec(memory_space=pl.ANY)
    loaded = ("inputs", "cotangent", "expert_in", "expert_out")
    found = pl.pallas_call(
        functools.partial(relay_kernel, names, d),
        out_shape=[pltpu.VMEM(shape, F32) for shape in results.values()],
        in_specs=[in_place if name in loaded else in_vmem for name in operands],
        out_specs=[in_vmem] * len(results),
        scratch_shapes=[pltpu.VMEM(shape, dtype) for shape, dtype in scratch.values()]
        + [pltpu.SemaphoreType.DMA((len(loaded),)), sems, sems],
        compiler_params=pltpu.CompilerParams(
            collective_id=0, has_side_effects=True, vmem_limit_bytes=52 * 2**20
        ),
        name="relay",
    )(*operands.values())
    shapes = [
        (R, 1, D) if name.startswith("section") else shape for name, shape in results.items()
    ]
    written = pl.pallas_call(
        functools.partial(write_kernel, len(results)),
        out_shape=[jax.ShapeDtypeStruct(shape, F32) for shape in shapes],
        in_specs=[in_vmem] * len(results),
        out_specs=[in_place] * len(results),
        scratch_shapes=[pltpu.SemaphoreType.DMA((len(results),))],
        compiler_params=pltpu.CompilerParams(vmem_limit_bytes=2**20),
        name="write",
    )(*[pltpu.with_memory_space_constraint(array, pltpu.VMEM) for array in found])
    found = types.SimpleNamespace(**dict(zip(results, written)))
    return (
        jnp.transpose(found.section_out, (1, 0, 2))[None],
        jnp.transpose(found.section_in_grad, (1, 0, 2))[None],
        found.grad_norm_scale[None],
        found.grad_norm_shift[None],
        jnp.transpose(found.grad_proj, (2, 0, 1))[None],
        found.grad_proj_bias[None],
        found.grad_attn_weight[None],
        found.grad_attn_bias,
        found.grad_expert_in[None, None],
        found.grad_expert_in_bias[None],
        found.grad_expert_out[None, None],
        found.grad_expert_out_bias[None],
    )


def solution(mesh):
    in_specs = (
        P(None, "expert", None),
        P(None, "expert", None),
        P("section", None, None),
        P("section", None, None),
        P("section", None, None, "tensor"),
        P("section", None, "tensor"),
        P("section", "tensor", None),
        P("section", None),
        P("section", "expert", None, "tensor"),
        P("section", "expert", "tensor"),
        P("section", "expert", "tensor", None),
        P("section", "expert", None),
        P("section", None, "expert", None),
        P("section", None, "expert", None),
    )
    out_specs = (
        P("section", None, "expert", None),
        P("section", None, "expert", None),
        P("section", None, None),
        P("section", None, None),
        P("section", None, None, "tensor"),
        P("section", None, "tensor"),
        P("section", "tensor", None),
        P("section", None),
        P("section", "expert", None, "tensor"),
        P("section", "expert", "tensor"),
        P("section", "expert", "tensor", None),
        P("section", "expert", None),
    )
    return jax.shard_map(
        on_device, mesh=mesh, in_specs=in_specs, out_specs=out_specs, check_vma=False
    )
```
